32 devices in a mesh: gx: 4 (over x, core), gy: 2 (over y), orb: 4 (over z).
Axes of the slice: x: 2, y: 2, z: 4, core: 2. Of those that a mesh axis runs over, the one named last changes fastest.
Arguments:
- orbitals: float32 [4, 32, 32, 384], P('orb', 'gx', 'gy'), may hold values from -6 to 6
- local_pot: float32 [32, 32, 384], P('gx', 'gy'), may hold values from -1 to 1
- proj_vals: bfloat16 [4, 32, 32, 384], P(None, 'gx', 'gy'), may hold values from -0.29882812 to 0.29882812
- proj_ids: int32 [4, 32, 32, 3], P(None, 'gx', 'gy'), may hold values from 0 to 4095, as said below
- proj_energy: float32 [4096], replicated, may hold values from 0.5 to 2
- cheb_coef: float32 [4], replicated, may hold values from 0.2 to 1
Outputs:
- density: float32 [32, 32, 384], P('gx', 'gy')
The draws below stay inside these ranges and needn't reach their ends.
Inputs may be any that keep to these rules, and one draw needn't show every extreme that they name: `proj_ids`: the owner o = id // 512 of each id names the column block (o // 2, o % 2); it differs from the block (x // 8, y // 16) of the slot's cells by at most one in each of the two coordinates, periodically.
All inputs are finite; a program needn't handle non-finite values.
Results may differ from the reference program's by a relative error of at most 0.0003.
Values sent between devices are 32-bit elements; how exact they have to be, the bound alone decides.
No kernel may reach another device: no remote copies, remote signals or barrier semaphores. Data moves between devices by JAX's collectives and lax.ppermute only.
A program may use at most 64 MiB of HBM per device.

```python
import math
import jax
import jax.numpy as jnp
from jax import lax

CX = 8
CY = 16
NZ = 384
ZB = 128
KSLOT = 4
PROJ_DEV = 512
STEPS = 3
NX = 32
NY = 32
NZB = 3
NPROJ = 4096
ORBS = 4


def draw_proj_ids(key, part):
    shape_all = (KSLOT, NX, NY, NZB)
    step_first = jax.random.randint(jax.random.fold_in(key, 11), shape_all, -1, 2)
    step_second = jax.random.randint(jax.random.fold_in(key, 12), shape_all, -1, 2)
    local_num = jax.random.randint(jax.random.fold_in(key, 13), shape_all, 0, PROJ_DEV)
    blocks_first = NX // CX
    blocks_second = NY // CY
    home_first = (jnp.arange(NX, dtype=jnp.int32) // CX)[None, :, None, None]
    home_second = (jnp.arange(NY, dtype=jnp.int32) // CY)[None, None, :, None]
    owner_first = (home_first + step_first) % blocks_first
    owner_second = (home_second + step_second) % blocks_second
    return ((owner_first * blocks_second + owner_second) * PROJ_DEV + local_num).astype(jnp.int32)


def levels(stream_key, dims, split, smallest, largest):
    def one(position, shards_of):
        steps = jax.random.uniform(jax.random.fold_in(jax.random.fold_in(stream_key, 6), position), (shards_of,), jnp.float32, smallest / len(split), largest / len(split))
        return jnp.repeat(jnp.exp(steps), dims[position] // shards_of).reshape((-1,) + (1,) * (len(dims) - position - 1))

    gain = one(*split[0])
    for cut in split[1:]:
        gain = gain * one(*cut)
    return gain


def bell_draw(own_key, dims, spread, most, cuts=(), kind=jnp.bfloat16):
    values = jax.random.normal(own_key, dims, jnp.float32) * spread
    if len(cuts) > 0:
        values = levels(own_key, dims, cuts, -0.22, 0.18) * values
    return jnp.clip(values, min=-most, max=most).astype(kind)


def setup_inputs(seed: int = 0) -> dict:
    key_of = jax.random.split(jax.random.key(seed), 7)
    orbitals = bell_draw(key_of[0], (ORBS, NX, NY, NZ), 1.0, 6.0, ((0, 4), (1, 4), (2, 2)), jnp.float32)
    local_pot = jnp.clip(jax.random.uniform(key_of[1], (NX, NY, NZ), jnp.float32, -1.0, 1.0) * levels(key_of[1], (NX, NY, NZ), ((0, 4), (1, 2)), -0.4, 0.0), -1.0, 1.0)
    proj_vals = bell_draw(key_of[2], (KSLOT, NX, NY, NZ), 0.05, 0.29882812, ((1, 4), (2, 2)))
    proj_ids = draw_proj_ids(jax.random.fold_in(key_of[6], 71), 0)
    proj_energy = jnp.clip(jnp.exp(jax.random.uniform(key_of[4], (NPROJ,), jnp.float32, math.log(0.5), math.log(2.0))), 0.5, 2.0)
    cheb_coef = jnp.clip(jax.random.uniform(key_of[5], (STEPS + 1,), jnp.float32, 0.2, 1.0), 0.2, 1.0)
    return dict(orbitals=orbitals, local_pot=local_pot, proj_vals=proj_vals, proj_ids=proj_ids, proj_energy=proj_energy, cheb_coef=cheb_coef)


E_MID = 4.0
E_HALF = 8.0


def laplace(values):
    result = -90.0 * values
    for axis_num in range(3):
        result = result + 16.0 * (jnp.roll(values, 1, axis_num) + jnp.roll(values, -1, axis_num)) - (jnp.roll(values, 2, axis_num) + jnp.roll(values, -2, axis_num))
    return result / 12.0


def hamilton(values, local_pot, shaped, proj_ids, proj_energy):
    blocks = jnp.einsum("kxyzb,xyzb->kxyz", shaped, values.reshape(NX, NY, NZB, ZB), precision=lax.Precision.HIGHEST)
    coef_sums = jax.ops.segment_sum(blocks.reshape(-1), proj_ids.reshape(-1), num_segments=NPROJ)
    scaled = coef_sums * proj_energy
    weights = scaled[proj_ids]
    projected = jnp.einsum("kxyzb,kxyz->xyzb", shaped, weights, precision=lax.Precision.HIGHEST).reshape(NX, NY, NZ)
    return (-0.5 * laplace(values) + local_pot * values + projected - E_MID * values) / E_HALF


def reference(orbitals, local_pot, proj_vals, proj_ids, proj_energy, cheb_coef):
    shaped = proj_vals.astype(jnp.float32).reshape(KSLOT, NX, NY, NZB, ZB)

    def one_orbital(density, start):
        previous = start
        current = hamilton(start, local_pot, shaped, proj_ids, proj_energy)
        filtered = cheb_coef[0] * previous + cheb_coef[1] * current
        for degree in range(2, STEPS + 1):
            following = 2.0 * hamilton(current, local_pot, shaped, proj_ids, proj_energy) - previous
            previous = current
            current = following
            filtered = filtered + cheb_coef[degree] * current
        return density + filtered * filtered, None

    density, unused = lax.scan(one_orbital, jnp.zeros((NX, NY, NZ), jnp.float32), orbitals)
    return density / ORBS
```

```python
import functools

import jax
import jax.numpy as jnp
from jax import lax
from jax.experimental import pallas as pl
from jax.experimental.pallas import tpu as pltpu
from jax.sharding import PartitionSpec as P

LANES = 128
SUBLANES = 8
STEPS = 3
E_MID = 4.0
E_HALF = 8.0
F32 = jnp.float32
BF16 = jnp.bfloat16


def pieces(vals):
    first = vals.astype(BF16)
    second = (vals - first.astype(F32)).astype(BF16)
    return first, second


def dot(a, b, contract):
    return lax.dot_general(a, b, (contract, ((), ())), preferred_element_type=F32)


NN = ((1,), (0,))
NT = ((1,), (1,))


def iota(shape, dim):
    return lax.broadcasted_iota(jnp.int32, shape, dim)


class Sizes:
    def __init__(self, extent_first, extent_second, extent_depth, slots, owner_size, rows):
        self.ex = extent_first
        self.ey = extent_second
        self.nz = extent_depth
        self.zb = extent_depth // LANES
        self.slots = slots
        self.cells = extent_first * extent_second
        self.rows = rows
        self.xedge = 2 * extent_second
        self.yedge = extent_first * SUBLANES // 2
        self.edge_rows = self.zb * self.xedge
        self.yedge_rows = self.zb * self.yedge
        assert extent_second == 2 * SUBLANES and extent_first % 2 == 0
        assert self.cells == LANES


def rows_of_ids(sz, ids_ref):
    ids = ids_ref[...].reshape(sz.slots * sz.cells, sz.zb)
    pick = jnp.where(
        iota((SUBLANES, sz.zb), 0) == iota((SUBLANES, sz.zb), 1), 1.0, 0.0
    ).astype(BF16)
    row = lax.shift_right_logical(ids, 7).astype(F32).astype(BF16)
    lane = jnp.bitwise_and(ids, LANES - 1).astype(F32).astype(BF16)
    return dot(pick, row, NT), dot(pick, lane, NT)


def chunk(sz, arr, zb, slot):
    return arr[zb : zb + 1, slot * sz.cells : (slot + 1) * sz.cells]


def chunks(sz):
    return [(zb, slot) for zb in range(sz.zb) for slot in range(sz.slots)]


def partial_table(sz, vals, pv_ref, row_of, hot_ref):
    eye = iota((sz.cells, LANES), 0) == iota((sz.cells, LANES), 1)
    eye_all = jnp.concatenate([eye] * sz.slots, axis=0)
    spread_first, spread_second = [], []
    table_iota = iota((sz.rows, LANES), 0).astype(F32)
    for zb in range(sz.zb):
        first, second = pieces(vals[:, zb * LANES : (zb + 1) * LANES])
        weights = pv_ref[:, zb * LANES : (zb + 1) * LANES]
        cross = dot(
            jnp.concatenate([weights, weights], axis=1),
            jnp.concatenate([first, second], axis=1),
            NT,
        )
        cross = jnp.where(eye_all, cross, 0.0)
        for slot in range(sz.slots):
            sums = jnp.sum(
                cross[slot * sz.cells : (slot + 1) * sz.cells], axis=0, keepdims=True
            )
            spread = jnp.where(chunk(sz, row_of, zb, slot) == table_iota, sums, 0.0)
            a, b = pieces(spread)
            spread_first.append(a)
            spread_second.append(b)
    lhs = jnp.concatenate(
        [jnp.concatenate(spread_first, axis=1), jnp.concatenate(spread_second, axis=1)], axis=0
    )
    both = dot(lhs, hot_ref[...], NT)
    return both[: sz.rows] + both[sz.rows :]


def projected(sz, table, pv_ref, row_of, hot_ref):
    first, second = pieces(table)
    found = dot(jnp.concatenate([first, second], axis=0), hot_ref[...], NN)
    found = found[: sz.rows] + found[sz.rows :]
    table_iota = iota((sz.rows, LANES), 0).astype(F32)
    eye = iota((sz.cells, LANES), 0) == iota((sz.cells, LANES), 1)
    result = []
    for zb in range(sz.zb):
        diag_first, diag_second = [], []
        for slot in range(sz.slots):
            at = (zb * sz.slots + slot) * LANES
            hit = chunk(sz, row_of, zb, slot) == table_iota
            weight = jnp.sum(
                jnp.where(hit, found[:, at : at + LANES], 0.0), axis=0, keepdims=True
            )
            a, b = pieces(jnp.where(eye, weight, 0.0))
            diag_first.append(a)
            diag_second.append(b)
        lhs = jnp.concatenate(
            [jnp.concatenate(diag_first, axis=1), jnp.concatenate(diag_second, axis=1)], axis=0
        )
        both = dot(lhs, pv_ref[:, zb * LANES : (zb + 1) * LANES], NN)
        result.append(both[: sz.cells] + both[sz.cells :])
    return result


def from_message(sz, msg_ref, rows):
    return jnp.concatenate(
        [msg_ref[zb * rows : (zb + 1) * rows, :] for zb in range(sz.zb)], axis=1
    )


def to_message(sz, msg_ref, vals):
    rows = vals.shape[0]
    for zb in range(sz.zb):
        msg_ref[zb * rows : (zb + 1) * rows, :] = vals[:, zb * LANES : (zb + 1) * LANES]


def second_edges(sz, vals):
    tiles = vals.reshape(sz.ex, 2, SUBLANES, sz.nz)
    sub = iota((sz.ex // 2, SUBLANES, sz.nz), 1)
    even = tiles.reshape(sz.ex // 2, 2, 2, SUBLANES, sz.nz)
    outer_even = jnp.where(sub < 4, even[:, 0, 0], even[:, 0, 1])
    outer_odd = jnp.where(sub < 4, even[:, 1, 0], even[:, 1, 1])
    odd = pltpu.roll(outer_odd, 4, axis=1)
    keep = jnp.logical_or(sub < 2, sub >= 6)
    return jnp.where(keep, outer_even, odd).reshape(sz.yedge, sz.nz)


def second_halo(sz, packed):
    pairs = packed.reshape(sz.ex // 2, SUBLANES, sz.nz)
    odd = pltpu.roll(pairs, 4, axis=1)
    return jnp.stack([pairs, odd], axis=1).reshape(sz.ex, SUBLANES, sz.nz)


def stencil(sz, vals, low, high, below, above):
    result = -90.0 * vals
    tall = jnp.concatenate([low, vals, high], axis=0)
    step = sz.ey
    cells = sz.cells
    near = tall[step : step + cells] + tall[3 * step : 3 * step + cells]
    far = tall[0:cells] + tall[4 * step : 4 * step + cells]

    near = near + pltpu.roll(vals, 1, axis=1) + pltpu.roll(vals, sz.nz - 1, axis=1)
    far = far + pltpu.roll(vals, 2, axis=1) + pltpu.roll(vals, sz.nz - 2, axis=1)

    tiles = vals.reshape(2 * sz.ex, SUBLANES, sz.nz)
    sub = iota((2 * sz.ex, SUBLANES, sz.nz), 1)

    def shifted(amount, outer, from_below):
        mine = pltpu.roll(tiles, amount, axis=1)
        theirs = pltpu.roll(outer, amount, axis=1)
        pairs = mine.reshape(sz.ex, 2, SUBLANES, sz.nz)
        if from_below:
            other = jnp.stack([theirs, pairs[:, 0]], axis=1)
            mask = sub < amount
        else:
            other = jnp.stack([pairs[:, 1], theirs], axis=1)
            mask = sub >= amount
        return jnp.where(mask, other.reshape(tiles.shape), mine).reshape(vals.shape)

    near = near + shifted(1, below, True) + shifted(SUBLANES - 1, above, False)
    far = far + shifted(2, below, True) + shifted(SUBLANES - 2, above, False)
    return result + 16.0 * near - far


def emit(sz, vals, flag_ref, pv_ref, row_of, hot_ref, ab_ref, bb_ref, yb_ref, table_ref):
    table = partial_table(sz, vals, pv_ref, row_of, hot_ref)
    table_ref[...] = table
    flag = flag_ref[0]
    top = vals[sz.cells - sz.xedge :]
    bottom = vals[: sz.xedge]
    is_high = flag == 0
    to_message(sz, ab_ref, jnp.where(is_high, top, bottom))
    to_message(sz, bb_ref, jnp.where(is_high, bottom, top))
    bb_ref[sz.edge_rows :, :] = table
    to_message(sz, yb_ref, second_edges(sz, vals))
    yb_ref[sz.yedge_rows :, :] = table


def first_kernel(
    sz, flag_ref, vals_ref, pv_ref, ids_ref, ab_ref, bb_ref, yb_ref, table_ref, rows_ref, hot_ref
):
    row_of, lane_of = rows_of_ids(sz, ids_ref)
    rows_ref[...] = row_of
    lane_iota = iota((LANES, LANES), 0).astype(F32)
    for at, (zb, slot) in enumerate(chunks(sz)):
        hot_ref[:, at * LANES : (at + 1) * LANES] = jnp.where(
            chunk(sz, lane_of, zb, slot) == lane_iota, 1.0, 0.0
        ).astype(BF16)
    emit(
        sz, vals_ref[...], flag_ref, pv_ref, row_of, hot_ref, ab_ref, bb_ref, yb_ref, table_ref
    )


def step_kernel(sz, degree, n_tables, n_y, flag_ref, cheb_ref, *refs):
    refs = list(refs)
    table_refs = [refs.pop(0) for _ in range(n_tables)]
    energy_ref, a_ref, b_ref = refs.pop(0), refs.pop(0), refs.pop(0)
    y_refs = [refs.pop(0) for _ in range(n_y)]
    pv_ref, pot_ref, rows_ref, hot_ref = (refs.pop(0) for _ in range(4))
    history = [refs.pop(0) for _ in range(degree)]
    out_refs = refs
    vals = history[-1][...]
    row_of = rows_ref[...]

    from_a = from_message(sz, a_ref, sz.xedge)
    from_b = from_message(sz, b_ref, sz.xedge)
    is_high = flag_ref[0] == 0
    low = jnp.where(is_high, from_b, from_a)
    high = jnp.where(is_high, from_a, from_b)
    outer = [second_halo(sz, from_message(sz, ref, sz.yedge)) for ref in y_refs]
    laplace12 = stencil(sz, vals, low, high, outer[0], outer[-1])
    double = 1.0 if degree == 1 else 2.0
    result = laplace12 * (-0.5 / 12.0 / E_HALF * double) + vals * (
        (pot_ref[...] - E_MID) * (double / E_HALF)
    )
    if degree > 1:
        result = result - history[-2][...]

    table = table_refs[0][...]
    for ref in table_refs[1:]:
        table = table + ref[...]
    table = table * (energy_ref[...] * (double / E_HALF))
    result = result + jnp.concatenate(projected(sz, table, pv_ref, row_of, hot_ref), axis=1)

    if degree < STEPS:
        out_refs[0][...] = result
        emit(sz, result, flag_ref, pv_ref, row_of, hot_ref, *out_refs[1:])
    else:
        filtered = cheb_ref[STEPS] * result
        for n in range(STEPS):
            filtered = filtered + cheb_ref[n] * history[n][...]
        out_refs[0][...] = filtered * filtered


def vmem(count):
    return [pl.BlockSpec(memory_space=pltpu.VMEM)] * count


def smem(count):
    return [pl.BlockSpec(memory_space=pltpu.SMEM)] * count


def shift_table(table, blocks_first, blocks_second, size_first, size_second, dim, delta):
    blocks = table.reshape(blocks_first, blocks_second, -1)
    count = blocks.shape[dim]
    size = (size_first, size_second)[dim]
    parts = []
    for at in range(count):
        source = [s for s in range(count) if (s + delta) % size == at]
        if source:
            parts.append(lax.slice_in_dim(blocks, source[0], source[0] + 1, axis=dim))
        else:
            parts.append(jnp.zeros_like(lax.slice_in_dim(blocks, 0, 1, axis=dim)))
    return jnp.concatenate(parts, axis=dim).reshape(table.shape)


def offsets(size):
    return sorted({d % size for d in (-2, -1, 1, 2)} - {0})


def shift(arr, axis, amount):
    size = lax.axis_size(axis)
    return lax.ppermute(arr, axis, [(i, (i + amount) % size) for i in range(size)])


def swap(arr, target):
    size_first = lax.axis_size("gx")
    size_second = lax.axis_size("gy")
    pairs = []
    for i in range(size_first):
        for j in range(size_second):
            ti, tj = target(i, j)
            pairs.append((i * size_second + j, ti * size_second + tj))
    return lax.ppermute(arr, ("gx", "gy"), pairs)


def orb_sum(vals, scale):
    size = lax.axis_size("orb")
    if size != 4:
        return lax.psum(vals, "orb") * scale
    vals = vals + lax.ppermute(vals, "orb", [(i, i ^ 1) for i in range(4)])
    return (vals + lax.ppermute(vals, "orb", [(i, 3 - i) for i in range(4)])) * scale


def local(orbitals, local_pot, proj_vals, proj_ids, proj_energy, cheb_coef):
    count_orb, ex, ey, nz = orbitals.shape
    slots = proj_vals.shape[0]
    size_first = lax.axis_size("gx")
    size_second = lax.axis_size("gy")
    owner_size = proj_energy.shape[0] // (size_first * size_second)
    whole = size_first == 4 and size_second == 2
    if whole:
        windows = (size_first, size_second)
    else:
        windows = (min(3, size_first), min(3, size_second))
    rows = windows[0] * windows[1] * owner_size // LANES
    sz = Sizes(ex, ey, nz, slots, owner_size, rows)
    here_first = lax.axis_index("gx")
    here_second = lax.axis_index("gy")

    if whole:
        flag = jnp.bitwise_and(here_first, 1).astype(jnp.int32).reshape(1)
        energy = proj_energy.reshape(rows, LANES)
        ids = proj_ids
    else:
        flag = jnp.zeros((1,), jnp.int32)
        owner = proj_ids // owner_size
        rel_first = (owner // size_second - here_first + 1) % size_first
        rel_second = (owner % size_second - here_second + 1) % size_second
        ids = (rel_first * windows[1] + rel_second) * owner_size + proj_ids % owner_size
        grid = proj_energy.reshape(size_first, size_second, owner_size)
        grid = jnp.roll(grid, (1 - here_first, 1 - here_second), (0, 1))
        energy = grid[: windows[0], : windows[1]].reshape(rows, LANES)

    pv = proj_vals.reshape(slots * sz.cells, nz)
    pot = local_pot.reshape(sz.cells, nz)
    message_shapes = (
        jax.ShapeDtypeStruct((sz.edge_rows, LANES), F32),
        jax.ShapeDtypeStruct((sz.edge_rows + rows, LANES), F32),
        jax.ShapeDtypeStruct((sz.yedge_rows + rows, LANES), F32),
        jax.ShapeDtypeStruct((rows, LANES), F32),
    )
    field = jax.ShapeDtypeStruct((sz.cells, nz), F32)
    params = pltpu.CompilerParams(vmem_limit_bytes=48 << 20)

    def exchange(to_a, to_b, to_y, table):
        if whole:
            from_b = swap(to_b, lambda i, j: (size_first - 1 - i, j))
            from_y = swap(to_y, lambda i, j: (i, 1 - j))
            from_d = swap(table, lambda i, j: (size_first - 1 - i, 1 - j))
            from_a = swap(to_a, lambda i, j: (i ^ 1, j))
            table = table + from_d + from_b[sz.edge_rows :] + from_y[sz.yedge_rows :]
            other = swap(table, lambda i, j: (i ^ 1, j))
            return [table, other], from_a, from_b, [from_y]
        edges_b = to_b[: sz.edge_rows]
        edges_y = to_y[: sz.yedge_rows]
        below = shift(edges_y, "gy", 1)
        above = shift(edges_y, "gy", -1)
        from_a = shift(edges_b, "gx", -1)
        from_b = shift(to_a, "gx", 1)
        for dim, axis in ((1, "gy"), (0, "gx")):
            total = table
            for delta in offsets((size_first, size_second)[dim]):
                moved = shift(table, axis, -delta)
                total = total + shift_table(
                    moved, windows[0], windows[1], size_first, size_second, dim, delta
                )
            table = total
        return [table], from_a, from_b, [below, above]

    def one_orbital(start):
        *messages, row_of, hot = pl.pallas_call(
            functools.partial(first_kernel, sz),
            out_shape=message_shapes
            + (
                jax.ShapeDtypeStruct((SUBLANES, slots * sz.cells), F32),
                jax.ShapeDtypeStruct((LANES, slots * sz.zb * sz.cells), BF16),
            ),
            in_specs=smem(1) + vmem(3),
            out_specs=tuple(vmem(6)),
            compiler_params=params,
            name="project_first",
        )(flag, start, pv, ids)
        history = [start]
        for degree in range(1, STEPS + 1):
            tables, from_a, from_b, from_y = exchange(*messages)
            last = degree == STEPS
            args = (
                *tables,
                energy,
                from_a,
                from_b,
                *from_y,
                pv,
                pot,
                row_of,
                hot,
                *history,
            )
            out = pl.pallas_call(
                functools.partial(step_kernel, sz, degree, len(tables), len(from_y)),
                out_shape=(field,) if last else (field,) + message_shapes,
                in_specs=smem(2) + vmem(len(args)),
                out_specs=tuple(vmem(1 if last else 5)),
                compiler_params=params,
                name=f"hamilton_{degree}",
            )(flag, cheb_coef, *args)
            if last:
                return out[0]
            history.append(out[0])
            messages = out[1:]

    density = one_orbital(orbitals[0].reshape(sz.cells, nz))
    for at in range(1, count_orb):
        density = density + one_orbital(orbitals[at].reshape(sz.cells, nz))
    scale = 1.0 / (count_orb * lax.axis_size("orb"))
    return orb_sum(density, scale).reshape(ex, ey, nz)


def solution(mesh):
    return jax.shard_map(
        local,
        mesh=mesh,
        in_specs=(
            P("orb", "gx", "gy", None),
            P("gx", "gy", None),
            P(None, "gx", "gy", None),
            P(None, "gx", "gy", None),
            P(),
            P(),
        ),
        out_specs=P("gx", "gy", None),
        check_vma=False,
    )
```

```python
import functools

import jax
import jax.numpy as jnp
from jax import lax
from jax.experimental import pallas as pl
from jax.experimental.pallas import tpu as pltpu
from jax.sharding import PartitionSpec as P

LANES = 128
SUBLANES = 8
STEPS = 3
E_MID = 4.0
E_HALF = 8.0
F32 = jnp.float32
BF16 = jnp.bfloat16


def pieces(vals):
    first = vals.astype(BF16)
    second = (vals - first.astype(F32)).astype(BF16)
    return first, second


def dot(a, b, contract):
    return lax.dot_general(a, b, (contract, ((), ())), preferred_element_type=F32)


NN = ((1,), (0,))
NT = ((1,), (1,))


def iota(shape, dim):
    return lax.broadcasted_iota(jnp.int32, shape, dim)


class Sizes:
    def __init__(self, extent_first, extent_second, extent_depth, slots, owner_size, rows):
        self.ex = extent_first
        self.ey = extent_second
        self.nz = extent_depth
        self.zb = extent_depth // LANES
        self.slots = slots
        self.cells = extent_first * extent_second
        self.rows = rows
        self.xedge = 2 * extent_second
        self.yedge = extent_first * SUBLANES // 2
        self.edge_rows = self.zb * self.xedge
        self.yedge_rows = self.zb * self.yedge
        assert extent_second == 2 * SUBLANES and extent_first % 2 == 0
        assert self.cells == LANES and extent_first == SUBLANES


def rows_of_ids(sz, ids):
    copies = jnp.where(
        jnp.bitwise_and(iota((sz.ey, LANES), 1), sz.ey - 1) == iota((sz.ey, LANES), 0), 1.0, 0.0
    ).astype(BF16)
    shape = (sz.slots * sz.zb, sz.ex, LANES)
    own = iota(shape, 2) // sz.ey == iota(shape, 1)

    def flat(part):
        spread = dot(part.astype(F32).astype(BF16), copies, NN).reshape(shape)
        return jnp.sum(jnp.where(own, spread, 0.0), axis=1)

    return flat(lax.shift_right_logical(ids, 7)), flat(jnp.bitwise_and(ids, LANES - 1))


def chunk(sz, arr, zb, slot):
    at = slot * sz.zb + zb
    return arr[at : at + 1, :]


def chunks(sz):
    return [(zb, slot) for zb in range(sz.zb) for slot in range(sz.slots)]


def partial_table(sz, vals, pv_ref, row_of, hot_ref):
    eye = iota((sz.cells, LANES), 0) == iota((sz.cells, LANES), 1)
    eye_all = jnp.concatenate([eye] * sz.slots, axis=0)
    spread_first, spread_second = [], []
    table_iota = iota((sz.rows, LANES), 0).astype(F32)
    for zb in range(sz.zb):
        first, second = pieces(vals[:, zb * LANES : (zb + 1) * LANES])
        weights = pv_ref[:, zb * LANES : (zb + 1) * LANES]
        cross = dot(
            jnp.concatenate([weights, weights], axis=1),
            jnp.concatenate([first, second], axis=1),
            NT,
        )
        cross = jnp.where(eye_all, cross, 0.0)
        for slot in range(sz.slots):
            sums = jnp.sum(
                cross[slot * sz.cells : (slot + 1) * sz.cells], axis=0, keepdims=True
            )
            spread = jnp.where(chunk(sz, row_of, zb, slot) == table_iota, sums, 0.0)
            a, b = pieces(spread)
            spread_first.append(a)
            spread_second.append(b)
    lhs = jnp.concatenate(
        [jnp.concatenate(spread_first, axis=1), jnp.concatenate(spread_second, axis=1)], axis=0
    )
    both = dot(lhs, hot_ref[...], NT)
    return both[: sz.rows] + both[sz.rows :]


def projected(sz, table, pv_ref, row_of, hot_ref):
    first, second = pieces(table)
    found = dot(jnp.concatenate([first, second], axis=0), hot_ref[...], NN)
    found = found[: sz.rows] + found[sz.rows :]
    table_iota = iota((sz.rows, LANES), 0).astype(F32)
    eye = iota((sz.cells, LANES), 0) == iota((sz.cells, LANES), 1)
    result = []
    for zb in range(sz.zb):
        diag_first, diag_second = [], []
        for slot in range(sz.slots):
            at = (zb * sz.slots + slot) * LANES
            hit = chunk(sz, row_of, zb, slot) == table_iota
            weight = jnp.sum(
                jnp.where(hit, found[:, at : at + LANES], 0.0), axis=0, keepdims=True
            )
            a, b = pieces(jnp.where(eye, weight, 0.0))
            diag_first.append(a)
            diag_second.append(b)
        lhs = jnp.concatenate(
            [jnp.concatenate(diag_first, axis=1), jnp.concatenate(diag_second, axis=1)], axis=0
        )
        both = dot(lhs, pv_ref[:, zb * LANES : (zb + 1) * LANES], NN)
        result.append(both[: sz.cells] + both[sz.cells :])
    return result


def from_message(sz, msg_ref, rows):
    return jnp.concatenate(
        [msg_ref[zb * rows : (zb + 1) * rows, :] for zb in range(sz.zb)], axis=1
    )


def to_message(sz, msg_ref, vals):
    rows = vals.shape[0]
    for zb in range(sz.zb):
        msg_ref[zb * rows : (zb + 1) * rows, :] = vals[:, zb * LANES : (zb + 1) * LANES]


def second_edges(sz, vals):
    tiles = vals.reshape(sz.ex, 2, SUBLANES, sz.nz)
    sub = iota((sz.ex // 2, SUBLANES, sz.nz), 1)
    even = tiles.reshape(sz.ex // 2, 2, 2, SUBLANES, sz.nz)
    outer_even = jnp.where(sub < 4, even[:, 0, 0], even[:, 0, 1])
    outer_odd = jnp.where(sub < 4, even[:, 1, 0], even[:, 1, 1])
    odd = pltpu.roll(outer_odd, 4, axis=1)
    keep = jnp.logical_or(sub < 2, sub >= 6)
    return jnp.where(keep, outer_even, odd).reshape(sz.yedge, sz.nz)


def second_halo(sz, packed):
    pairs = packed.reshape(sz.ex // 2, SUBLANES, sz.nz)
    odd = pltpu.roll(pairs, 4, axis=1)
    return jnp.stack([pairs, odd], axis=1).reshape(sz.ex, SUBLANES, sz.nz)


def stencil(sz, vals, low, high, below, above):
    result = -90.0 * vals
    tall = jnp.concatenate([low, vals, high], axis=0)
    step = sz.ey
    cells = sz.cells
    near = tall[step : step + cells] + tall[3 * step : 3 * step + cells]
    far = tall[0:cells] + tall[4 * step : 4 * step + cells]

    near = near + pltpu.roll(vals, 1, axis=1) + pltpu.roll(vals, sz.nz - 1, axis=1)
    far = far + pltpu.roll(vals, 2, axis=1) + pltpu.roll(vals, sz.nz - 2, axis=1)

    tiles = vals.reshape(2 * sz.ex, SUBLANES, sz.nz)
    sub = iota((2 * sz.ex, SUBLANES, sz.nz), 1)

    def shifted(amount, outer, from_below):
        mine = pltpu.roll(tiles, amount, axis=1)
        theirs = pltpu.roll(outer, amount, axis=1)
        pairs = mine.reshape(sz.ex, 2, SUBLANES, sz.nz)
        if from_below:
            other = jnp.stack([theirs, pairs[:, 0]], axis=1)
            mask = sub < amount
        else:
            other = jnp.stack([pairs[:, 1], theirs], axis=1)
            mask = sub >= amount
        return jnp.where(mask, other.reshape(tiles.shape), mine).reshape(vals.shape)

    near = near + shifted(1, below, True) + shifted(SUBLANES - 1, above, False)
    far = far + shifted(2, below, True) + shifted(SUBLANES - 2, above, False)
    return result + 16.0 * near - far


def emit(sz, vals, flag_ref, pv_ref, row_of, hot_ref, ab_ref, bb_ref, yb_ref, table_ref):
    table = partial_table(sz, vals, pv_ref, row_of, hot_ref)
    table_ref[...] = table
    flag = flag_ref[0]
    top = vals[sz.cells - sz.xedge :]
    bottom = vals[: sz.xedge]
    is_high = flag == 0
    to_message(sz, ab_ref, jnp.where(is_high, top, bottom))
    to_message(sz, bb_ref, jnp.where(is_high, bottom, top))
    bb_ref[sz.edge_rows :, :] = table
    to_message(sz, yb_ref, second_edges(sz, vals))
    yb_ref[sz.yedge_rows :, :] = table


def first_kernel(
    sz,
    flag_ref,
    vals_hbm,
    pv_hbm,
    ids_hbm,
    ab_ref,
    bb_ref,
    yb_ref,
    table_ref,
    rows_ref,
    hot_ref,
    vals_ref,
    pv_ref,
    ids_ref,
    sems,
):
    get_ids = pltpu.make_async_copy(ids_hbm, ids_ref, sems.at[0])
    get_pv = pltpu.make_async_copy(pv_hbm, pv_ref, sems.at[1])
    get_vals = pltpu.make_async_copy(vals_hbm, vals_ref, sems.at[2])
    get_ids.start()
    get_vals.start()
    get_pv.start()
    get_ids.wait()
    row_of, lane_of = rows_of_ids(sz, ids_ref[...])
    rows_ref[...] = row_of
    lane_iota = iota((LANES, LANES), 0).astype(F32)
    for at, (zb, slot) in enumerate(chunks(sz)):
        hot_ref[:, at * LANES : (at + 1) * LANES] = jnp.where(
            chunk(sz, lane_of, zb, slot) == lane_iota, 1.0, 0.0
        ).astype(BF16)
    get_vals.wait()
    get_pv.wait()
    emit(
        sz, vals_ref[...], flag_ref, pv_ref, row_of, hot_ref, ab_ref, bb_ref, yb_ref, table_ref
    )


def local_kernel(sz, degree, n_y, flag_ref, *refs):
    refs = list(refs)
    cheb_ref = refs.pop(0) if degree == STEPS else None
    a_ref, b_ref = refs.pop(0), refs.pop(0)
    y_refs = [refs.pop(0) for _ in range(n_y)]
    pot_ref = refs.pop(0)
    *history, out_ref = refs
    vals = history[-1][...]

    from_a = from_message(sz, a_ref, sz.xedge)
    from_b = from_message(sz, b_ref, sz.xedge)
    is_high = flag_ref[0] == 0
    low = jnp.where(is_high, from_b, from_a)
    high = jnp.where(is_high, from_a, from_b)
    outer = [second_halo(sz, from_message(sz, ref, sz.yedge)) for ref in y_refs]
    laplace12 = stencil(sz, vals, low, high, outer[0], outer[-1])
    double = 1.0 if degree == 1 else 2.0
    result = laplace12 * (-0.5 / 12.0 / E_HALF * double) + vals * (
        (pot_ref[...] - E_MID) * (double / E_HALF)
    )
    if degree > 1:
        result = result - history[-2][...]
    if degree == STEPS:
        result = cheb_ref[STEPS] * result
        for n in range(STEPS):
            result = result + cheb_ref[n] * history[n][...]
    out_ref[...] = result


def added(table_refs):
    table = table_refs[0][...]
    for ref in table_refs[1:]:
        table = table + ref[...]
    return table


def nonlocal_kernel(sz, degree, n_tables, flag_ref, *refs):
    refs = list(refs)
    table_refs = [refs.pop(0) for _ in range(n_tables)]
    energy_ref, rest_ref, pv_ref, rows_ref, hot_ref = (refs.pop(0) for _ in range(5))
    row_of = rows_ref[...]
    double = 1.0 if degree == 1 else 2.0
    table = added(table_refs) * (energy_ref[...] * (double / E_HALF))
    result = rest_ref[...] + jnp.concatenate(
        projected(sz, table, pv_ref, row_of, hot_ref), axis=1
    )
    refs[0][...] = result
    emit(sz, result, flag_ref, pv_ref, row_of, hot_ref, *refs[1:])


def last_kernel(sz, n_tables, cheb_ref, *refs):
    refs = list(refs)
    table_refs = [refs.pop(0) for _ in range(n_tables)]
    energy_ref, rest_ref, pv_ref, rows_ref, hot_ref, out_ref = refs
    table = added(table_refs) * (energy_ref[...] * (2.0 / E_HALF * cheb_ref[STEPS]))
    result = rest_ref[...] + jnp.concatenate(
        projected(sz, table, pv_ref, rows_ref[...], hot_ref), axis=1
    )
    out_ref[...] = result * result


def vmem(count):
    return [pl.BlockSpec(memory_space=pltpu.VMEM)] * count


def smem(count):
    return [pl.BlockSpec(memory_space=pltpu.SMEM)] * count


def shift_table(table, blocks_first, blocks_second, size_first, size_second, dim, delta):
    blocks = table.reshape(blocks_first, blocks_second, -1)
    count = blocks.shape[dim]
    size = (size_first, size_second)[dim]
    parts = []
    for at in range(count):
        source = [s for s in range(count) if (s + delta) % size == at]
        if source:
            parts.append(lax.slice_in_dim(blocks, source[0], source[0] + 1, axis=dim))
        else:
            parts.append(jnp.zeros_like(lax.slice_in_dim(blocks, 0, 1, axis=dim)))
    return jnp.concatenate(parts, axis=dim).reshape(table.shape)


def offsets(size):
    return sorted({d % size for d in (-2, -1, 1, 2)} - {0})


def shift(arr, axis, amount):
    size = lax.axis_size(axis)
    return lax.ppermute(arr, axis, [(i, (i + amount) % size) for i in range(size)])


def swap(arr, target):
    size_first = lax.axis_size("gx")
    size_second = lax.axis_size("gy")
    pairs = []
    for i in range(size_first):
        for j in range(size_second):
            ti, tj = target(i, j)
            pairs.append((i * size_second + j, ti * size_second + tj))
    return lax.ppermute(arr, ("gx", "gy"), pairs)


def orb_sum(vals, scale):
    size = lax.axis_size("orb")
    if size != 4:
        return lax.psum(vals, "orb") * scale
    vals = vals + lax.ppermute(vals, "orb", [(i, i ^ 1) for i in range(4)])
    return (vals + lax.ppermute(vals, "orb", [(i, 3 - i) for i in range(4)])) * scale


def local(orbitals, local_pot, proj_vals, proj_ids, proj_energy, cheb_coef):
    count_orb, ex, ey, nz = orbitals.shape
    slots = proj_vals.shape[0]
    size_first = lax.axis_size("gx")
    size_second = lax.axis_size("gy")
    owner_size = proj_energy.shape[0] // (size_first * size_second)
    whole = size_first == 4 and size_second == 2
    if whole:
        windows = (size_first, size_second)
    else:
        windows = (min(3, size_first), min(3, size_second))
    rows = windows[0] * windows[1] * owner_size // LANES
    sz = Sizes(ex, ey, nz, slots, owner_size, rows)
    here_first = lax.axis_index("gx")
    here_second = lax.axis_index("gy")

    if whole:
        flag = jnp.bitwise_and(here_first, 1).astype(jnp.int32).reshape(1)
        energy = proj_energy.reshape(rows, LANES)
        ids = proj_ids
    else:
        flag = jnp.zeros((1,), jnp.int32)
        owner = proj_ids // owner_size
        rel_first = (owner // size_second - here_first + 1) % size_first
        rel_second = (owner % size_second - here_second + 1) % size_second
        ids = (rel_first * windows[1] + rel_second) * owner_size + proj_ids % owner_size
        grid = proj_energy.reshape(size_first, size_second, owner_size)
        grid = jnp.roll(grid, (1 - here_first, 1 - here_second), (0, 1))
        energy = grid[: windows[0], : windows[1]].reshape(rows, LANES)

    ids = jnp.transpose(ids, (0, 3, 1, 2)).reshape(slots * sz.zb * ex, ey)
    pv = proj_vals.reshape(slots * sz.cells, nz)
    pot = local_pot.reshape(sz.cells, nz)
    message_shapes = (
        jax.ShapeDtypeStruct((sz.edge_rows, LANES), F32),
        jax.ShapeDtypeStruct((sz.edge_rows + rows, LANES), F32),
        jax.ShapeDtypeStruct((sz.yedge_rows + rows, LANES), F32),
        jax.ShapeDtypeStruct((rows, LANES), F32),
    )
    field = jax.ShapeDtypeStruct((sz.cells, nz), F32)
    params = pltpu.CompilerParams(vmem_limit_bytes=48 << 20)

    def exchange(to_a, to_b, to_y, table):
        if whole:
            from_b = swap(to_b, lambda i, j: (size_first - 1 - i, j))
            from_y = swap(to_y, lambda i, j: (i, 1 - j))
            from_d = swap(table, lambda i, j: (size_first - 1 - i, 1 - j))
            from_a = swap(to_a, lambda i, j: (i ^ 1, j))
            table = table + from_d + from_b[sz.edge_rows :] + from_y[sz.yedge_rows :]
            other = swap(table, lambda i, j: (i ^ 1, j))
            return [table, other], from_a, from_b, [from_y]
        edges_b = to_b[: sz.edge_rows]
        edges_y = to_y[: sz.yedge_rows]
        below = shift(edges_y, "gy", 1)
        above = shift(edges_y, "gy", -1)
        from_a = shift(edges_b, "gx", -1)
        from_b = shift(to_a, "gx", 1)
        for dim, axis in ((1, "gy"), (0, "gx")):
            total = table
            for delta in offsets((size_first, size_second)[dim]):
                moved = shift(table, axis, -delta)
                total = total + shift_table(
                    moved, windows[0], windows[1], size_first, size_second, dim, delta
                )
            table = total
        return [table], from_a, from_b, [below, above]

    def one_orbital(start):
        *messages, row_of, hot = pl.pallas_call(
            functools.partial(first_kernel, sz),
            out_shape=message_shapes
            + (
                jax.ShapeDtypeStruct((slots * sz.zb, LANES), F32),
                jax.ShapeDtypeStruct((LANES, slots * sz.zb * sz.cells), BF16),
            ),
            in_specs=smem(1) + [pl.BlockSpec(memory_space=pltpu.HBM)] * 3,
            out_specs=tuple(vmem(6)),
            scratch_shapes=[
                pltpu.VMEM(start.shape, start.dtype),
                pltpu.VMEM(pv.shape, pv.dtype),
                pltpu.VMEM(ids.shape, ids.dtype),
                pltpu.SemaphoreType.DMA((3,)),
            ],
            compiler_params=params,
            name="project_first",
        )(flag, start, pv, ids)
        history = [start]
        for degree in range(1, STEPS + 1):
            tables, from_a, from_b, from_y = exchange(*messages)
            last = degree == STEPS
            scalars = (flag, cheb_coef) if last else (flag,)
            args = (from_a, from_b, *from_y, pot, *history)
            rest = pl.pallas_call(
                functools.partial(local_kernel, sz, degree, len(from_y)),
                out_shape=field,
                in_specs=smem(len(scalars)) + vmem(len(args)),
                out_specs=vmem(1)[0],
                compiler_params=params,
                name=f"local_{degree}",
            )(*scalars, *args)
            args = (*tables, energy, rest, pv, row_of, hot)
            if last:
                return pl.pallas_call(
                    functools.partial(last_kernel, sz, len(tables)),
                    out_shape=field,
                    in_specs=smem(1) + vmem(len(args)),
                    out_specs=vmem(1)[0],
                    compiler_params=params,
                    name="filtered",
                )(cheb_coef, *args)
            out = pl.pallas_call(
                functools.partial(nonlocal_kernel, sz, degree, len(tables)),
                out_shape=(field,) + message_shapes,
                in_specs=smem(1) + vmem(len(args)),
                out_specs=tuple(vmem(5)),
                compiler_params=params,
                name=f"nonlocal_{degree}",
            )(flag, *args)
            history.append(out[0])
            messages = out[1:]

    density = one_orbital(orbitals[0].reshape(sz.cells, nz))
    for at in range(1, count_orb):
        density = density + one_orbital(orbitals[at].reshape(sz.cells, nz))
    scale = 1.0 / (count_orb * lax.axis_size("orb"))
    return orb_sum(density, scale).reshape(ex, ey, nz)


def solution(mesh):
    return jax.shard_map(
        local,
        mesh=mesh,
        in_specs=(
            P("orb", "gx", "gy", None),
            P("gx", "gy", None),
            P(None, "gx", "gy", None),
            P(None, "gx", "gy", None),
            P(),
            P(),
        ),
        out_specs=P("gx", "gy", None),
        check_vma=False,
    )
```

```python
import functools

import jax
import jax.numpy as jnp
from jax import lax
from jax.experimental import pallas as pl
from jax.experimental.pallas import tpu as pltpu
from jax.sharding import PartitionSpec as P

LANES = 128
SUBLANES = 8
STEPS = 3
E_MID = 4.0
E_HALF = 8.0
F32 = jnp.float32
BF16 = jnp.bfloat16


def pieces(vals):
    first = vals.astype(BF16)
    second = (vals - first.astype(F32)).astype(BF16)
    return first, second


def dot(a, b, contract):
    return lax.dot_general(a, b, (contract, ((), ())), preferred_element_type=F32)


NN = ((1,), (0,))
NT = ((1,), (1,))


def iota(shape, dim):
    return lax.broadcasted_iota(jnp.int32, shape, dim)


class Sizes:
    def __init__(self, extent_first, extent_second, extent_depth, slots, owner_size, rows):
        self.ex = extent_first
        self.ey = extent_second
        self.nz = extent_depth
        self.zb = extent_depth // LANES
        self.slots = slots
        self.cells = extent_first * extent_second
        self.rows = rows
        self.xedge = 2 * extent_second
        self.yedge = extent_first * SUBLANES // 2
        self.edge_rows = self.zb * self.xedge
        self.yedge_rows = self.zb * self.yedge
        assert extent_second == 2 * SUBLANES and extent_first % 2 == 0
        assert self.cells == LANES and extent_first == SUBLANES


def rows_of_ids(sz, ids):
    copies = jnp.where(
        jnp.bitwise_and(iota((sz.ey, LANES), 1), sz.ey - 1) == iota((sz.ey, LANES), 0), 1.0, 0.0
    ).astype(BF16)
    shape = (sz.slots * sz.zb, sz.ex, LANES)
    own = iota(shape, 2) // sz.ey == iota(shape, 1)

    def flat(part):
        spread = dot(part.astype(F32).astype(BF16), copies, NN).reshape(shape)
        return jnp.sum(jnp.where(own, spread, 0.0), axis=1)

    return flat(lax.shift_right_logical(ids, 7)), flat(jnp.bitwise_and(ids, LANES - 1))


def chunk(sz, arr, zb, slot):
    at = slot * sz.zb + zb
    return arr[at : at + 1, :]


def chunks(sz):
    return [(zb, slot) for zb in range(sz.zb) for slot in range(sz.slots)]


def partial_table(sz, vals, pv_ref, row_of, hot_ref):
    eye = iota((sz.cells, LANES), 0) == iota((sz.cells, LANES), 1)
    eye_all = jnp.concatenate([eye] * sz.slots, axis=0)
    spread_first, spread_second = [], []
    table_iota = iota((sz.rows, LANES), 0).astype(F32)
    for zb in range(sz.zb):
        first, second = pieces(vals[:, zb * LANES : (zb + 1) * LANES])
        weights = pv_ref[:, zb * LANES : (zb + 1) * LANES]
        cross = dot(
            jnp.concatenate([weights, weights], axis=1),
            jnp.concatenate([first, second], axis=1),
            NT,
        )
        cross = jnp.where(eye_all, cross, 0.0)
        for slot in range(sz.slots):
            sums = jnp.sum(
                cross[slot * sz.cells : (slot + 1) * sz.cells], axis=0, keepdims=True
            )
            spread = jnp.where(chunk(sz, row_of, zb, slot) == table_iota, sums, 0.0)
            a, b = pieces(spread)
            spread_first.append(a)
            spread_second.append(b)
    lhs = jnp.concatenate(
        [jnp.concatenate(spread_first, axis=1), jnp.concatenate(spread_second, axis=1)], axis=0
    )
    both = dot(lhs, hot_ref[...], NT)
    return both[: sz.rows] + both[sz.rows :]


def projected(sz, table, pv_ref, row_of, hot_ref):
    first, second = pieces(table)
    found = dot(jnp.concatenate([first, second], axis=0), hot_ref[...], NN)
    found = found[: sz.rows] + found[sz.rows :]
    table_iota = iota((sz.rows, LANES), 0).astype(F32)
    eye = iota((sz.cells, LANES), 0) == iota((sz.cells, LANES), 1)
    result = []
    for zb in range(sz.zb):
        diag_first, diag_second = [], []
        for slot in range(sz.slots):
            at = (zb * sz.slots + slot) * LANES
            hit = chunk(sz, row_of, zb, slot) == table_iota
            weight = jnp.sum(
                jnp.where(hit, found[:, at : at + LANES], 0.0), axis=0, keepdims=True
            )
            a, b = pieces(jnp.where(eye, weight, 0.0))
            diag_first.append(a)
            diag_second.append(b)
        lhs = jnp.concatenate(
            [jnp.concatenate(diag_first, axis=1), jnp.concatenate(diag_second, axis=1)], axis=0
        )
        both = dot(lhs, pv_ref[:, zb * LANES : (zb + 1) * LANES], NN)
        result.append(both[: sz.cells] + both[sz.cells :])
    return result


def from_message(sz, msg_ref, rows):
    return jnp.concatenate(
        [msg_ref[zb * rows : (zb + 1) * rows, :] for zb in range(sz.zb)], axis=1
    )


def to_message(sz, msg_ref, vals):
    rows = vals.shape[0]
    for zb in range(sz.zb):
        msg_ref[zb * rows : (zb + 1) * rows, :] = vals[:, zb * LANES : (zb + 1) * LANES]


def second_edges(sz, vals):
    tiles = vals.reshape(sz.ex, 2, SUBLANES, sz.nz)
    sub = iota((sz.ex // 2, SUBLANES, sz.nz), 1)
    even = tiles.reshape(sz.ex // 2, 2, 2, SUBLANES, sz.nz)
    outer_even = jnp.where(sub < 4, even[:, 0, 0], even[:, 0, 1])
    outer_odd = jnp.where(sub < 4, even[:, 1, 0], even[:, 1, 1])
    odd = pltpu.roll(outer_odd, 4, axis=1)
    keep = jnp.logical_or(sub < 2, sub >= 6)
    return jnp.where(keep, outer_even, odd).reshape(sz.yedge, sz.nz)


def second_halo(sz, packed):
    pairs = packed.reshape(sz.ex // 2, SUBLANES, sz.nz)
    odd = pltpu.roll(pairs, 4, axis=1)
    return jnp.stack([pairs, odd], axis=1).reshape(sz.ex, SUBLANES, sz.nz)


def stencil(sz, vals, low, high, below, above):
    result = -90.0 * vals
    tall = jnp.concatenate([low, vals, high], axis=0)
    step = sz.ey
    cells = sz.cells
    near = tall[step : step + cells] + tall[3 * step : 3 * step + cells]
    far = tall[0:cells] + tall[4 * step : 4 * step + cells]

    near = near + pltpu.roll(vals, 1, axis=1) + pltpu.roll(vals, sz.nz - 1, axis=1)
    far = far + pltpu.roll(vals, 2, axis=1) + pltpu.roll(vals, sz.nz - 2, axis=1)

    tiles = vals.reshape(2 * sz.ex, SUBLANES, sz.nz)
    sub = iota((2 * sz.ex, SUBLANES, sz.nz), 1)

    def shifted(amount, outer, from_below):
        mine = pltpu.roll(tiles, amount, axis=1)
        theirs = pltpu.roll(outer, amount, axis=1)
        pairs = mine.reshape(sz.ex, 2, SUBLANES, sz.nz)
        if from_below:
            other = jnp.stack([theirs, pairs[:, 0]], axis=1)
            mask = sub < amount
        else:
            other = jnp.stack([pairs[:, 1], theirs], axis=1)
            mask = sub >= amount
        return jnp.where(mask, other.reshape(tiles.shape), mine).reshape(vals.shape)

    near = near + shifted(1, below, True) + shifted(SUBLANES - 1, above, False)
    far = far + shifted(2, below, True) + shifted(SUBLANES - 2, above, False)
    return result + 16.0 * near - far


def emit(sz, vals, flag_ref, pv_ref, row_of, hot_ref, ab_ref, bb_ref, yb_ref, table_ref):
    table = partial_table(sz, vals, pv_ref, row_of, hot_ref)
    table_ref[...] = table
    flag = flag_ref[0]
    top = vals[sz.cells - sz.xedge :]
    bottom = vals[: sz.xedge]
    is_high = flag == 0
    to_message(sz, ab_ref, jnp.where(is_high, top, bottom))
    to_message(sz, bb_ref, jnp.where(is_high, bottom, top))
    bb_ref[sz.edge_rows :, :] = table
    to_message(sz, yb_ref, second_edges(sz, vals))
    yb_ref[sz.yedge_rows :, :] = table


def first_kernel(
    sz,
    flag_ref,
    vals_hbm,
    pv_hbm,
    ids_hbm,
    ab_ref,
    bb_ref,
    yb_ref,
    table_ref,
    rows_ref,
    hot_ref,
    vals_ref,
    pv_ref,
    ids_ref,
    sems,
):
    get_ids = pltpu.make_async_copy(ids_hbm, ids_ref, sems.at[0])
    get_pv = pltpu.make_async_copy(pv_hbm, pv_ref, sems.at[1])
    get_vals = pltpu.make_async_copy(vals_hbm, vals_ref, sems.at[2])
    get_ids.start()
    get_vals.start()
    get_pv.start()
    get_ids.wait()
    row_of, lane_of = rows_of_ids(sz, ids_ref[...])
    rows_ref[...] = row_of
    lane_iota = iota((LANES, LANES), 0).astype(F32)
    for at, (zb, slot) in enumerate(chunks(sz)):
        hot_ref[:, at * LANES : (at + 1) * LANES] = jnp.where(
            chunk(sz, lane_of, zb, slot) == lane_iota, 1.0, 0.0
        ).astype(BF16)
    get_vals.wait()
    get_pv.wait()
    emit(
        sz, vals_ref[...], flag_ref, pv_ref, row_of, hot_ref, ab_ref, bb_ref, yb_ref, table_ref
    )


def coefficient(sz, cheb_ref, n):
    row = cheb_ref[n : n + 1, :]
    return jnp.concatenate([row] * sz.zb, axis=1)


def local_kernel(sz, degree, n_y, flag_ref, *refs):
    refs = list(refs)
    cheb_ref = refs.pop(0) if degree == STEPS else None
    a_ref, b_ref = refs.pop(0), refs.pop(0)
    y_refs = [refs.pop(0) for _ in range(n_y)]
    pot_ref = refs.pop(0)
    *history, out_ref = refs
    vals = history[-1][...]

    from_a = from_message(sz, a_ref, sz.xedge)
    from_b = from_message(sz, b_ref, sz.xedge)
    is_high = flag_ref[0] == 0
    low = jnp.where(is_high, from_b, from_a)
    high = jnp.where(is_high, from_a, from_b)
    outer = [second_halo(sz, from_message(sz, ref, sz.yedge)) for ref in y_refs]
    laplace12 = stencil(sz, vals, low, high, outer[0], outer[-1])
    double = 1.0 if degree == 1 else 2.0
    result = laplace12 * (-0.5 / 12.0 / E_HALF * double) + vals * (
        (pot_ref[...] - E_MID) * (double / E_HALF)
    )
    if degree > 1:
        result = result - history[-2][...]
    if degree == STEPS:
        result = coefficient(sz, cheb_ref, STEPS) * result
        for n in range(STEPS):
            result = result + coefficient(sz, cheb_ref, n) * history[n][...]
    out_ref[...] = result


def added(table_refs):
    table = table_refs[0][...]
    for ref in table_refs[1:]:
        table = table + ref[...]
    return table


def nonlocal_kernel(sz, degree, n_tables, flag_ref, *refs):
    refs = list(refs)
    if degree == 1:
        cheb_ref, cheb_out = refs.pop(0), refs.pop()
        for n in range(STEPS + 1):
            cheb_out[n : n + 1, :] = jnp.full((1, LANES), cheb_ref[n], F32)
    table_refs = [refs.pop(0) for _ in range(n_tables)]
    energy_ref, rest_ref, pv_ref, rows_ref, hot_ref = (refs.pop(0) for _ in range(5))
    row_of = rows_ref[...]
    double = 1.0 if degree == 1 else 2.0
    table = added(table_refs) * (energy_ref[...] * (double / E_HALF))
    result = rest_ref[...] + jnp.concatenate(
        projected(sz, table, pv_ref, row_of, hot_ref), axis=1
    )
    refs[0][...] = result
    emit(sz, result, flag_ref, pv_ref, row_of, hot_ref, *refs[1:])


def last_kernel(sz, n_tables, cheb_ref, *refs):
    refs = list(refs)
    table_refs = [refs.pop(0) for _ in range(n_tables)]
    energy_ref, rest_ref, pv_ref, rows_ref, hot_ref, out_ref = refs
    table = added(table_refs) * (energy_ref[...] * (2.0 / E_HALF * cheb_ref[STEPS : STEPS + 1, :]))
    result = rest_ref[...] + jnp.concatenate(
        projected(sz, table, pv_ref, rows_ref[...], hot_ref), axis=1
    )
    out_ref[...] = result * result


def vmem(count):
    return [pl.BlockSpec(memory_space=pltpu.VMEM)] * count


def smem(count):
    return [pl.BlockSpec(memory_space=pltpu.SMEM)] * count


def shift_table(table, blocks_first, blocks_second, size_first, size_second, dim, delta):
    blocks = table.reshape(blocks_first, blocks_second, -1)
    count = blocks.shape[dim]
    size = (size_first, size_second)[dim]
    parts = []
    for at in range(count):
        source = [s for s in range(count) if (s + delta) % size == at]
        if source:
            parts.append(lax.slice_in_dim(blocks, source[0], source[0] + 1, axis=dim))
        else:
            parts.append(jnp.zeros_like(lax.slice_in_dim(blocks, 0, 1, axis=dim)))
    return jnp.concatenate(parts, axis=dim).reshape(table.shape)


def offsets(size):
    return sorted({d % size for d in (-2, -1, 1, 2)} - {0})


def shift(arr, axis, amount):
    size = lax.axis_size(axis)
    return lax.ppermute(arr, axis, [(i, (i + amount) % size) for i in range(size)])


def swap(arr, target):
    size_first = lax.axis_size("gx")
    size_second = lax.axis_size("gy")
    pairs = []
    for i in range(size_first):
        for j in range(size_second):
            ti, tj = target(i, j)
            pairs.append((i * size_second + j, ti * size_second + tj))
    return lax.ppermute(arr, ("gx", "gy"), pairs)


def orb_sum(vals, scale):
    size = lax.axis_size("orb")
    if size != 4:
        return lax.psum(vals, "orb") * scale
    vals = vals + lax.ppermute(vals, "orb", [(i, i ^ 1) for i in range(4)])
    return (vals + lax.ppermute(vals, "orb", [(i, 3 - i) for i in range(4)])) * scale


def local(orbitals, local_pot, proj_vals, proj_ids, proj_energy, cheb_coef):
    count_orb, ex, ey, nz = orbitals.shape
    slots = proj_vals.shape[0]
    size_first = lax.axis_size("gx")
    size_second = lax.axis_size("gy")
    owner_size = proj_energy.shape[0] // (size_first * size_second)
    whole = size_first == 4 and size_second == 2
    if whole:
        windows = (size_first, size_second)
    else:
        windows = (min(3, size_first), min(3, size_second))
    rows = windows[0] * windows[1] * owner_size // LANES
    sz = Sizes(ex, ey, nz, slots, owner_size, rows)
    here_first = lax.axis_index("gx")
    here_second = lax.axis_index("gy")

    if whole:
        flag = jnp.bitwise_and(here_first, 1).astype(jnp.int32).reshape(1)
        energy = proj_energy.reshape(rows, LANES)
        ids = proj_ids
    else:
        flag = jnp.zeros((1,), jnp.int32)
        owner = proj_ids // owner_size
        rel_first = (owner // size_second - here_first + 1) % size_first
        rel_second = (owner % size_second - here_second + 1) % size_second
        ids = (rel_first * windows[1] + rel_second) * owner_size + proj_ids % owner_size
        grid = proj_energy.reshape(size_first, size_second, owner_size)
        grid = jnp.roll(grid, (1 - here_first, 1 - here_second), (0, 1))
        energy = grid[: windows[0], : windows[1]].reshape(rows, LANES)

    ids = jnp.transpose(ids, (0, 3, 1, 2)).reshape(slots * sz.zb * ex, ey)
    pv = proj_vals.reshape(slots * sz.cells, nz)
    pot = local_pot.reshape(sz.cells, nz)
    message_shapes = (
        jax.ShapeDtypeStruct((sz.edge_rows, LANES), F32),
        jax.ShapeDtypeStruct((sz.edge_rows + rows, LANES), F32),
        jax.ShapeDtypeStruct((sz.yedge_rows + rows, LANES), F32),
        jax.ShapeDtypeStruct((rows, LANES), F32),
    )
    field = jax.ShapeDtypeStruct((sz.cells, nz), F32)
    params = pltpu.CompilerParams(vmem_limit_bytes=48 << 20)

    def exchange(to_a, to_b, to_y, table):
        if whole:
            from_b = swap(to_b, lambda i, j: (size_first - 1 - i, j))
            from_y = swap(to_y, lambda i, j: (i, 1 - j))
            from_d = swap(table, lambda i, j: (size_first - 1 - i, 1 - j))
            from_a = swap(to_a, lambda i, j: (i ^ 1, j))
            table = table + from_d + from_b[sz.edge_rows :] + from_y[sz.yedge_rows :]
            other = swap(table, lambda i, j: (i ^ 1, j))
            return [table, other], from_a, from_b, [from_y]
        edges_b = to_b[: sz.edge_rows]
        edges_y = to_y[: sz.yedge_rows]
        below = shift(edges_y, "gy", 1)
        above = shift(edges_y, "gy", -1)
        from_a = shift(edges_b, "gx", -1)
        from_b = shift(to_a, "gx", 1)
        for dim, axis in ((1, "gy"), (0, "gx")):
            total = table
            for delta in offsets((size_first, size_second)[dim]):
                moved = shift(table, axis, -delta)
                total = total + shift_table(
                    moved, windows[0], windows[1], size_first, size_second, dim, delta
                )
            table = total
        return [table], from_a, from_b, [below, above]

    def one_orbital(start):
        *messages, row_of, hot = pl.pallas_call(
            functools.partial(first_kernel, sz),
            out_shape=message_shapes
            + (
                jax.ShapeDtypeStruct((slots * sz.zb, LANES), F32),
                jax.ShapeDtypeStruct((LANES, slots * sz.zb * sz.cells), BF16),
            ),
            in_specs=smem(1) + [pl.BlockSpec(memory_space=pltpu.HBM)] * 3,
            out_specs=tuple(vmem(6)),
            scratch_shapes=[
                pltpu.VMEM(start.shape, start.dtype),
                pltpu.VMEM(pv.shape, pv.dtype),
                pltpu.VMEM(ids.shape, ids.dtype),
                pltpu.SemaphoreType.DMA((3,)),
            ],
            compiler_params=pltpu.CompilerParams(vmem_limit_bytes=62 << 20),
            name="project_first",
        )(flag, start, pv, ids)
        history = [start]
        for degree in range(1, STEPS + 1):
            tables, from_a, from_b, from_y = exchange(*messages)
            last = degree == STEPS
            args = (from_a, from_b, *from_y, pot, *history)
            if last:
                args = (cheb, *args)
            rest = pl.pallas_call(
                functools.partial(local_kernel, sz, degree, len(from_y)),
                out_shape=field,
                in_specs=smem(1) + vmem(len(args)),
                out_specs=vmem(1)[0],
                compiler_params=params,
                name=f"local_{degree}",
            )(flag, *args)
            args = (*tables, energy, rest, pv, row_of, hot)
            if last:
                return pl.pallas_call(
                    functools.partial(last_kernel, sz, len(tables)),
                    out_shape=field,
                    in_specs=vmem(1 + len(args)),
                    out_specs=vmem(1)[0],
                    compiler_params=params,
                    name="filtered",
                )(cheb, *args)
            scalars = (flag, cheb_coef) if degree == 1 else (flag,)
            extra = (jax.ShapeDtypeStruct((SUBLANES, LANES), F32),) if degree == 1 else ()
            out = pl.pallas_call(
                functools.partial(nonlocal_kernel, sz, degree, len(tables)),
                out_shape=(field,) + message_shapes + extra,
                in_specs=smem(len(scalars)) + vmem(len(args)),
                out_specs=tuple(vmem(5 + len(extra))),
                compiler_params=params,
                name=f"nonlocal_{degree}",
            )(*scalars, *args)
            if degree == 1:
                cheb = out[-1]
            history.append(out[0])
            messages = out[1:5]

    density = one_orbital(orbitals[0].reshape(sz.cells, nz))
    for at in range(1, count_orb):
        density = density + one_orbital(orbitals[at].reshape(sz.cells, nz))
    scale = 1.0 / (count_orb * lax.axis_size("orb"))
    return orb_sum(density, scale).reshape(ex, ey, nz)


def solution(mesh):
    return jax.shard_map(
        local,
        mesh=mesh,
        in_specs=(
            P("orb", "gx", "gy", None),
            P("gx", "gy", None),
            P(None, "gx", "gy", None),
            P(None, "gx", "gy", None),
            P(),
            P(),
        ),
        out_specs=P("gx", "gy", None),
        check_vma=False,
    )
```

```python
import functools

import jax
import jax.numpy as jnp
from jax import lax
from jax.experimental import pallas as pl
from jax.experimental.pallas import tpu as pltpu
from jax.sharding import PartitionSpec as P

LANES = 128
SUBLANES = 8
STEPS = 3
E_MID = 4.0
E_HALF = 8.0
F32 = jnp.float32
BF16 = jnp.bfloat16


def pieces(vals):
    first = vals.astype(BF16)
    second = (vals - first.astype(F32)).astype(BF16)
    return first, second


def dot(a, b, contract):
    return lax.dot_general(a, b, (contract, ((), ())), preferred_element_type=F32)


NN = ((1,), (0,))
NT = ((1,), (1,))


def iota(shape, dim):
    return lax.broadcasted_iota(jnp.int32, shape, dim)


class Sizes:
    def __init__(self, extent_first, extent_second, extent_depth, slots, owner_size, rows):
        self.ex = extent_first
        self.ey = extent_second
        self.nz = extent_depth
        self.zb = extent_depth // LANES
        self.slots = slots
        self.cells = extent_first * extent_second
        self.rows = rows
        self.xedge = 2 * extent_second
        self.yedge = extent_first * SUBLANES // 2
        self.edge_rows = self.zb * self.xedge
        self.yedge_rows = self.zb * self.yedge
        assert extent_second == 2 * SUBLANES and extent_first % 2 == 0
        assert self.cells == LANES and extent_first == SUBLANES


def rows_of_ids(sz, ids):
    copies = jnp.where(
        jnp.bitwise_and(iota((sz.ey, LANES), 1), sz.ey - 1) == iota((sz.ey, LANES), 0), 1.0, 0.0
    ).astype(BF16)
    shape = (sz.slots * sz.zb, sz.ex, LANES)
    own = iota(shape, 2) // sz.ey == iota(shape, 1)

    def flat(part):
        spread = dot(part.astype(F32).astype(BF16), copies, NN).reshape(shape)
        return jnp.sum(jnp.where(own, spread, 0.0), axis=1)

    return flat(lax.shift_right_logical(ids, 7)), flat(jnp.bitwise_and(ids, LANES - 1))


def chunk(sz, arr, zb, slot):
    at = slot * sz.zb + zb
    return arr[at : at + 1, :]


def chunks(sz):
    return [(zb, slot) for zb in range(sz.zb) for slot in range(sz.slots)]


def partial_table(sz, vals, pv_ref, row_of, hot_ref):
    eye = iota((sz.cells, LANES), 0) == iota((sz.cells, LANES), 1)
    eye_all = jnp.concatenate([eye] * sz.slots, axis=0)
    spread_first, spread_second = [], []
    table_iota = iota((sz.rows, LANES), 0).astype(F32)
    for zb in range(sz.zb):
        first, second = pieces(vals[:, zb * LANES : (zb + 1) * LANES])
        weights = pv_ref[:, zb * LANES : (zb + 1) * LANES]
        cross = dot(
            jnp.concatenate([weights, weights], axis=1),
            jnp.concatenate([first, second], axis=1),
            NT,
        )
        cross = jnp.where(eye_all, cross, 0.0)
        for slot in range(sz.slots):
            sums = jnp.sum(
                cross[slot * sz.cells : (slot + 1) * sz.cells], axis=0, keepdims=True
            )
            spread = jnp.where(chunk(sz, row_of, zb, slot) == table_iota, sums, 0.0)
            a, b = pieces(spread)
            spread_first.append(a)
            spread_second.append(b)
    lhs = jnp.concatenate(
        [jnp.concatenate(spread_first, axis=1), jnp.concatenate(spread_second, axis=1)], axis=0
    )
    both = dot(lhs, hot_ref[...], NT)
    return both[: sz.rows] + both[sz.rows :]


def projected(sz, table, pv_ref, row_of, hot_ref):
    first, second = pieces(table)
    found = dot(jnp.concatenate([first, second], axis=0), hot_ref[...], NN)
    found = found[: sz.rows] + found[sz.rows :]
    table_iota = iota((sz.rows, LANES), 0).astype(F32)
    eye = iota((sz.cells, LANES), 0) == iota((sz.cells, LANES), 1)
    result = []
    for zb in range(sz.zb):
        diag_first, diag_second = [], []
        for slot in range(sz.slots):
            at = (zb * sz.slots + slot) * LANES
            hit = chunk(sz, row_of, zb, slot) == table_iota
            weight = jnp.sum(
                jnp.where(hit, found[:, at : at + LANES], 0.0), axis=0, keepdims=True
            )
            a, b = pieces(jnp.where(eye, weight, 0.0))
            diag_first.append(a)
            diag_second.append(b)
        lhs = jnp.concatenate(
            [jnp.concatenate(diag_first, axis=1), jnp.concatenate(diag_second, axis=1)], axis=0
        )
        both = dot(lhs, pv_ref[:, zb * LANES : (zb + 1) * LANES], NN)
        result.append(both[: sz.cells] + both[sz.cells :])
    return result


def from_message(sz, msg_ref, rows):
    return jnp.concatenate(
        [msg_ref[zb * rows : (zb + 1) * rows, :] for zb in range(sz.zb)], axis=1
    )


def to_message(sz, msg_ref, vals):
    rows = vals.shape[0]
    for zb in range(sz.zb):
        msg_ref[zb * rows : (zb + 1) * rows, :] = vals[:, zb * LANES : (zb + 1) * LANES]


def second_edges(sz, vals):
    tiles = vals.reshape(sz.ex, 2, SUBLANES, sz.nz)
    sub = iota((sz.ex // 2, SUBLANES, sz.nz), 1)
    even = tiles.reshape(sz.ex // 2, 2, 2, SUBLANES, sz.nz)
    outer_even = jnp.where(sub < 4, even[:, 0, 0], even[:, 0, 1])
    outer_odd = jnp.where(sub < 4, even[:, 1, 0], even[:, 1, 1])
    odd = pltpu.roll(outer_odd, 4, axis=1)
    keep = jnp.logical_or(sub < 2, sub >= 6)
    return jnp.where(keep, outer_even, odd).reshape(sz.yedge, sz.nz)


def second_halo(sz, packed):
    pairs = packed.reshape(sz.ex // 2, SUBLANES, sz.nz)
    odd = pltpu.roll(pairs, 4, axis=1)
    return jnp.stack([pairs, odd], axis=1).reshape(sz.ex, SUBLANES, sz.nz)


def stencil(sz, vals, low, high, below, above):
    result = -90.0 * vals
    tall = jnp.concatenate([low, vals, high], axis=0)
    step = sz.ey
    cells = sz.cells
    near = tall[step : step + cells] + tall[3 * step : 3 * step + cells]
    far = tall[0:cells] + tall[4 * step : 4 * step + cells]

    near = near + pltpu.roll(vals, 1, axis=1) + pltpu.roll(vals, sz.nz - 1, axis=1)
    far = far + pltpu.roll(vals, 2, axis=1) + pltpu.roll(vals, sz.nz - 2, axis=1)

    tiles = vals.reshape(2 * sz.ex, SUBLANES, sz.nz)
    sub = iota((2 * sz.ex, SUBLANES, sz.nz), 1)

    def shifted(amount, outer, from_below):
        mine = pltpu.roll(tiles, amount, axis=1)
        theirs = pltpu.roll(outer, amount, axis=1)
        pairs = mine.reshape(sz.ex, 2, SUBLANES, sz.nz)
        if from_below:
            other = jnp.stack([theirs, pairs[:, 0]], axis=1)
            mask = sub < amount
        else:
            other = jnp.stack([pairs[:, 1], theirs], axis=1)
            mask = sub >= amount
        return jnp.where(mask, other.reshape(tiles.shape), mine).reshape(vals.shape)

    near = near + shifted(1, below, True) + shifted(SUBLANES - 1, above, False)
    far = far + shifted(2, below, True) + shifted(SUBLANES - 2, above, False)
    return result + 16.0 * near - far


def emit(sz, vals, flag_ref, pv_ref, row_of, hot_ref, ab_ref, bb_ref, yb_ref, table_ref):
    table = partial_table(sz, vals, pv_ref, row_of, hot_ref)
    table_ref[...] = table
    flag = flag_ref[0]
    top = vals[sz.cells - sz.xedge :]
    bottom = vals[: sz.xedge]
    is_high = flag == 0
    to_message(sz, ab_ref, jnp.where(is_high, top, bottom))
    to_message(sz, bb_ref, jnp.where(is_high, bottom, top))
    bb_ref[sz.edge_rows :, :] = table
    to_message(sz, yb_ref, second_edges(sz, vals))
    yb_ref[sz.yedge_rows :, :] = table


def first_kernel(
    sz,
    flag_ref,
    vals_hbm,
    pv_hbm,
    ids_hbm,
    cheb_hbm,
    ab_ref,
    bb_ref,
    yb_ref,
    table_ref,
    rows_ref,
    hot_ref,
    cheb_out,
    vals_ref,
    pv_ref,
    ids_ref,
    cheb_ref,
    sems,
):
    get_ids = pltpu.make_async_copy(ids_hbm, ids_ref, sems.at[0])
    get_pv = pltpu.make_async_copy(pv_hbm, pv_ref, sems.at[1])
    get_vals = pltpu.make_async_copy(vals_hbm, vals_ref, sems.at[2])
    get_cheb = pltpu.make_async_copy(cheb_hbm, cheb_ref, sems.at[3])
    get_ids.start()
    get_vals.start()
    get_pv.start()
    get_cheb.start()
    get_ids.wait()
    row_of, lane_of = rows_of_ids(sz, ids_ref[...])
    rows_ref[...] = row_of
    lane_iota = iota((LANES, LANES), 0).astype(F32)
    for at, (zb, slot) in enumerate(chunks(sz)):
        hot_ref[:, at * LANES : (at + 1) * LANES] = jnp.where(
            chunk(sz, lane_of, zb, slot) == lane_iota, 1.0, 0.0
        ).astype(BF16)
    get_vals.wait()
    get_pv.wait()
    emit(
        sz, vals_ref[...], flag_ref, pv_ref, row_of, hot_ref, ab_ref, bb_ref, yb_ref, table_ref
    )
    get_cheb.wait()
    for n in range(STEPS + 1):
        cheb_out[n : n + 1, :] = jnp.full((1, LANES), cheb_ref[n], F32)


def coefficient(sz, cheb_ref, n):
    row = cheb_ref[n : n + 1, :]
    return jnp.concatenate([row] * sz.zb, axis=1)


def local_kernel(sz, degree, n_y, flag_ref, *refs):
    refs = list(refs)
    cheb_ref = refs.pop(0) if degree == STEPS else None
    a_ref, b_ref = refs.pop(0), refs.pop(0)
    y_refs = [refs.pop(0) for _ in range(n_y)]
    pot_ref = refs.pop(0)
    *history, out_ref = refs
    vals = history[-1][...]

    from_a = from_message(sz, a_ref, sz.xedge)
    from_b = from_message(sz, b_ref, sz.xedge)
    is_high = flag_ref[0] == 0
    low = jnp.where(is_high, from_b, from_a)
    high = jnp.where(is_high, from_a, from_b)
    outer = [second_halo(sz, from_message(sz, ref, sz.yedge)) for ref in y_refs]
    laplace12 = stencil(sz, vals, low, high, outer[0], outer[-1])
    double = 1.0 if degree == 1 else 2.0
    result = laplace12 * (-0.5 / 12.0 / E_HALF * double) + vals * (
        (pot_ref[...] - E_MID) * (double / E_HALF)
    )
    if degree > 1:
        result = result - history[-2][...]
    if degree == STEPS:
        result = coefficient(sz, cheb_ref, STEPS) * result
        for n in range(STEPS):
            result = result + coefficient(sz, cheb_ref, n) * history[n][...]
    out_ref[...] = result


def added(table_refs):
    table = table_refs[0][...]
    for ref in table_refs[1:]:
        table = table + ref[...]
    return table


def nonlocal_kernel(sz, degree, n_tables, flag_ref, *refs):
    refs = list(refs)
    table_refs = [refs.pop(0) for _ in range(n_tables)]
    energy_ref, rest_ref, pv_ref, rows_ref, hot_ref = (refs.pop(0) for _ in range(5))
    row_of = rows_ref[...]
    double = 1.0 if degree == 1 else 2.0
    table = added(table_refs) * (energy_ref[...] * (double / E_HALF))
    result = rest_ref[...] + jnp.concatenate(
        projected(sz, table, pv_ref, row_of, hot_ref), axis=1
    )
    refs[0][...] = result
    emit(sz, result, flag_ref, pv_ref, row_of, hot_ref, *refs[1:])


def last_kernel(sz, n_tables, cheb_ref, *refs):
    refs = list(refs)
    table_refs = [refs.pop(0) for _ in range(n_tables)]
    energy_ref, rest_ref, pv_ref, rows_ref, hot_ref, out_ref = refs
    table = added(table_refs) * (energy_ref[...] * (2.0 / E_HALF * cheb_ref[STEPS : STEPS + 1, :]))
    result = rest_ref[...] + jnp.concatenate(
        projected(sz, table, pv_ref, rows_ref[...], hot_ref), axis=1
    )
    out_ref[...] = result * result


def vmem(count):
    return [pl.BlockSpec(memory_space=pltpu.VMEM)] * count


def smem(count):
    return [pl.BlockSpec(memory_space=pltpu.SMEM)] * count


def in_place(arr):
    return pltpu.with_memory_space_constraint(arr, pltpu.HBM)


def shift_table(table, blocks_first, blocks_second, size_first, size_second, dim, delta):
    blocks = table.reshape(blocks_first, blocks_second, -1)
    count = blocks.shape[dim]
    size = (size_first, size_second)[dim]
    parts = []
    for at in range(count):
        source = [s for s in range(count) if (s + delta) % size == at]
        if source:
            parts.append(lax.slice_in_dim(blocks, source[0], source[0] + 1, axis=dim))
        else:
            parts.append(jnp.zeros_like(lax.slice_in_dim(blocks, 0, 1, axis=dim)))
    return jnp.concatenate(parts, axis=dim).reshape(table.shape)


def offsets(size):
    return sorted({d % size for d in (-2, -1, 1, 2)} - {0})


def shift(arr, axis, amount):
    size = lax.axis_size(axis)
    return lax.ppermute(arr, axis, [(i, (i + amount) % size) for i in range(size)])


def swap(arr, target):
    size_first = lax.axis_size("gx")
    size_second = lax.axis_size("gy")
    pairs = []
    for i in range(size_first):
        for j in range(size_second):
            ti, tj = target(i, j)
            pairs.append((i * size_second + j, ti * size_second + tj))
    return lax.ppermute(arr, ("gx", "gy"), pairs)


def orb_sum(vals, scale):
    size = lax.axis_size("orb")
    if size != 4:
        return lax.psum(vals, "orb") * scale
    vals = vals + lax.ppermute(vals, "orb", [(i, i ^ 1) for i in range(4)])
    return (vals + lax.ppermute(vals, "orb", [(i, 3 - i) for i in range(4)])) * scale


def local(orbitals, local_pot, proj_vals, proj_ids, proj_energy, cheb_coef):
    count_orb, ex, ey, nz = orbitals.shape
    slots = proj_vals.shape[0]
    size_first = lax.axis_size("gx")
    size_second = lax.axis_size("gy")
    owner_size = proj_energy.shape[0] // (size_first * size_second)
    whole = size_first == 4 and size_second == 2
    if whole:
        windows = (size_first, size_second)
    else:
        windows = (min(3, size_first), min(3, size_second))
    rows = windows[0] * windows[1] * owner_size // LANES
    sz = Sizes(ex, ey, nz, slots, owner_size, rows)
    here_first = lax.axis_index("gx")
    here_second = lax.axis_index("gy")

    if whole:
        flag = jnp.bitwise_and(here_first, 1).astype(jnp.int32).reshape(1)
        energy = proj_energy.reshape(rows, LANES)
        ids = proj_ids
    else:
        flag = jnp.zeros((1,), jnp.int32)
        owner = proj_ids // owner_size
        rel_first = (owner // size_second - here_first + 1) % size_first
        rel_second = (owner % size_second - here_second + 1) % size_second
        ids = (rel_first * windows[1] + rel_second) * owner_size + proj_ids % owner_size
        grid = proj_energy.reshape(size_first, size_second, owner_size)
        grid = jnp.roll(grid, (1 - here_first, 1 - here_second), (0, 1))
        energy = grid[: windows[0], : windows[1]].reshape(rows, LANES)

    ids = jnp.transpose(ids, (0, 3, 1, 2)).reshape(slots * sz.zb * ex, ey)
    pv = proj_vals.reshape(slots * sz.cells, nz)
    pot = local_pot.reshape(sz.cells, nz)
    message_shapes = (
        jax.ShapeDtypeStruct((sz.edge_rows, LANES), F32),
        jax.ShapeDtypeStruct((sz.edge_rows + rows, LANES), F32),
        jax.ShapeDtypeStruct((sz.yedge_rows + rows, LANES), F32),
        jax.ShapeDtypeStruct((rows, LANES), F32),
    )
    field = jax.ShapeDtypeStruct((sz.cells, nz), F32)
    params = pltpu.CompilerParams(vmem_limit_bytes=48 << 20)

    def exchange(to_a, to_b, to_y, table):
        if whole:
            from_b = swap(to_b, lambda i, j: (size_first - 1 - i, j))
            from_y = swap(to_y, lambda i, j: (i, 1 - j))
            from_d = swap(table, lambda i, j: (size_first - 1 - i, 1 - j))
            from_a = swap(to_a, lambda i, j: (i ^ 1, j))
            table = table + from_d + from_b[sz.edge_rows :] + from_y[sz.yedge_rows :]
            other = swap(table, lambda i, j: (i ^ 1, j))
            return [table, other], from_a, from_b, [from_y]
        edges_b = to_b[: sz.edge_rows]
        edges_y = to_y[: sz.yedge_rows]
        below = shift(edges_y, "gy", 1)
        above = shift(edges_y, "gy", -1)
        from_a = shift(edges_b, "gx", -1)
        from_b = shift(to_a, "gx", 1)
        for dim, axis in ((1, "gy"), (0, "gx")):
            total = table
            for delta in offsets((size_first, size_second)[dim]):
                moved = shift(table, axis, -delta)
                total = total + shift_table(
                    moved, windows[0], windows[1], size_first, size_second, dim, delta
                )
            table = total
        return [table], from_a, from_b, [below, above]

    def one_orbital(start):
        *messages, row_of, hot, cheb = pl.pallas_call(
            functools.partial(first_kernel, sz),
            out_shape=message_shapes
            + (
                jax.ShapeDtypeStruct((slots * sz.zb, LANES), F32),
                jax.ShapeDtypeStruct((LANES, slots * sz.zb * sz.cells), BF16),
                jax.ShapeDtypeStruct((SUBLANES, LANES), F32),
            ),
            in_specs=smem(1) + [pl.BlockSpec(memory_space=pltpu.HBM)] * 4,
            out_specs=tuple(vmem(7)),
            scratch_shapes=[
                pltpu.VMEM(start.shape, start.dtype),
                pltpu.VMEM(pv.shape, pv.dtype),
                pltpu.VMEM(ids.shape, ids.dtype),
                pltpu.SMEM(cheb_coef.shape, cheb_coef.dtype),
                pltpu.SemaphoreType.DMA((4,)),
            ],
            compiler_params=params,
            name="project_first",
        )(flag, *(in_place(arr) for arr in (start, pv, ids, cheb_coef)))
        history = [start]
        for degree in range(1, STEPS + 1):
            tables, from_a, from_b, from_y = exchange(*messages)
            last = degree == STEPS
            args = (from_a, from_b, *from_y, pot, *history)
            if last:
                args = (cheb, *args)
            rest = pl.pallas_call(
                functools.partial(local_kernel, sz, degree, len(from_y)),
                out_shape=field,
                in_specs=smem(1) + vmem(len(args)),
                out_specs=vmem(1)[0],
                compiler_params=params,
                name=f"local_{degree}",
            )(flag, *args)
            args = (*tables, energy, rest, pv, row_of, hot)
            if last:
                return pl.pallas_call(
                    functools.partial(last_kernel, sz, len(tables)),
                    out_shape=field,
                    in_specs=vmem(1 + len(args)),
                    out_specs=vmem(1)[0],
                    compiler_params=params,
                    name="filtered",
                )(cheb, *args)
            out = pl.pallas_call(
                functools.partial(nonlocal_kernel, sz, degree, len(tables)),
                out_shape=(field,) + message_shapes,
                in_specs=smem(1) + vmem(len(args)),
                out_specs=tuple(vmem(5)),
                compiler_params=params,
                name=f"nonlocal_{degree}",
            )(flag, *args)
            history.append(out[0])
            messages = out[1:]

    density = one_orbital(orbitals[0].reshape(sz.cells, nz))
    for at in range(1, count_orb):
        density = density + one_orbital(orbitals[at].reshape(sz.cells, nz))
    scale = 1.0 / (count_orb * lax.axis_size("orb"))
    return orb_sum(density, scale).reshape(ex, ey, nz)


def solution(mesh):
    return jax.shard_map(
        local,
        mesh=mesh,
        in_specs=(
            P("orb", "gx", "gy", None),
            P("gx", "gy", None),
            P(None, "gx", "gy", None),
            P(None, "gx", "gy", None),
            P(),
            P(),
        ),
        out_specs=P("gx", "gy", None),
        check_vma=False,
    )
```

```python
import functools

import jax
import jax.numpy as jnp
from jax import lax
from jax.experimental import pallas as pl
from jax.experimental.pallas import tpu as pltpu
from jax.sharding import PartitionSpec as P

LANES = 128
SUBLANES = 8
STEPS = 3
E_MID = 4.0
E_HALF = 8.0
F32 = jnp.float32
BF16 = jnp.bfloat16


def pieces(vals):
    first = vals.astype(BF16)
    second = (vals - first.astype(F32)).astype(BF16)
    return first, second


def dot(a, b, contract):
    return lax.dot_general(a, b, (contract, ((), ())), preferred_element_type=F32)


NN = ((1,), (0,))
NT = ((1,), (1,))


def iota(shape, dim):
    return lax.broadcasted_iota(jnp.int32, shape, dim)


class Sizes:
    def __init__(self, extent_first, extent_second, extent_depth, slots, owner_size, rows):
        self.ex = extent_first
        self.ey = extent_second
        self.nz = extent_depth
        self.zb = extent_depth // LANES
        self.slots = slots
        self.cells = extent_first * extent_second
        self.rows = rows
        self.xedge = 2 * extent_second
        self.yedge = extent_first * SUBLANES // 2
        self.edge_rows = self.zb * self.xedge
        self.yedge_rows = self.zb * self.yedge
        assert extent_second == 2 * SUBLANES and extent_first % 2 == 0
        assert self.cells == LANES and extent_first == SUBLANES


def rows_of_ids(sz, ids):
    copies = jnp.where(
        jnp.bitwise_and(iota((sz.ey, LANES), 1), sz.ey - 1) == iota((sz.ey, LANES), 0), 1.0, 0.0
    ).astype(BF16)
    shape = (sz.slots * sz.zb, sz.ex, LANES)
    own = iota(shape, 2) // sz.ey == iota(shape, 1)

    def flat(part):
        spread = dot(part.astype(F32).astype(BF16), copies, NN).reshape(shape)
        return jnp.sum(jnp.where(own, spread, 0.0), axis=1)

    return flat(lax.shift_right_logical(ids, 7)), flat(jnp.bitwise_and(ids, LANES - 1))


def chunk(sz, arr, zb, slot):
    at = slot * sz.zb + zb
    return arr[at : at + 1, :]


def chunks(sz):
    return [(zb, slot) for zb in range(sz.zb) for slot in range(sz.slots)]


def partial_table(sz, vals, pv_ref, row_of, hot_ref):
    eye = iota((sz.cells, LANES), 0) == iota((sz.cells, LANES), 1)
    eye_all = jnp.concatenate([eye] * sz.slots, axis=0)
    spread_first, spread_second = [], []
    table_iota = iota((sz.rows, LANES), 0).astype(F32)
    for zb in range(sz.zb):
        first, second = pieces(vals[:, zb * LANES : (zb + 1) * LANES])
        weights = pv_ref[:, zb * LANES : (zb + 1) * LANES]
        cross = dot(
            jnp.concatenate([weights, weights], axis=1),
            jnp.concatenate([first, second], axis=1),
            NT,
        )
        cross = jnp.where(eye_all, cross, 0.0)
        for slot in range(sz.slots):
            sums = jnp.sum(
                cross[slot * sz.cells : (slot + 1) * sz.cells], axis=0, keepdims=True
            )
            spread = jnp.where(chunk(sz, row_of, zb, slot) == table_iota, sums, 0.0)
            a, b = pieces(spread)
            spread_first.append(a)
            spread_second.append(b)
    lhs = jnp.concatenate(
        [jnp.concatenate(spread_first, axis=1), jnp.concatenate(spread_second, axis=1)], axis=0
    )
    both = dot(lhs, hot_ref[...], NT)
    return both[: sz.rows] + both[sz.rows :]


def projected(sz, tables, pv_ref, row_of, hot_ref):
    count = len(tables)
    split = [piece for table in tables for piece in pieces(table)]
    found = dot(jnp.concatenate(split, axis=0), hot_ref[...], NN)
    found = [
        found[2 * n * sz.rows : (2 * n + 1) * sz.rows]
        + found[(2 * n + 1) * sz.rows : (2 * n + 2) * sz.rows]
        for n in range(count)
    ]
    table_iota = iota((sz.rows, LANES), 0).astype(F32)
    eye = iota((sz.cells, LANES), 0) == iota((sz.cells, LANES), 1)
    result = [[] for _ in tables]
    for zb in range(sz.zb):
        diag = [[] for _ in range(2 * count)]
        for slot in range(sz.slots):
            at = (zb * sz.slots + slot) * LANES
            hit = chunk(sz, row_of, zb, slot) == table_iota
            for n in range(count):
                weight = jnp.sum(
                    jnp.where(hit, found[n][:, at : at + LANES], 0.0), axis=0, keepdims=True
                )
                a, b = pieces(jnp.where(eye, weight, 0.0))
                diag[2 * n].append(a)
                diag[2 * n + 1].append(b)
        lhs = jnp.concatenate([jnp.concatenate(parts, axis=1) for parts in diag], axis=0)
        both = dot(lhs, pv_ref[:, zb * LANES : (zb + 1) * LANES], NN)
        for n in range(count):
            at = 2 * n * sz.cells
            result[n].append(both[at : at + sz.cells] + both[at + sz.cells : at + 2 * sz.cells])
    return [jnp.concatenate(parts, axis=1) for parts in result]


def from_message(sz, msg_ref, rows):
    return jnp.concatenate(
        [msg_ref[zb * rows : (zb + 1) * rows, :] for zb in range(sz.zb)], axis=1
    )


def to_message(sz, msg_ref, vals):
    rows = vals.shape[0]
    for zb in range(sz.zb):
        msg_ref[zb * rows : (zb + 1) * rows, :] = vals[:, zb * LANES : (zb + 1) * LANES]


def second_edges(sz, vals):
    tiles = vals.reshape(sz.ex, 2, SUBLANES, sz.nz)
    sub = iota((sz.ex // 2, SUBLANES, sz.nz), 1)
    even = tiles.reshape(sz.ex // 2, 2, 2, SUBLANES, sz.nz)
    outer_even = jnp.where(sub < 4, even[:, 0, 0], even[:, 0, 1])
    outer_odd = jnp.where(sub < 4, even[:, 1, 0], even[:, 1, 1])
    odd = pltpu.roll(outer_odd, 4, axis=1)
    keep = jnp.logical_or(sub < 2, sub >= 6)
    return jnp.where(keep, outer_even, odd).reshape(sz.yedge, sz.nz)


def second_halo(sz, packed):
    pairs = packed.reshape(sz.ex // 2, SUBLANES, sz.nz)
    odd = pltpu.roll(pairs, 4, axis=1)
    return jnp.stack([pairs, odd], axis=1).reshape(sz.ex, SUBLANES, sz.nz)


def stencil(sz, vals, low, high, below, above):
    result = -90.0 * vals
    tall = jnp.concatenate([low, vals, high], axis=0)
    step = sz.ey
    cells = sz.cells
    near = tall[step : step + cells] + tall[3 * step : 3 * step + cells]
    far = tall[0:cells] + tall[4 * step : 4 * step + cells]

    near = near + pltpu.roll(vals, 1, axis=1) + pltpu.roll(vals, sz.nz - 1, axis=1)
    far = far + pltpu.roll(vals, 2, axis=1) + pltpu.roll(vals, sz.nz - 2, axis=1)

    tiles = vals.reshape(2 * sz.ex, SUBLANES, sz.nz)
    sub = iota((2 * sz.ex, SUBLANES, sz.nz), 1)

    def shifted(amount, outer, from_below):
        mine = pltpu.roll(tiles, amount, axis=1)
        theirs = pltpu.roll(outer, amount, axis=1)
        pairs = mine.reshape(sz.ex, 2, SUBLANES, sz.nz)
        if from_below:
            other = jnp.stack([theirs, pairs[:, 0]], axis=1)
            mask = sub < amount
        else:
            other = jnp.stack([pairs[:, 1], theirs], axis=1)
            mask = sub >= amount
        return jnp.where(mask, other.reshape(tiles.shape), mine).reshape(vals.shape)

    near = near + shifted(1, below, True) + shifted(SUBLANES - 1, above, False)
    far = far + shifted(2, below, True) + shifted(SUBLANES - 2, above, False)
    return result + 16.0 * near - far


def emit(sz, vals, flag_ref, pv_ref, row_of, hot_ref, ab_ref, bb_ref, yb_ref, table_ref):
    table = partial_table(sz, vals, pv_ref, row_of, hot_ref)
    table_ref[...] = table
    flag = flag_ref[0]
    top = vals[sz.cells - sz.xedge :]
    bottom = vals[: sz.xedge]
    is_high = flag == 0
    to_message(sz, ab_ref, jnp.where(is_high, top, bottom))
    to_message(sz, bb_ref, jnp.where(is_high, bottom, top))
    bb_ref[sz.edge_rows :, :] = table
    to_message(sz, yb_ref, second_edges(sz, vals))
    yb_ref[sz.yedge_rows :, :] = table


def first_kernel(
    sz,
    flag_ref,
    vals_hbm,
    pv_hbm,
    ids_hbm,
    cheb_hbm,
    ab_ref,
    bb_ref,
    yb_ref,
    table_ref,
    rows_ref,
    hot_ref,
    cheb_out,
    vals_ref,
    pv_ref,
    ids_ref,
    cheb_ref,
    sems,
):
    get_ids = pltpu.make_async_copy(ids_hbm, ids_ref, sems.at[0])
    get_pv = pltpu.make_async_copy(pv_hbm, pv_ref, sems.at[1])
    get_vals = pltpu.make_async_copy(vals_hbm, vals_ref, sems.at[2])
    get_cheb = pltpu.make_async_copy(cheb_hbm, cheb_ref, sems.at[3])
    get_ids.start()
    get_vals.start()
    get_pv.start()
    get_cheb.start()
    get_ids.wait()
    row_of, lane_of = rows_of_ids(sz, ids_ref[...])
    rows_ref[...] = row_of
    lane_iota = iota((LANES, LANES), 0).astype(F32)
    for at, (zb, slot) in enumerate(chunks(sz)):
        hot_ref[:, at * LANES : (at + 1) * LANES] = jnp.where(
            chunk(sz, lane_of, zb, slot) == lane_iota, 1.0, 0.0
        ).astype(BF16)
    get_vals.wait()
    get_pv.wait()
    emit(
        sz, vals_ref[...], flag_ref, pv_ref, row_of, hot_ref, ab_ref, bb_ref, yb_ref, table_ref
    )
    get_cheb.wait()
    for n in range(STEPS + 1):
        cheb_out[n : n + 1, :] = jnp.full((1, LANES), cheb_ref[n], F32)


def coefficient(sz, cheb_ref, n):
    row = cheb_ref[n : n + 1, :]
    return jnp.concatenate([row] * sz.zb, axis=1)


def local_kernel(sz, degree, n_y, flag_ref, *refs):
    refs = list(refs)
    cheb_ref = refs.pop(0) if degree == STEPS else None
    a_ref, b_ref = refs.pop(0), refs.pop(0)
    y_refs = [refs.pop(0) for _ in range(n_y)]
    pot_ref = refs.pop(0)
    *history, out_ref = refs
    vals = history[-1][...]

    from_a = from_message(sz, a_ref, sz.xedge)
    from_b = from_message(sz, b_ref, sz.xedge)
    is_high = flag_ref[0] == 0
    low = jnp.where(is_high, from_b, from_a)
    high = jnp.where(is_high, from_a, from_b)
    outer = [second_halo(sz, from_message(sz, ref, sz.yedge)) for ref in y_refs]
    laplace12 = stencil(sz, vals, low, high, outer[0], outer[-1])
    double = 1.0 if degree == 1 else 2.0
    result = laplace12 * (-0.5 / 12.0 / E_HALF * double) + vals * (
        (pot_ref[...] - E_MID) * (double / E_HALF)
    )
    if degree > 1:
        result = result - history[-2][...]
    if degree == STEPS:
        result = coefficient(sz, cheb_ref, STEPS) * result
        for n in range(STEPS):
            result = result + coefficient(sz, cheb_ref, n) * history[n][...]
    out_ref[...] = result


def added(table_refs):
    table = table_refs[0][...]
    for ref in table_refs[1:]:
        table = table + ref[...]
    return table


def nonlocal_kernel(sz, degree, n_tables, flag_ref, *refs):
    refs = list(refs)
    table_refs = [refs.pop(0) for _ in range(n_tables)]
    energy_ref, rest_ref, pv_ref, rows_ref, hot_ref = (refs.pop(0) for _ in range(5))
    row_of = rows_ref[...]
    double = 1.0 if degree == 1 else 2.0
    table = added(table_refs) * (energy_ref[...] * (double / E_HALF))
    result = rest_ref[...] + projected(sz, [table], pv_ref, row_of, hot_ref)[0]
    refs[0][...] = result
    emit(sz, result, flag_ref, pv_ref, row_of, hot_ref, *refs[1:])


def last_kernel(sz, n_orbitals, n_tables, cheb_ref, *refs):
    refs = list(refs)
    energy_ref, pv_ref, rows_ref, hot_ref = (refs.pop(0) for _ in range(4))
    scale = energy_ref[...] * (2.0 / E_HALF * cheb_ref[STEPS : STEPS + 1, :])
    rests, tables = [], []
    for _ in range(n_orbitals):
        rests.append(refs.pop(0))
        tables.append(added([refs.pop(0) for _ in range(n_tables)]) * scale)
    total = None
    for rest_ref, part in zip(rests, projected(sz, tables, pv_ref, rows_ref[...], hot_ref)):
        filtered = rest_ref[...] + part
        squared = filtered * filtered
        total = squared if total is None else total + squared
    refs[0][...] = total


def vmem(count):
    return [pl.BlockSpec(memory_space=pltpu.VMEM)] * count


def smem(count):
    return [pl.BlockSpec(memory_space=pltpu.SMEM)] * count


def in_place(arr):
    return pltpu.with_memory_space_constraint(arr, pltpu.HBM)


def shift_table(table, blocks_first, blocks_second, size_first, size_second, dim, delta):
    blocks = table.reshape(blocks_first, blocks_second, -1)
    count = blocks.shape[dim]
    size = (size_first, size_second)[dim]
    parts = []
    for at in range(count):
        source = [s for s in range(count) if (s + delta) % size == at]
        if source:
            parts.append(lax.slice_in_dim(blocks, source[0], source[0] + 1, axis=dim))
        else:
            parts.append(jnp.zeros_like(lax.slice_in_dim(blocks, 0, 1, axis=dim)))
    return jnp.concatenate(parts, axis=dim).reshape(table.shape)


def offsets(size):
    return sorted({d % size for d in (-2, -1, 1, 2)} - {0})


def shift(arr, axis, amount):
    size = lax.axis_size(axis)
    return lax.ppermute(arr, axis, [(i, (i + amount) % size) for i in range(size)])


def swap(arr, target):
    size_first = lax.axis_size("gx")
    size_second = lax.axis_size("gy")
    pairs = []
    for i in range(size_first):
        for j in range(size_second):
            ti, tj = target(i, j)
            pairs.append((i * size_second + j, ti * size_second + tj))
    return lax.ppermute(arr, ("gx", "gy"), pairs)


def orb_swap(vals, bit):
    size = lax.axis_size("orb")
    return lax.ppermute(vals, "orb", [(i, i ^ bit) for i in range(size)])


def local(orbitals, local_pot, proj_vals, proj_ids, proj_energy, cheb_coef):
    count_orb, ex, ey, nz = orbitals.shape
    slots = proj_vals.shape[0]
    size_first = lax.axis_size("gx")
    size_second = lax.axis_size("gy")
    size_orb = lax.axis_size("orb")
    paired = size_orb == 4 and count_orb == 1
    owner_size = proj_energy.shape[0] // (size_first * size_second)
    whole = size_first == 4 and size_second == 2
    if whole:
        windows = (size_first, size_second)
    else:
        windows = (min(3, size_first), min(3, size_second))
    rows = windows[0] * windows[1] * owner_size // LANES
    sz = Sizes(ex, ey, nz, slots, owner_size, rows)
    here_first = lax.axis_index("gx")
    here_second = lax.axis_index("gy")

    if whole:
        flag = jnp.bitwise_and(here_first, 1).astype(jnp.int32).reshape(1)
        energy = proj_energy.reshape(rows, LANES)
        ids = proj_ids
    else:
        flag = jnp.zeros((1,), jnp.int32)
        owner = proj_ids // owner_size
        rel_first = (owner // size_second - here_first + 1) % size_first
        rel_second = (owner % size_second - here_second + 1) % size_second
        ids = (rel_first * windows[1] + rel_second) * owner_size + proj_ids % owner_size
        grid = proj_energy.reshape(size_first, size_second, owner_size)
        grid = jnp.roll(grid, (1 - here_first, 1 - here_second), (0, 1))
        energy = grid[: windows[0], : windows[1]].reshape(rows, LANES)

    ids = jnp.transpose(ids, (0, 3, 1, 2)).reshape(slots * sz.zb * ex, ey)
    pv = proj_vals.reshape(slots * sz.cells, nz)
    pot = local_pot.reshape(sz.cells, nz)
    message_shapes = (
        jax.ShapeDtypeStruct((sz.edge_rows, LANES), F32),
        jax.ShapeDtypeStruct((sz.edge_rows + rows, LANES), F32),
        jax.ShapeDtypeStruct((sz.yedge_rows + rows, LANES), F32),
        jax.ShapeDtypeStruct((rows, LANES), F32),
    )
    field = jax.ShapeDtypeStruct((sz.cells, nz), F32)
    params = pltpu.CompilerParams(vmem_limit_bytes=48 << 20)

    def exchange(to_a, to_b, to_y, table):
        if whole:
            from_b = swap(to_b, lambda i, j: (size_first - 1 - i, j))
            from_y = swap(to_y, lambda i, j: (i, 1 - j))
            from_d = swap(table, lambda i, j: (size_first - 1 - i, 1 - j))
            from_a = swap(to_a, lambda i, j: (i ^ 1, j))
            table = table + from_d + from_b[sz.edge_rows :] + from_y[sz.yedge_rows :]
            other = swap(table, lambda i, j: (i ^ 1, j))
            return [table, other], from_a, from_b, [from_y]
        edges_b = to_b[: sz.edge_rows]
        edges_y = to_y[: sz.yedge_rows]
        below = shift(edges_y, "gy", 1)
        above = shift(edges_y, "gy", -1)
        from_a = shift(edges_b, "gx", -1)
        from_b = shift(to_a, "gx", 1)
        for dim, axis in ((1, "gy"), (0, "gx")):
            total = table
            for delta in offsets((size_first, size_second)[dim]):
                moved = shift(table, axis, -delta)
                total = total + shift_table(
                    moved, windows[0], windows[1], size_first, size_second, dim, delta
                )
            table = total
        return [table], from_a, from_b, [below, above]

    def one_orbital(start):
        *messages, row_of, hot, cheb = pl.pallas_call(
            functools.partial(first_kernel, sz),
            out_shape=message_shapes
            + (
                jax.ShapeDtypeStruct((slots * sz.zb, LANES), F32),
                jax.ShapeDtypeStruct((LANES, slots * sz.zb * sz.cells), BF16),
                jax.ShapeDtypeStruct((SUBLANES, LANES), F32),
            ),
            in_specs=smem(1) + [pl.BlockSpec(memory_space=pltpu.HBM)] * 4,
            out_specs=tuple(vmem(7)),
            scratch_shapes=[
                pltpu.VMEM(start.shape, start.dtype),
                pltpu.VMEM(pv.shape, pv.dtype),
                pltpu.VMEM(ids.shape, ids.dtype),
                pltpu.SMEM(cheb_coef.shape, cheb_coef.dtype),
                pltpu.SemaphoreType.DMA((4,)),
            ],
            compiler_params=params,
            name="project_first",
        )(flag, *(in_place(arr) for arr in (start, pv, ids, cheb_coef)))
        history = [start]
        for degree in range(1, STEPS + 1):
            tables, from_a, from_b, from_y = exchange(*messages)
            last = degree == STEPS
            args = (from_a, from_b, *from_y, pot, *history)
            if last:
                args = (cheb, *args)
            rest = pl.pallas_call(
                functools.partial(local_kernel, sz, degree, len(from_y)),
                out_shape=field,
                in_specs=smem(1) + vmem(len(args)),
                out_specs=vmem(1)[0],
                compiler_params=params,
                name=f"local_{degree}",
            )(flag, *args)
            if last:
                orbitals_here = [(rest, *tables)]
                if paired:
                    total = functools.reduce(jnp.add, tables)
                    orbitals_here = [(rest, total), (orb_swap(rest, 2), orb_swap(total, 2))]
                args = (cheb, energy, pv, row_of, hot, *sum(orbitals_here, ()))
                return pl.pallas_call(
                    functools.partial(
                        last_kernel, sz, len(orbitals_here), len(orbitals_here[0]) - 1
                    ),
                    out_shape=field,
                    in_specs=vmem(len(args)),
                    out_specs=vmem(1)[0],
                    compiler_params=params,
                    name="filtered",
                )(*args)
            args = (*tables, energy, rest, pv, row_of, hot)
            out = pl.pallas_call(
                functools.partial(nonlocal_kernel, sz, degree, len(tables)),
                out_shape=(field,) + message_shapes,
                in_specs=smem(1) + vmem(len(args)),
                out_specs=tuple(vmem(5)),
                compiler_params=params,
                name=f"nonlocal_{degree}",
            )(flag, *args)
            history.append(out[0])
            messages = out[1:]

    density = one_orbital(orbitals[0].reshape(sz.cells, nz))
    for at in range(1, count_orb):
        density = density + one_orbital(orbitals[at].reshape(sz.cells, nz))
    scale = 1.0 / (count_orb * size_orb)
    if paired:
        density = density + orb_swap(density, 1)
    else:
        density = lax.psum(density, "orb")
    return (density * scale).reshape(ex, ey, nz)


def solution(mesh):
    return jax.shard_map(
        local,
        mesh=mesh,
        in_specs=(
            P("orb", "gx", "gy", None),
            P("gx", "gy", None),
            P(None, "gx", "gy", None),
            P(None, "gx", "gy", None),
            P(),
            P(),
        ),
        out_specs=P("gx", "gy", None),
        check_vma=False,
    )
```

```python
import functools

import jax
import jax.numpy as jnp
from jax import lax
from jax.experimental import pallas as pl
from jax.experimental.pallas import tpu as pltpu
from jax.sharding import PartitionSpec as P

LANES = 128
SUBLANES = 8
STEPS = 3
E_MID = 4.0
E_HALF = 8.0
F32 = jnp.float32
BF16 = jnp.bfloat16


def pieces(vals):
    first = vals.astype(BF16)
    second = (vals - first.astype(F32)).astype(BF16)
    return first, second


def dot(a, b, contract):
    return lax.dot_general(a, b, (contract, ((), ())), preferred_element_type=F32)


NN = ((1,), (0,))
NT = ((1,), (1,))


def iota(shape, dim):
    return lax.broadcasted_iota(jnp.int32, shape, dim)


class Sizes:
    def __init__(self, extent_first, extent_second, extent_depth, slots, owner_size, rows):
        self.ex = extent_first
        self.ey = extent_second
        self.nz = extent_depth
        self.zb = extent_depth // LANES
        self.slots = slots
        self.cells = extent_first * extent_second
        self.rows = rows
        self.xedge = 2 * extent_second
        self.yedge = extent_first * SUBLANES // 2
        self.edge_rows = self.zb * self.xedge
        self.yedge_rows = self.zb * self.yedge
        assert extent_second == 2 * SUBLANES and extent_first % 2 == 0
        assert self.cells == LANES and extent_first == SUBLANES


def rows_of_ids(sz, ids):
    copies = jnp.where(
        jnp.bitwise_and(iota((sz.ey, LANES), 1), sz.ey - 1) == iota((sz.ey, LANES), 0), 1.0, 0.0
    ).astype(BF16)
    shape = (sz.slots * sz.zb, sz.ex, LANES)
    own = iota(shape, 2) // sz.ey == iota(shape, 1)

    def flat(part):
        spread = dot(part.astype(F32).astype(BF16), copies, NN).reshape(shape)
        return jnp.sum(jnp.where(own, spread, 0.0), axis=1)

    return flat(lax.shift_right_logical(ids, 7)), flat(jnp.bitwise_and(ids, LANES - 1))


def chunk(sz, arr, zb, slot):
    at = slot * sz.zb + zb
    return arr[at : at + 1, :]


def chunks(sz):
    return [(zb, slot) for zb in range(sz.zb) for slot in range(sz.slots)]


def partial_table(sz, vals, pv_ref, row_of, hot_ref):
    eye = iota((sz.cells, LANES), 0) == iota((sz.cells, LANES), 1)
    eye_all = jnp.concatenate([eye] * sz.slots, axis=0)
    spread_first, spread_second = [], []
    table_iota = iota((sz.rows, LANES), 0).astype(F32)
    for zb in range(sz.zb):
        first, second = pieces(vals[:, zb * LANES : (zb + 1) * LANES])
        weights = pv_ref[:, zb * LANES : (zb + 1) * LANES]
        cross = dot(
            jnp.concatenate([weights, weights], axis=1),
            jnp.concatenate([first, second], axis=1),
            NT,
        )
        cross = jnp.where(eye_all, cross, 0.0)
        for slot in range(sz.slots):
            sums = jnp.sum(
                cross[slot * sz.cells : (slot + 1) * sz.cells], axis=0, keepdims=True
            )
            spread = jnp.where(chunk(sz, row_of, zb, slot) == table_iota, sums, 0.0)
            a, b = pieces(spread)
            spread_first.append(a)
            spread_second.append(b)
    lhs = jnp.concatenate(
        [jnp.concatenate(spread_first, axis=1), jnp.concatenate(spread_second, axis=1)], axis=0
    )
    both = dot(lhs, hot_ref[...], NT)
    return both[: sz.rows] + both[sz.rows :]


def projected(sz, tables, pv_ref, row_of, hot_ref):
    count = len(tables)
    split = [piece for table in tables for piece in pieces(table)]
    found = dot(jnp.concatenate(split, axis=0), hot_ref[...], NN)
    found = [
        found[2 * n * sz.rows : (2 * n + 1) * sz.rows]
        + found[(2 * n + 1) * sz.rows : (2 * n + 2) * sz.rows]
        for n in range(count)
    ]
    table_iota = iota((sz.rows, LANES), 0).astype(F32)
    eye = iota((sz.cells, LANES), 0) == iota((sz.cells, LANES), 1)
    result = [[] for _ in tables]
    for zb in range(sz.zb):
        diag = [[] for _ in range(2 * count)]
        for slot in range(sz.slots):
            at = (zb * sz.slots + slot) * LANES
            hit = chunk(sz, row_of, zb, slot) == table_iota
            for n in range(count):
                weight = jnp.sum(
                    jnp.where(hit, found[n][:, at : at + LANES], 0.0), axis=0, keepdims=True
                )
                a, b = pieces(jnp.where(eye, weight, 0.0))
                diag[2 * n].append(a)
                diag[2 * n + 1].append(b)
        lhs = jnp.concatenate([jnp.concatenate(parts, axis=1) for parts in diag], axis=0)
        both = dot(lhs, pv_ref[:, zb * LANES : (zb + 1) * LANES], NN)
        for n in range(count):
            at = 2 * n * sz.cells
            result[n].append(both[at : at + sz.cells] + both[at + sz.cells : at + 2 * sz.cells])
    return [jnp.concatenate(parts, axis=1) for parts in result]


def from_message(sz, msg_ref, rows):
    return jnp.concatenate(
        [msg_ref[zb * rows : (zb + 1) * rows, :] for zb in range(sz.zb)], axis=1
    )


def to_message(sz, msg_ref, vals):
    rows = vals.shape[0]
    for zb in range(sz.zb):
        msg_ref[zb * rows : (zb + 1) * rows, :] = vals[:, zb * LANES : (zb + 1) * LANES]


def second_edges(sz, vals):
    tiles = vals.reshape(sz.ex, 2, SUBLANES, sz.nz)
    sub = iota((sz.ex // 2, SUBLANES, sz.nz), 1)
    even = tiles.reshape(sz.ex // 2, 2, 2, SUBLANES, sz.nz)
    outer_even = jnp.where(sub < 4, even[:, 0, 0], even[:, 0, 1])
    outer_odd = jnp.where(sub < 4, even[:, 1, 0], even[:, 1, 1])
    odd = pltpu.roll(outer_odd, 4, axis=1)
    keep = jnp.logical_or(sub < 2, sub >= 6)
    return jnp.where(keep, outer_even, odd).reshape(sz.yedge, sz.nz)


def second_halo(sz, packed):
    pairs = packed.reshape(sz.ex // 2, SUBLANES, sz.nz)
    odd = pltpu.roll(pairs, 4, axis=1)
    return jnp.stack([pairs, odd], axis=1).reshape(sz.ex, SUBLANES, sz.nz)


def stencil(sz, vals, low, high, below, above):
    result = -90.0 * vals
    tall = jnp.concatenate([low, vals, high], axis=0)
    step = sz.ey
    cells = sz.cells
    near = tall[step : step + cells] + tall[3 * step : 3 * step + cells]
    far = tall[0:cells] + tall[4 * step : 4 * step + cells]

    near = near + pltpu.roll(vals, 1, axis=1) + pltpu.roll(vals, sz.nz - 1, axis=1)
    far = far + pltpu.roll(vals, 2, axis=1) + pltpu.roll(vals, sz.nz - 2, axis=1)

    tiles = vals.reshape(2 * sz.ex, SUBLANES, sz.nz)
    sub = iota((2 * sz.ex, SUBLANES, sz.nz), 1)

    def shifted(amount, outer, from_below):
        mine = pltpu.roll(tiles, amount, axis=1)
        theirs = pltpu.roll(outer, amount, axis=1)
        pairs = mine.reshape(sz.ex, 2, SUBLANES, sz.nz)
        if from_below:
            other = jnp.stack([theirs, pairs[:, 0]], axis=1)
            mask = sub < amount
        else:
            other = jnp.stack([pairs[:, 1], theirs], axis=1)
            mask = sub >= amount
        return jnp.where(mask, other.reshape(tiles.shape), mine).reshape(vals.shape)

    near = near + shifted(1, below, True) + shifted(SUBLANES - 1, above, False)
    far = far + shifted(2, below, True) + shifted(SUBLANES - 2, above, False)
    return result + 16.0 * near - far


def emit(sz, vals, flag_ref, pv_ref, row_of, hot_ref, ab_ref, bb_ref, yb_ref, table_ref):
    table = partial_table(sz, vals, pv_ref, row_of, hot_ref)
    table_ref[...] = table
    flag = flag_ref[0]
    top = vals[sz.cells - sz.xedge :]
    bottom = vals[: sz.xedge]
    is_high = flag == 0
    to_message(sz, ab_ref, jnp.where(is_high, top, bottom))
    to_message(sz, bb_ref, jnp.where(is_high, bottom, top))
    bb_ref[sz.edge_rows :, :] = table
    to_message(sz, yb_ref, second_edges(sz, vals))
    yb_ref[sz.yedge_rows :, :] = table


def first_kernel(
    sz,
    flag_ref,
    vals_hbm,
    pv_hbm,
    ids_hbm,
    cheb_hbm,
    ab_ref,
    bb_ref,
    yb_ref,
    table_ref,
    rows_ref,
    hot_ref,
    cheb_out,
    vals_ref,
    pv_ref,
    ids_ref,
    cheb_ref,
    sems,
):
    get_ids = pltpu.make_async_copy(ids_hbm, ids_ref, sems.at[0])
    get_pv = pltpu.make_async_copy(pv_hbm, pv_ref, sems.at[1])
    get_vals = pltpu.make_async_copy(vals_hbm, vals_ref, sems.at[2])
    get_cheb = pltpu.make_async_copy(cheb_hbm, cheb_ref, sems.at[3])
    get_ids.start()
    get_vals.start()
    get_pv.start()
    get_cheb.start()
    get_ids.wait()
    row_of, lane_of = rows_of_ids(sz, ids_ref[...])
    rows_ref[...] = row_of
    lane_iota = iota((LANES, LANES), 0).astype(F32)
    for at, (zb, slot) in enumerate(chunks(sz)):
        hot_ref[:, at * LANES : (at + 1) * LANES] = jnp.where(
            chunk(sz, lane_of, zb, slot) == lane_iota, 1.0, 0.0
        ).astype(BF16)
    get_vals.wait()
    get_pv.wait()
    emit(
        sz, vals_ref[...], flag_ref, pv_ref, row_of, hot_ref, ab_ref, bb_ref, yb_ref, table_ref
    )
    get_cheb.wait()
    for n in range(STEPS + 1):
        cheb_out[n : n + 1, :] = jnp.full((1, LANES), cheb_ref[n], F32)


def coefficient(sz, cheb_ref, n):
    row = cheb_ref[n : n + 1, :]
    return jnp.concatenate([row] * sz.zb, axis=1)


def local_kernel(sz, degree, n_y, flag_ref, *refs):
    refs = list(refs)
    cheb_ref = refs.pop(0) if degree == STEPS else None
    a_ref, b_ref = refs.pop(0), refs.pop(0)
    y_refs = [refs.pop(0) for _ in range(n_y)]
    pot_ref = refs.pop(0)
    *history, out_ref = refs
    vals = history[-1][...]

    from_a = from_message(sz, a_ref, sz.xedge)
    from_b = from_message(sz, b_ref, sz.xedge)
    is_high = flag_ref[0] == 0
    low = jnp.where(is_high, from_b, from_a)
    high = jnp.where(is_high, from_a, from_b)
    outer = [second_halo(sz, from_message(sz, ref, sz.yedge)) for ref in y_refs]
    laplace12 = stencil(sz, vals, low, high, outer[0], outer[-1])
    double = 1.0 if degree == 1 else 2.0
    result = laplace12 * (-0.5 / 12.0 / E_HALF * double) + vals * (
        (pot_ref[...] - E_MID) * (double / E_HALF)
    )
    if degree > 1:
        result = result - history[-2][...]
    if degree == STEPS:
        result = coefficient(sz, cheb_ref, STEPS) * result
        for n in range(STEPS):
            result = result + coefficient(sz, cheb_ref, n) * history[n][...]
    out_ref[...] = result


def added(table_refs):
    table = table_refs[0][...]
    for ref in table_refs[1:]:
        table = table + ref[...]
    return table


def nonlocal_kernel(sz, degree, n_tables, flag_ref, *refs):
    refs = list(refs)
    table_refs = [refs.pop(0) for _ in range(n_tables)]
    energy_ref, rest_ref, pv_ref, rows_ref, hot_ref = (refs.pop(0) for _ in range(5))
    row_of = rows_ref[...]
    double = 1.0 if degree == 1 else 2.0
    table = added(table_refs) * (energy_ref[...] * (double / E_HALF))
    result = rest_ref[...] + projected(sz, [table], pv_ref, row_of, hot_ref)[0]
    refs[0][...] = result
    emit(sz, result, flag_ref, pv_ref, row_of, hot_ref, *refs[1:])


def last_kernel(sz, n_orbitals, n_tables, cheb_ref, *refs):
    refs = list(refs)
    energy_ref, pv_ref, rows_ref, hot_ref = (refs.pop(0) for _ in range(4))
    scale = energy_ref[...] * (2.0 / E_HALF * cheb_ref[STEPS : STEPS + 1, :])
    rests, tables = [], []
    for _ in range(n_orbitals):
        rests.append(refs.pop(0))
        tables.append(added([refs.pop(0) for _ in range(n_tables)]) * scale)
    total = None
    for rest_ref, part in zip(rests, projected(sz, tables, pv_ref, rows_ref[...], hot_ref)):
        filtered = rest_ref[...] + part
        squared = filtered * filtered
        total = squared if total is None else total + squared
    refs[0][...] = total


def vmem(count):
    return [pl.BlockSpec(memory_space=pltpu.VMEM)] * count


def smem(count):
    return [pl.BlockSpec(memory_space=pltpu.SMEM)] * count


def in_place(arr):
    return pltpu.with_memory_space_constraint(arr, pltpu.HBM)


def shift_table(table, blocks_first, blocks_second, size_first, size_second, dim, delta):
    blocks = table.reshape(blocks_first, blocks_second, -1)
    count = blocks.shape[dim]
    size = (size_first, size_second)[dim]
    parts = []
    for at in range(count):
        source = [s for s in range(count) if (s + delta) % size == at]
        if source:
            parts.append(lax.slice_in_dim(blocks, source[0], source[0] + 1, axis=dim))
        else:
            parts.append(jnp.zeros_like(lax.slice_in_dim(blocks, 0, 1, axis=dim)))
    return jnp.concatenate(parts, axis=dim).reshape(table.shape)


def offsets(size):
    return sorted({d % size for d in (-2, -1, 1, 2)} - {0})


def shift(arr, axis, amount):
    size = lax.axis_size(axis)
    return lax.ppermute(arr, axis, [(i, (i + amount) % size) for i in range(size)])


def swap(arr, target):
    size_first = lax.axis_size("gx")
    size_second = lax.axis_size("gy")
    pairs = []
    for i in range(size_first):
        for j in range(size_second):
            ti, tj = target(i, j)
            pairs.append((i * size_second + j, ti * size_second + tj))
    return lax.ppermute(arr, ("gx", "gy"), pairs)


def orb_swap(vals, bit):
    size = lax.axis_size("orb")
    return lax.ppermute(vals, "orb", [(i, i ^ bit) for i in range(size)])


def local(orbitals, local_pot, proj_vals, proj_ids, proj_energy, cheb_coef):
    count_orb, ex, ey, nz = orbitals.shape
    slots = proj_vals.shape[0]
    size_first = lax.axis_size("gx")
    size_second = lax.axis_size("gy")
    size_orb = lax.axis_size("orb")
    paired = size_orb == 4 and count_orb == 1
    owner_size = proj_energy.shape[0] // (size_first * size_second)
    whole = size_first == 4 and size_second == 2
    if whole:
        windows = (size_first, size_second)
    else:
        windows = (min(3, size_first), min(3, size_second))
    rows = windows[0] * windows[1] * owner_size // LANES
    sz = Sizes(ex, ey, nz, slots, owner_size, rows)
    here_first = lax.axis_index("gx")
    here_second = lax.axis_index("gy")

    if whole:
        flag = jnp.bitwise_and(here_first, 1).astype(jnp.int32).reshape(1)
        energy = proj_energy.reshape(rows, LANES)
        ids = proj_ids
    else:
        flag = jnp.zeros((1,), jnp.int32)
        owner = proj_ids // owner_size
        rel_first = (owner // size_second - here_first + 1) % size_first
        rel_second = (owner % size_second - here_second + 1) % size_second
        ids = (rel_first * windows[1] + rel_second) * owner_size + proj_ids % owner_size
        grid = proj_energy.reshape(size_first, size_second, owner_size)
        grid = jnp.roll(grid, (1 - here_first, 1 - here_second), (0, 1))
        energy = grid[: windows[0], : windows[1]].reshape(rows, LANES)

    ids = jnp.transpose(ids, (0, 3, 1, 2)).reshape(slots * sz.zb * ex, ey)
    pv = proj_vals.reshape(slots * sz.cells, nz)
    pot = local_pot.reshape(sz.cells, nz)
    message_shapes = (
        jax.ShapeDtypeStruct((sz.edge_rows, LANES), F32),
        jax.ShapeDtypeStruct((sz.edge_rows + rows, LANES), F32),
        jax.ShapeDtypeStruct((sz.yedge_rows + rows, LANES), F32),
        jax.ShapeDtypeStruct((rows, LANES), F32),
    )
    field = jax.ShapeDtypeStruct((sz.cells, nz), F32)
    params = pltpu.CompilerParams(vmem_limit_bytes=48 << 20)

    def exchange(to_a, to_b, to_y, table):
        if whole:
            from_b = swap(to_b, lambda i, j: (size_first - 1 - i, j))
            from_y = swap(to_y, lambda i, j: (i, 1 - j))
            from_d = swap(table, lambda i, j: (size_first - 1 - i, 1 - j))
            from_a = swap(to_a, lambda i, j: (i ^ 1, j))
            table = table + from_d + from_b[sz.edge_rows :] + from_y[sz.yedge_rows :]
            other = swap(table, lambda i, j: (i ^ 1, j))
            return [table, other], from_a, from_b, [from_y]
        edges_b = to_b[: sz.edge_rows]
        edges_y = to_y[: sz.yedge_rows]
        below = shift(edges_y, "gy", 1)
        above = shift(edges_y, "gy", -1)
        from_a = shift(edges_b, "gx", -1)
        from_b = shift(to_a, "gx", 1)
        for dim, axis in ((1, "gy"), (0, "gx")):
            total = table
            for delta in offsets((size_first, size_second)[dim]):
                moved = shift(table, axis, -delta)
                total = total + shift_table(
                    moved, windows[0], windows[1], size_first, size_second, dim, delta
                )
            table = total
        return [table], from_a, from_b, [below, above]

    def one_orbital(start):
        *messages, row_of, hot, cheb = pl.pallas_call(
            functools.partial(first_kernel, sz),
            out_shape=message_shapes
            + (
                jax.ShapeDtypeStruct((slots * sz.zb, LANES), F32),
                jax.ShapeDtypeStruct((LANES, slots * sz.zb * sz.cells), BF16),
                jax.ShapeDtypeStruct((SUBLANES, LANES), F32),
            ),
            in_specs=smem(1) + [pl.BlockSpec(memory_space=pltpu.HBM)] * 4,
            out_specs=tuple(vmem(7)),
            scratch_shapes=[
                pltpu.VMEM(start.shape, start.dtype),
                pltpu.VMEM(pv.shape, pv.dtype),
                pltpu.VMEM(ids.shape, ids.dtype),
                pltpu.SMEM(cheb_coef.shape, cheb_coef.dtype),
                pltpu.SemaphoreType.DMA((4,)),
            ],
            compiler_params=params,
            name="project_first",
        )(flag, *(in_place(arr) for arr in (start, pv, ids, cheb_coef)))
        history = [start]
        for degree in range(1, STEPS + 1):
            tables, from_a, from_b, from_y = exchange(*messages)
            last = degree == STEPS
            args = (from_a, from_b, *from_y, pot, *history)
            if last:
                args = (cheb, *args)
            rest = pl.pallas_call(
                functools.partial(local_kernel, sz, degree, len(from_y)),
                out_shape=field,
                in_specs=smem(1) + vmem(len(args)),
                out_specs=vmem(1)[0],
                compiler_params=params,
                name=f"local_{degree}",
            )(flag, *args)
            if last:
                orbitals_here = [(rest, *tables)]
                if paired:
                    total = functools.reduce(jnp.add, tables)
                    orbitals_here = [(rest, total), (orb_swap(rest, 1), orb_swap(total, 1))]
                args = (cheb, energy, pv, row_of, hot, *sum(orbitals_here, ()))
                return pl.pallas_call(
                    functools.partial(
                        last_kernel, sz, len(orbitals_here), len(orbitals_here[0]) - 1
                    ),
                    out_shape=field,
                    in_specs=vmem(len(args)),
                    out_specs=vmem(1)[0],
                    compiler_params=params,
                    name="filtered",
                )(*args)
            args = (*tables, energy, rest, pv, row_of, hot)
            out = pl.pallas_call(
                functools.partial(nonlocal_kernel, sz, degree, len(tables)),
                out_shape=(field,) + message_shapes,
                in_specs=smem(1) + vmem(len(args)),
                out_specs=tuple(vmem(5)),
                compiler_params=params,
                name=f"nonlocal_{degree}",
            )(flag, *args)
            history.append(out[0])
            messages = out[1:]

    density = one_orbital(orbitals[0].reshape(sz.cells, nz))
    for at in range(1, count_orb):
        density = density + one_orbital(orbitals[at].reshape(sz.cells, nz))
    scale = 1.0 / (count_orb * size_orb)
    if paired:
        density = density + orb_swap(density, 3)
    else:
        density = lax.psum(density, "orb")
    return (density * scale).reshape(ex, ey, nz)


def solution(mesh):
    return jax.shard_map(
        local,
        mesh=mesh,
        in_specs=(
            P("orb", "gx", "gy", None),
            P("gx", "gy", None),
            P(None, "gx", "gy", None),
            P(None, "gx", "gy", None),
            P(),
            P(),
        ),
        out_specs=P("gx", "gy", None),
        check_vma=False,
    )
```

```python
import functools

import jax
import jax.numpy as jnp
from jax import lax
from jax.experimental import pallas as pl
from jax.experimental.pallas import tpu as pltpu
from jax.sharding import PartitionSpec as P

LANES = 128
SUBLANES = 8
STEPS = 3
E_MID = 4.0
E_HALF = 8.0
F32 = jnp.float32
BF16 = jnp.bfloat16


def pieces(vals):
    first = vals.astype(BF16)
    second = (vals - first.astype(F32)).astype(BF16)
    return first, second


def dot(a, b, contract):
    return lax.dot_general(a, b, (contract, ((), ())), preferred_element_type=F32)


NN = ((1,), (0,))
NT = ((1,), (1,))


def iota(shape, dim):
    return lax.broadcasted_iota(jnp.int32, shape, dim)


class Sizes:
    def __init__(self, extent_first, extent_second, extent_depth, slots, owner_size, rows):
        self.ex = extent_first
        self.ey = extent_second
        self.nz = extent_depth
        self.zb = extent_depth // LANES
        self.slots = slots
        self.cells = extent_first * extent_second
        self.rows = rows
        self.xedge = 2 * extent_second
        self.yedge = extent_first * SUBLANES // 2
        self.edge_rows = self.zb * self.xedge
        self.yedge_rows = self.zb * self.yedge
        assert extent_second == 2 * SUBLANES and extent_first % 2 == 0
        assert self.cells == LANES and extent_first == SUBLANES


def rows_of_ids(sz, ids):
    copies = jnp.where(
        jnp.bitwise_and(iota((sz.ey, LANES), 1), sz.ey - 1) == iota((sz.ey, LANES), 0), 1.0, 0.0
    ).astype(BF16)
    shape = (sz.slots * sz.zb, sz.ex, LANES)
    own = iota(shape, 2) // sz.ey == iota(shape, 1)

    def flat(part):
        spread = dot(part.astype(F32).astype(BF16), copies, NN).reshape(shape)
        return jnp.sum(jnp.where(own, spread, 0.0), axis=1)

    return flat(lax.shift_right_logical(ids, 7)), flat(jnp.bitwise_and(ids, LANES - 1))


def chunk(sz, arr, zb, slot):
    at = slot * sz.zb + zb
    return arr[at : at + 1, :]


def chunks(sz):
    return [(zb, slot) for zb in range(sz.zb) for slot in range(sz.slots)]


def slot_sums(sz, vals, pv_ref):
    eye = iota((sz.cells, LANES), 0) == iota((sz.cells, LANES), 1)
    eye_all = jnp.concatenate([eye] * sz.slots, axis=0)
    sums = {}
    for zb in range(sz.zb):
        first, second = pieces(vals[:, zb * LANES : (zb + 1) * LANES])
        weights = pv_ref[:, zb * LANES : (zb + 1) * LANES]
        cross = dot(
            jnp.concatenate([weights, weights], axis=1),
            jnp.concatenate([first, second], axis=1),
            NT,
        )
        cross = jnp.where(eye_all, cross, 0.0)
        for slot in range(sz.slots):
            part = cross[slot * sz.cells : (slot + 1) * sz.cells]
            sums[zb, slot] = jnp.sum(part, axis=0, keepdims=True)
    return sums


def partial_table(sz, sums, row_of, hot_ref):
    spread_first, spread_second = [], []
    table_iota = iota((sz.rows, LANES), 0).astype(F32)
    for zb, slot in chunks(sz):
        hit = chunk(sz, row_of, zb, slot) == table_iota
        a, b = pieces(sums[zb, slot])
        spread_first.append(jnp.where(hit, a.astype(F32), 0.0).astype(BF16))
        spread_second.append(jnp.where(hit, b.astype(F32), 0.0).astype(BF16))
    lhs = jnp.concatenate(
        [jnp.concatenate(spread_first, axis=1), jnp.concatenate(spread_second, axis=1)], axis=0
    )
    both = dot(lhs, hot_ref[...], NT)
    return both[: sz.rows] + both[sz.rows :]


def overlap_row(sz, slot, other, zb):
    return (slot * sz.slots + other) * sz.zb + zb


def overlap_kernel(sz, after_ref, pv_ref, overlap_ref):
    eye = iota((sz.cells, LANES), 0) == iota((sz.cells, LANES), 1)
    for zb in range(sz.zb):
        weights = pv_ref[:, zb * LANES : (zb + 1) * LANES]
        cross = dot(weights, weights, NT)
        for slot in range(sz.slots):
            rows = cross[slot * sz.cells : (slot + 1) * sz.cells]
            for other in range(slot, sz.slots):
                block = rows[:, other * sz.cells : (other + 1) * sz.cells]
                row = jnp.sum(jnp.where(eye, block, 0.0), axis=0, keepdims=True)
                for at in {(slot, other), (other, slot)}:
                    at = overlap_row(sz, *at, zb)
                    overlap_ref[at : at + 1, :] = row


def projected(sz, tables, pv_ref, row_of, hot_ref):
    count = len(tables)
    split = [piece for table in tables for piece in pieces(table)]
    found = dot(jnp.concatenate(split, axis=0), hot_ref[...], NN)
    found = [
        found[2 * n * sz.rows : (2 * n + 1) * sz.rows]
        + found[(2 * n + 1) * sz.rows : (2 * n + 2) * sz.rows]
        for n in range(count)
    ]
    table_iota = iota((sz.rows, LANES), 0).astype(F32)
    eye = iota((sz.cells, LANES), 0) == iota((sz.cells, LANES), 1)
    result = [[] for _ in tables]
    weights = [{} for _ in tables]
    for zb in range(sz.zb):
        diag = [[] for _ in range(2 * count)]
        for slot in range(sz.slots):
            at = (zb * sz.slots + slot) * LANES
            hit = chunk(sz, row_of, zb, slot) == table_iota
            for n in range(count):
                weight = jnp.sum(
                    jnp.where(hit, found[n][:, at : at + LANES], 0.0), axis=0, keepdims=True
                )
                weights[n][zb, slot] = weight
                a, b = pieces(jnp.where(eye, weight, 0.0))
                diag[2 * n].append(a)
                diag[2 * n + 1].append(b)
        lhs = jnp.concatenate([jnp.concatenate(parts, axis=1) for parts in diag], axis=0)
        both = dot(lhs, pv_ref[:, zb * LANES : (zb + 1) * LANES], NN)
        for n in range(count):
            at = 2 * n * sz.cells
            result[n].append(both[at : at + sz.cells] + both[at + sz.cells : at + 2 * sz.cells])
    return [jnp.concatenate(parts, axis=1) for parts in result], weights


def from_message(sz, msg_ref, rows):
    return jnp.concatenate(
        [msg_ref[zb * rows : (zb + 1) * rows, :] for zb in range(sz.zb)], axis=1
    )


def to_message(sz, msg_ref, vals):
    rows = vals.shape[0]
    for zb in range(sz.zb):
        msg_ref[zb * rows : (zb + 1) * rows, :] = vals[:, zb * LANES : (zb + 1) * LANES]


def second_edges(sz, vals):
    tiles = vals.reshape(sz.ex, 2, SUBLANES, sz.nz)
    sub = iota((sz.ex // 2, SUBLANES, sz.nz), 1)
    even = tiles.reshape(sz.ex // 2, 2, 2, SUBLANES, sz.nz)
    outer_even = jnp.where(sub < 4, even[:, 0, 0], even[:, 0, 1])
    outer_odd = jnp.where(sub < 4, even[:, 1, 0], even[:, 1, 1])
    odd = pltpu.roll(outer_odd, 4, axis=1)
    keep = jnp.logical_or(sub < 2, sub >= 6)
    return jnp.where(keep, outer_even, odd).reshape(sz.yedge, sz.nz)


def second_halo(sz, packed):
    pairs = packed.reshape(sz.ex // 2, SUBLANES, sz.nz)
    odd = pltpu.roll(pairs, 4, axis=1)
    return jnp.stack([pairs, odd], axis=1).reshape(sz.ex, SUBLANES, sz.nz)


def stencil(sz, vals, low, high, below, above):
    result = -90.0 * vals
    tall = jnp.concatenate([low, vals, high], axis=0)
    step = sz.ey
    cells = sz.cells
    near = tall[step : step + cells] + tall[3 * step : 3 * step + cells]
    far = tall[0:cells] + tall[4 * step : 4 * step + cells]

    near = near + pltpu.roll(vals, 1, axis=1) + pltpu.roll(vals, sz.nz - 1, axis=1)
    far = far + pltpu.roll(vals, 2, axis=1) + pltpu.roll(vals, sz.nz - 2, axis=1)

    tiles = vals.reshape(2 * sz.ex, SUBLANES, sz.nz)
    sub = iota((2 * sz.ex, SUBLANES, sz.nz), 1)

    def shifted(amount, outer, from_below):
        mine = pltpu.roll(tiles, amount, axis=1)
        theirs = pltpu.roll(outer, amount, axis=1)
        pairs = mine.reshape(sz.ex, 2, SUBLANES, sz.nz)
        if from_below:
            other = jnp.stack([theirs, pairs[:, 0]], axis=1)
            mask = sub < amount
        else:
            other = jnp.stack([pairs[:, 1], theirs], axis=1)
            mask = sub >= amount
        return jnp.where(mask, other.reshape(tiles.shape), mine).reshape(vals.shape)

    near = near + shifted(1, below, True) + shifted(SUBLANES - 1, above, False)
    far = far + shifted(2, below, True) + shifted(SUBLANES - 2, above, False)
    return result + 16.0 * near - far


def emit(sz, vals, table, flag_ref, ab_ref, bb_ref, yb_ref, table_ref):
    table_ref[...] = table
    flag = flag_ref[0]
    top = vals[sz.cells - sz.xedge :]
    bottom = vals[: sz.xedge]
    is_high = flag == 0
    to_message(sz, ab_ref, jnp.where(is_high, top, bottom))
    to_message(sz, bb_ref, jnp.where(is_high, bottom, top))
    bb_ref[sz.edge_rows :, :] = table
    to_message(sz, yb_ref, second_edges(sz, vals))
    yb_ref[sz.yedge_rows :, :] = table


def first_kernel(
    sz,
    flag_ref,
    vals_hbm,
    pv_hbm,
    ids_hbm,
    cheb_hbm,
    ab_ref,
    bb_ref,
    yb_ref,
    table_ref,
    rows_ref,
    hot_ref,
    cheb_out,
    vals_ref,
    pv_ref,
    ids_ref,
    cheb_ref,
    sems,
):
    get_ids = pltpu.make_async_copy(ids_hbm, ids_ref, sems.at[0])
    get_pv = pltpu.make_async_copy(pv_hbm, pv_ref, sems.at[1])
    get_vals = pltpu.make_async_copy(vals_hbm, vals_ref, sems.at[2])
    get_cheb = pltpu.make_async_copy(cheb_hbm, cheb_ref, sems.at[3])
    get_ids.start()
    get_vals.start()
    get_pv.start()
    get_cheb.start()
    get_ids.wait()
    row_of, lane_of = rows_of_ids(sz, ids_ref[...])
    rows_ref[...] = row_of
    lane_iota = iota((LANES, LANES), 0).astype(F32)
    for at, (zb, slot) in enumerate(chunks(sz)):
        hot_ref[:, at * LANES : (at + 1) * LANES] = jnp.where(
            chunk(sz, lane_of, zb, slot) == lane_iota, 1.0, 0.0
        ).astype(BF16)
    get_vals.wait()
    get_pv.wait()
    vals = vals_ref[...]
    table = partial_table(sz, slot_sums(sz, vals, pv_ref), row_of, hot_ref)
    emit(sz, vals, table, flag_ref, ab_ref, bb_ref, yb_ref, table_ref)
    get_cheb.wait()
    for n in range(STEPS + 1):
        cheb_out[n : n + 1, :] = jnp.full((1, LANES), cheb_ref[n], F32)


def coefficient(sz, cheb_ref, n):
    row = cheb_ref[n : n + 1, :]
    return jnp.concatenate([row] * sz.zb, axis=1)


def local_kernel(sz, degree, n_y, flag_ref, *refs):
    refs = list(refs)
    cheb_ref = refs.pop(0) if degree == STEPS else None
    a_ref, b_ref = refs.pop(0), refs.pop(0)
    y_refs = [refs.pop(0) for _ in range(n_y)]
    pot_ref = refs.pop(0)
    if degree < STEPS:
        pv_ref, sums_ref = refs.pop(0), refs.pop()
    *history, out_ref = refs
    vals = history[-1][...]

    from_a = from_message(sz, a_ref, sz.xedge)
    from_b = from_message(sz, b_ref, sz.xedge)
    is_high = flag_ref[0] == 0
    low = jnp.where(is_high, from_b, from_a)
    high = jnp.where(is_high, from_a, from_b)
    outer = [second_halo(sz, from_message(sz, ref, sz.yedge)) for ref in y_refs]
    laplace12 = stencil(sz, vals, low, high, outer[0], outer[-1])
    double = 1.0 if degree == 1 else 2.0
    result = laplace12 * (-0.5 / 12.0 / E_HALF * double) + vals * (
        (pot_ref[...] - E_MID) * (double / E_HALF)
    )
    if degree > 1:
        result = result - history[-2][...]
    if degree == STEPS:
        result = coefficient(sz, cheb_ref, STEPS) * result
        for n in range(STEPS):
            result = result + coefficient(sz, cheb_ref, n) * history[n][...]
    out_ref[...] = result
    if degree < STEPS:
        for (zb, slot), row in slot_sums(sz, result, pv_ref).items():
            at = slot * sz.zb + zb
            sums_ref[at : at + 1, :] = row


def added(table_refs):
    table = table_refs[0][...]
    for ref in table_refs[1:]:
        table = table + ref[...]
    return table


def nonlocal_kernel(sz, degree, n_tables, flag_ref, *refs):
    refs = list(refs)
    table_refs = [refs.pop(0) for _ in range(n_tables)]
    energy_ref, rest_ref, pv_ref, rows_ref, hot_ref = (refs.pop(0) for _ in range(5))
    sums_ref, overlap_ref = refs.pop(0), refs.pop(0)
    row_of = rows_ref[...]
    double = 1.0 if degree == 1 else 2.0
    table = added(table_refs) * (energy_ref[...] * (double / E_HALF))
    (part,), (weights,) = projected(sz, [table], pv_ref, row_of, hot_ref)
    sums = {}
    for zb, slot in chunks(sz):
        total = chunk(sz, sums_ref, zb, slot)
        for other in range(sz.slots):
            at = overlap_row(sz, slot, other, zb)
            total = total + overlap_ref[at : at + 1, :] * weights[zb, other]
        sums[zb, slot] = total
    table = partial_table(sz, sums, row_of, hot_ref)
    result = rest_ref[...] + part
    refs[0][...] = result
    emit(sz, result, table, flag_ref, *refs[1:])


def last_kernel(sz, n_orbitals, n_tables, cheb_ref, *refs):
    refs = list(refs)
    energy_ref, pv_ref, rows_ref, hot_ref = (refs.pop(0) for _ in range(4))
    scale = energy_ref[...] * (2.0 / E_HALF * cheb_ref[STEPS : STEPS + 1, :])
    rests, tables = [], []
    for _ in range(n_orbitals):
        rests.append(refs.pop(0))
        tables.append(added([refs.pop(0) for _ in range(n_tables)]) * scale)
    total = None
    parts, _ = projected(sz, tables, pv_ref, rows_ref[...], hot_ref)
    for rest_ref, part in zip(rests, parts):
        filtered = rest_ref[...] + part
        squared = filtered * filtered
        total = squared if total is None else total + squared
    refs[0][...] = total


def vmem(count):
    return [pl.BlockSpec(memory_space=pltpu.VMEM)] * count


def smem(count):
    return [pl.BlockSpec(memory_space=pltpu.SMEM)] * count


def in_place(arr):
    return pltpu.with_memory_space_constraint(arr, pltpu.HBM)


def shift_table(table, blocks_first, blocks_second, size_first, size_second, dim, delta):
    blocks = table.reshape(blocks_first, blocks_second, -1)
    count = blocks.shape[dim]
    size = (size_first, size_second)[dim]
    parts = []
    for at in range(count):
        source = [s for s in range(count) if (s + delta) % size == at]
        if source:
            parts.append(lax.slice_in_dim(blocks, source[0], source[0] + 1, axis=dim))
        else:
            parts.append(jnp.zeros_like(lax.slice_in_dim(blocks, 0, 1, axis=dim)))
    return jnp.concatenate(parts, axis=dim).reshape(table.shape)


def offsets(size):
    return sorted({d % size for d in (-2, -1, 1, 2)} - {0})


def shift(arr, axis, amount):
    size = lax.axis_size(axis)
    return lax.ppermute(arr, axis, [(i, (i + amount) % size) for i in range(size)])


def swap(arr, target):
    size_first = lax.axis_size("gx")
    size_second = lax.axis_size("gy")
    pairs = []
    for i in range(size_first):
        for j in range(size_second):
            ti, tj = target(i, j)
            pairs.append((i * size_second + j, ti * size_second + tj))
    return lax.ppermute(arr, ("gx", "gy"), pairs)


def orb_swap(vals, bit):
    size = lax.axis_size("orb")
    return lax.ppermute(vals, "orb", [(i, i ^ bit) for i in range(size)])


def local(orbitals, local_pot, proj_vals, proj_ids, proj_energy, cheb_coef):
    count_orb, ex, ey, nz = orbitals.shape
    slots = proj_vals.shape[0]
    size_first = lax.axis_size("gx")
    size_second = lax.axis_size("gy")
    size_orb = lax.axis_size("orb")
    paired = size_orb == 4 and count_orb == 1
    owner_size = proj_energy.shape[0] // (size_first * size_second)
    whole = size_first == 4 and size_second == 2
    if whole:
        windows = (size_first, size_second)
    else:
        windows = (min(3, size_first), min(3, size_second))
    rows = windows[0] * windows[1] * owner_size // LANES
    sz = Sizes(ex, ey, nz, slots, owner_size, rows)
    here_first = lax.axis_index("gx")
    here_second = lax.axis_index("gy")

    if whole:
        flag = jnp.bitwise_and(here_first, 1).astype(jnp.int32).reshape(1)
        energy = proj_energy.reshape(rows, LANES)
        ids = proj_ids
    else:
        flag = jnp.zeros((1,), jnp.int32)
        owner = proj_ids // owner_size
        rel_first = (owner // size_second - here_first + 1) % size_first
        rel_second = (owner % size_second - here_second + 1) % size_second
        ids = (rel_first * windows[1] + rel_second) * owner_size + proj_ids % owner_size
        grid = proj_energy.reshape(size_first, size_second, owner_size)
        grid = jnp.roll(grid, (1 - here_first, 1 - here_second), (0, 1))
        energy = grid[: windows[0], : windows[1]].reshape(rows, LANES)

    ids = jnp.transpose(ids, (0, 3, 1, 2)).reshape(slots * sz.zb * ex, ey)
    pv = proj_vals.reshape(slots * sz.cells, nz)
    pot = local_pot.reshape(sz.cells, nz)
    message_shapes = (
        jax.ShapeDtypeStruct((sz.edge_rows, LANES), F32),
        jax.ShapeDtypeStruct((sz.edge_rows + rows, LANES), F32),
        jax.ShapeDtypeStruct((sz.yedge_rows + rows, LANES), F32),
        jax.ShapeDtypeStruct((rows, LANES), F32),
    )
    field = jax.ShapeDtypeStruct((sz.cells, nz), F32)
    params = pltpu.CompilerParams(vmem_limit_bytes=48 << 20)

    def exchange(to_a, to_b, to_y, table, aside):
        if whole:
            from_b = swap(to_b, lambda i, j: (size_first - 1 - i, j))
            from_y = swap(to_y, lambda i, j: (i, 1 - j))
            from_d = swap(table, lambda i, j: (size_first - 1 - i, 1 - j))
            from_a = swap(to_a, lambda i, j: (i ^ 1, j))
            if aside is not None:
                from_d, aside = lax.optimization_barrier((from_d, aside))
            table = table + from_d + from_b[sz.edge_rows :] + from_y[sz.yedge_rows :]
            other = swap(table, lambda i, j: (i ^ 1, j))
            return [table, other], from_a, from_b, [from_y], aside
        edges_b = to_b[: sz.edge_rows]
        edges_y = to_y[: sz.yedge_rows]
        below = shift(edges_y, "gy", 1)
        above = shift(edges_y, "gy", -1)
        from_a = shift(edges_b, "gx", -1)
        from_b = shift(to_a, "gx", 1)
        for dim, axis in ((1, "gy"), (0, "gx")):
            total = table
            for delta in offsets((size_first, size_second)[dim]):
                moved = shift(table, axis, -delta)
                total = total + shift_table(
                    moved, windows[0], windows[1], size_first, size_second, dim, delta
                )
            table = total
        return [table], from_a, from_b, [below, above], aside

    def one_orbital(start):
        *messages, row_of, hot, cheb = pl.pallas_call(
            functools.partial(first_kernel, sz),
            out_shape=message_shapes
            + (
                jax.ShapeDtypeStruct((slots * sz.zb, LANES), F32),
                jax.ShapeDtypeStruct((LANES, slots * sz.zb * sz.cells), BF16),
                jax.ShapeDtypeStruct((SUBLANES, LANES), F32),
            ),
            in_specs=smem(1) + [pl.BlockSpec(memory_space=pltpu.HBM)] * 4,
            out_specs=tuple(vmem(7)),
            scratch_shapes=[
                pltpu.VMEM(start.shape, start.dtype),
                pltpu.VMEM(pv.shape, pv.dtype),
                pltpu.VMEM(ids.shape, ids.dtype),
                pltpu.SMEM(cheb_coef.shape, cheb_coef.dtype),
                pltpu.SemaphoreType.DMA((4,)),
            ],
            compiler_params=params,
            name="project_first",
        )(flag, *(in_place(arr) for arr in (start, pv, ids, cheb_coef)))
        overlap = pl.pallas_call(
            functools.partial(overlap_kernel, sz),
            out_shape=jax.ShapeDtypeStruct((slots * slots * sz.zb, LANES), F32),
            in_specs=vmem(2),
            out_specs=vmem(1)[0],
            compiler_params=params,
            name="overlap",
        )(row_of, pv)
        history = [start]
        for degree in range(1, STEPS + 1):
            tables, from_a, from_b, from_y, aside = exchange(
                *messages, overlap if degree == 1 else None
            )
            overlap = overlap if aside is None else aside
            last = degree == STEPS
            sums_shape = jax.ShapeDtypeStruct((slots * sz.zb, LANES), F32)
            if last:
                args = (cheb, from_a, from_b, *from_y, pot, *history)
            else:
                args = (from_a, from_b, *from_y, pot, pv, *history)
            rest, *sums = pl.pallas_call(
                functools.partial(local_kernel, sz, degree, len(from_y)),
                out_shape=(field,) if last else (field, sums_shape),
                in_specs=smem(1) + vmem(len(args)),
                out_specs=tuple(vmem(1 if last else 2)),
                compiler_params=params,
                name=f"local_{degree}",
            )(flag, *args)
            if last:
                orbitals_here = [(rest, *tables)]
                if paired:
                    total = functools.reduce(jnp.add, tables)
                    orbitals_here = [(rest, total), (orb_swap(rest, 1), orb_swap(total, 1))]
                args = (cheb, energy, pv, row_of, hot, *sum(orbitals_here, ()))
                return pl.pallas_call(
                    functools.partial(
                        last_kernel, sz, len(orbitals_here), len(orbitals_here[0]) - 1
                    ),
                    out_shape=field,
                    in_specs=vmem(len(args)),
                    out_specs=vmem(1)[0],
                    compiler_params=params,
                    name="filtered",
                )(*args)
            args = (*tables, energy, rest, pv, row_of, hot, *sums, overlap)
            out = pl.pallas_call(
                functools.partial(nonlocal_kernel, sz, degree, len(tables)),
                out_shape=(field,) + message_shapes,
                in_specs=smem(1) + vmem(len(args)),
                out_specs=tuple(vmem(5)),
                compiler_params=params,
                name=f"nonlocal_{degree}",
            )(flag, *args)
            history.append(out[0])
            messages = out[1:]

    density = one_orbital(orbitals[0].reshape(sz.cells, nz))
    for at in range(1, count_orb):
        density = density + one_orbital(orbitals[at].reshape(sz.cells, nz))
    scale = 1.0 / (count_orb * size_orb)
    if paired:
        density = density + orb_swap(density, 3)
    else:
        density = lax.psum(density, "orb")
    return (density * scale).reshape(ex, ey, nz)


def solution(mesh):
    return jax.shard_map(
        local,
        mesh=mesh,
        in_specs=(
            P("orb", "gx", "gy", None),
            P("gx", "gy", None),
            P(None, "gx", "gy", None),
            P(None, "gx", "gy", None),
            P(),
            P(),
        ),
        out_specs=P("gx", "gy", None),
        check_vma=False,
    )
```

```python
import functools

import jax
import jax.numpy as jnp
from jax import lax
from jax.experimental import pallas as pl
from jax.experimental.pallas import tpu as pltpu
from jax.sharding import PartitionSpec as P

LANES = 128
SUBLANES = 8
STEPS = 3
E_MID = 4.0
E_HALF = 8.0
F32 = jnp.float32
BF16 = jnp.bfloat16


def pieces(vals):
    first = vals.astype(BF16)
    second = (vals - first.astype(F32)).astype(BF16)
    return first, second


def dot(a, b, contract):
    return lax.dot_general(a, b, (contract, ((), ())), preferred_element_type=F32)


NN = ((1,), (0,))
NT = ((1,), (1,))


def iota(shape, dim):
    return lax.broadcasted_iota(jnp.int32, shape, dim)


class Sizes:
    def __init__(self, extent_first, extent_second, extent_depth, slots, owner_size, rows):
        self.ex = extent_first
        self.ey = extent_second
        self.nz = extent_depth
        self.zb = extent_depth // LANES
        self.slots = slots
        self.cells = extent_first * extent_second
        self.rows = rows
        self.xedge = 2 * extent_second
        self.yedge = extent_first * SUBLANES // 2
        self.edge_rows = self.zb * self.xedge
        self.yedge_rows = self.zb * self.yedge
        assert extent_second == 2 * SUBLANES and extent_first % 2 == 0
        assert self.cells == LANES and extent_first == SUBLANES


def rows_of_ids(sz, ids):
    copies = jnp.where(
        jnp.bitwise_and(iota((sz.ey, LANES), 1), sz.ey - 1) == iota((sz.ey, LANES), 0), 1.0, 0.0
    ).astype(BF16)
    shape = (sz.slots * sz.zb, sz.ex, LANES)
    own = iota(shape, 2) // sz.ey == iota(shape, 1)

    def flat(part):
        spread = dot(part.astype(F32).astype(BF16), copies, NN).reshape(shape)
        return jnp.sum(jnp.where(own, spread, 0.0), axis=1)

    return flat(lax.shift_right_logical(ids, 7)), flat(jnp.bitwise_and(ids, LANES - 1))


def chunk(sz, arr, zb, slot):
    at = slot * sz.zb + zb
    return arr[at : at + 1, :]


def chunks(sz):
    return [(zb, slot) for zb in range(sz.zb) for slot in range(sz.slots)]


def slot_sums(sz, vals, pv_ref):
    eye = iota((sz.cells, LANES), 0) == iota((sz.cells, LANES), 1)
    eye_all = jnp.concatenate([eye] * sz.slots, axis=0)
    sums = {}
    for zb in range(sz.zb):
        first, second = pieces(vals[:, zb * LANES : (zb + 1) * LANES])
        weights = pv_ref[:, zb * LANES : (zb + 1) * LANES]
        cross = dot(
            jnp.concatenate([weights, weights], axis=1),
            jnp.concatenate([first, second], axis=1),
            NT,
        )
        cross = jnp.where(eye_all, cross, 0.0)
        for slot in range(sz.slots):
            part = cross[slot * sz.cells : (slot + 1) * sz.cells]
            sums[zb, slot] = jnp.sum(part, axis=0, keepdims=True)
    return sums


def partial_table(sz, sums, row_of, hot_ref):
    spread_first, spread_second = [], []
    table_iota = iota((sz.rows, LANES), 0).astype(F32)
    for zb, slot in chunks(sz):
        hit = chunk(sz, row_of, zb, slot) == table_iota
        a, b = pieces(sums[zb, slot])
        spread_first.append(jnp.where(hit, a.astype(F32), 0.0).astype(BF16))
        spread_second.append(jnp.where(hit, b.astype(F32), 0.0).astype(BF16))
    lhs = jnp.concatenate(
        [jnp.concatenate(spread_first, axis=1), jnp.concatenate(spread_second, axis=1)], axis=0
    )
    both = dot(lhs, hot_ref[...], NT)
    return both[: sz.rows] + both[sz.rows :]


def overlap_row(sz, slot, other, zb):
    return (slot * sz.slots + other) * sz.zb + zb


def overlap_kernel(sz, after_ref, pv_ref, overlap_ref):
    eye = iota((sz.cells, LANES), 0) == iota((sz.cells, LANES), 1)
    for zb in range(sz.zb):
        weights = pv_ref[:, zb * LANES : (zb + 1) * LANES]
        cross = dot(weights, weights, NT)
        for slot in range(sz.slots):
            rows = cross[slot * sz.cells : (slot + 1) * sz.cells]
            for other in range(slot, sz.slots):
                block = rows[:, other * sz.cells : (other + 1) * sz.cells]
                row = jnp.sum(jnp.where(eye, block, 0.0), axis=0, keepdims=True)
                for at in {(slot, other), (other, slot)}:
                    at = overlap_row(sz, *at, zb)
                    overlap_ref[at : at + 1, :] = row


def projected(sz, tables, pv_ref, row_of, hot_ref):
    count = len(tables)
    split = [piece for table in tables for piece in pieces(table)]
    found = dot(jnp.concatenate(split, axis=0), hot_ref[...], NN)
    found = [
        found[2 * n * sz.rows : (2 * n + 1) * sz.rows]
        + found[(2 * n + 1) * sz.rows : (2 * n + 2) * sz.rows]
        for n in range(count)
    ]
    table_iota = iota((sz.rows, LANES), 0).astype(F32)
    eye = iota((sz.cells, LANES), 0) == iota((sz.cells, LANES), 1)
    result = [[] for _ in tables]
    weights = [{} for _ in tables]
    for zb in range(sz.zb):
        diag = [[] for _ in range(2 * count)]
        for slot in range(sz.slots):
            at = (zb * sz.slots + slot) * LANES
            hit = chunk(sz, row_of, zb, slot) == table_iota
            for n in range(count):
                weight = jnp.sum(
                    jnp.where(hit, found[n][:, at : at + LANES], 0.0), axis=0, keepdims=True
                )
                weights[n][zb, slot] = weight
                a, b = pieces(jnp.where(eye, weight, 0.0))
                diag[2 * n].append(a)
                diag[2 * n + 1].append(b)
        lhs = jnp.concatenate([jnp.concatenate(parts, axis=1) for parts in diag], axis=0)
        both = dot(lhs, pv_ref[:, zb * LANES : (zb + 1) * LANES], NN)
        for n in range(count):
            at = 2 * n * sz.cells
            result[n].append(both[at : at + sz.cells] + both[at + sz.cells : at + 2 * sz.cells])
    return [jnp.concatenate(parts, axis=1) for parts in result], weights


def from_message(sz, msg_ref, rows):
    return jnp.concatenate(
        [msg_ref[zb * rows : (zb + 1) * rows, :] for zb in range(sz.zb)], axis=1
    )


def to_message(sz, msg_ref, vals):
    rows = vals.shape[0]
    for zb in range(sz.zb):
        msg_ref[zb * rows : (zb + 1) * rows, :] = vals[:, zb * LANES : (zb + 1) * LANES]


def second_edges(sz, vals):
    tiles = vals.reshape(sz.ex, 2, SUBLANES, sz.nz)
    sub = iota((sz.ex // 2, SUBLANES, sz.nz), 1)
    even = tiles.reshape(sz.ex // 2, 2, 2, SUBLANES, sz.nz)
    outer_even = jnp.where(sub < 4, even[:, 0, 0], even[:, 0, 1])
    outer_odd = jnp.where(sub < 4, even[:, 1, 0], even[:, 1, 1])
    odd = pltpu.roll(outer_odd, 4, axis=1)
    keep = jnp.logical_or(sub < 2, sub >= 6)
    return jnp.where(keep, outer_even, odd).reshape(sz.yedge, sz.nz)


def second_halo(sz, packed):
    pairs = packed.reshape(sz.ex // 2, SUBLANES, sz.nz)
    odd = pltpu.roll(pairs, 4, axis=1)
    return jnp.stack([pairs, odd], axis=1).reshape(sz.ex, SUBLANES, sz.nz)


def stencil(sz, vals, low, high, below, above):
    result = -90.0 * vals
    tall = jnp.concatenate([low, vals, high], axis=0)
    step = sz.ey
    cells = sz.cells
    near = tall[step : step + cells] + tall[3 * step : 3 * step + cells]
    far = tall[0:cells] + tall[4 * step : 4 * step + cells]

    near = near + pltpu.roll(vals, 1, axis=1) + pltpu.roll(vals, sz.nz - 1, axis=1)
    far = far + pltpu.roll(vals, 2, axis=1) + pltpu.roll(vals, sz.nz - 2, axis=1)

    tiles = vals.reshape(2 * sz.ex, SUBLANES, sz.nz)
    sub = iota((2 * sz.ex, SUBLANES, sz.nz), 1)

    def shifted(amount, outer, from_below):
        mine = pltpu.roll(tiles, amount, axis=1)
        theirs = pltpu.roll(outer, amount, axis=1)
        pairs = mine.reshape(sz.ex, 2, SUBLANES, sz.nz)
        if from_below:
            other = jnp.stack([theirs, pairs[:, 0]], axis=1)
            mask = sub < amount
        else:
            other = jnp.stack([pairs[:, 1], theirs], axis=1)
            mask = sub >= amount
        return jnp.where(mask, other.reshape(tiles.shape), mine).reshape(vals.shape)

    near = near + shifted(1, below, True) + shifted(SUBLANES - 1, above, False)
    far = far + shifted(2, below, True) + shifted(SUBLANES - 2, above, False)
    return result + 16.0 * near - far


def emit(sz, vals, table, flag_ref, ab_ref, bb_ref, yb_ref, table_ref):
    table_ref[...] = table
    flag = flag_ref[0]
    top = vals[sz.cells - sz.xedge :]
    bottom = vals[: sz.xedge]
    is_high = flag == 0
    to_message(sz, ab_ref, jnp.where(is_high, top, bottom))
    to_message(sz, bb_ref, jnp.where(is_high, bottom, top))
    bb_ref[sz.edge_rows :, :] = table
    to_message(sz, yb_ref, second_edges(sz, vals))
    yb_ref[sz.yedge_rows :, :] = table


def first_kernel(
    sz,
    flag_ref,
    vals_hbm,
    pv_hbm,
    ids_hbm,
    cheb_hbm,
    ab_ref,
    bb_ref,
    yb_ref,
    table_ref,
    rows_ref,
    hot_ref,
    cheb_out,
    vals_ref,
    pv_ref,
    ids_ref,
    cheb_ref,
    sems,
):
    get_ids = pltpu.make_async_copy(ids_hbm, ids_ref, sems.at[0])
    get_pv = pltpu.make_async_copy(pv_hbm, pv_ref, sems.at[1])
    get_vals = pltpu.make_async_copy(vals_hbm, vals_ref, sems.at[2])
    get_cheb = pltpu.make_async_copy(cheb_hbm, cheb_ref, sems.at[3])
    get_ids.start()
    get_vals.start()
    get_pv.start()
    get_cheb.start()
    get_ids.wait()
    row_of, lane_of = rows_of_ids(sz, ids_ref[...])
    rows_ref[...] = row_of
    lane_iota = iota((LANES, LANES), 0).astype(F32)
    for at, (zb, slot) in enumerate(chunks(sz)):
        hot_ref[:, at * LANES : (at + 1) * LANES] = jnp.where(
            chunk(sz, lane_of, zb, slot) == lane_iota, 1.0, 0.0
        ).astype(BF16)
    get_vals.wait()
    get_pv.wait()
    vals = vals_ref[...]
    table = partial_table(sz, slot_sums(sz, vals, pv_ref), row_of, hot_ref)
    emit(sz, vals, table, flag_ref, ab_ref, bb_ref, yb_ref, table_ref)
    get_cheb.wait()
    for n in range(STEPS + 1):
        cheb_out[n : n + 1, :] = jnp.full((1, LANES), cheb_ref[n], F32)


def coefficient(sz, cheb_ref, n):
    row = cheb_ref[n : n + 1, :]
    return jnp.concatenate([row] * sz.zb, axis=1)


def local_kernel(sz, degree, n_y, flag_ref, *refs):
    refs = list(refs)
    cheb_ref = refs.pop(0) if degree == STEPS else None
    a_ref, b_ref = refs.pop(0), refs.pop(0)
    y_refs = [refs.pop(0) for _ in range(n_y)]
    pot_ref = refs.pop(0)
    if degree < STEPS:
        pv_ref, sums_ref = refs.pop(0), refs.pop()
    *history, out_ref = refs
    vals = history[-1][...]

    from_a = from_message(sz, a_ref, sz.xedge)
    from_b = from_message(sz, b_ref, sz.xedge)
    is_high = flag_ref[0] == 0
    low = jnp.where(is_high, from_b, from_a)
    high = jnp.where(is_high, from_a, from_b)
    outer = [second_halo(sz, from_message(sz, ref, sz.yedge)) for ref in y_refs]
    laplace12 = stencil(sz, vals, low, high, outer[0], outer[-1])
    double = 1.0 if degree == 1 else 2.0
    result = laplace12 * (-0.5 / 12.0 / E_HALF * double) + vals * (
        (pot_ref[...] - E_MID) * (double / E_HALF)
    )
    if degree > 1:
        result = result - history[-2][...]
    if degree == STEPS:
        result = coefficient(sz, cheb_ref, STEPS) * result
        for n in range(STEPS):
            result = result + coefficient(sz, cheb_ref, n) * history[n][...]
    out_ref[...] = result
    if degree < STEPS:
        for (zb, slot), row in slot_sums(sz, result, pv_ref).items():
            at = slot * sz.zb + zb
            sums_ref[at : at + 1, :] = row


def added(table_refs):
    table = table_refs[0][...]
    for ref in table_refs[1:]:
        table = table + ref[...]
    return table


def nonlocal_kernel(sz, degree, n_tables, flag_ref, *refs):
    refs = list(refs)
    table_refs = [refs.pop(0) for _ in range(n_tables)]
    energy_ref, rest_ref, pv_ref, rows_ref, hot_ref = (refs.pop(0) for _ in range(5))
    sums_ref, overlap_ref = refs.pop(0), refs.pop(0)
    row_of = rows_ref[...]
    double = 1.0 if degree == 1 else 2.0
    table = added(table_refs) * (energy_ref[...] * (double / E_HALF))
    (part,), (weights,) = projected(sz, [table], pv_ref, row_of, hot_ref)
    sums = {}
    for zb, slot in chunks(sz):
        total = chunk(sz, sums_ref, zb, slot)
        for other in range(sz.slots):
            at = overlap_row(sz, slot, other, zb)
            total = total + overlap_ref[at : at + 1, :] * weights[zb, other]
        sums[zb, slot] = total
    table = partial_table(sz, sums, row_of, hot_ref)
    result = rest_ref[...] + part
    refs[0][...] = result
    emit(sz, result, table, flag_ref, *refs[1:])


def last_kernel(sz, n_tables, n_before, cheb_ref, *refs):
    refs = list(refs)
    energy_ref, pv_ref, rows_ref, hot_ref, rest_ref = (refs.pop(0) for _ in range(5))
    table = added([refs.pop(0) for _ in range(n_tables)])
    table = table * (energy_ref[...] * (2.0 / E_HALF * cheb_ref[STEPS : STEPS + 1, :]))
    (part,), _ = projected(sz, [table], pv_ref, rows_ref[...], hot_ref)
    filtered = rest_ref[...] + part
    total = filtered * filtered
    for _ in range(n_before):
        total = total + refs.pop(0)[...]
    refs[0][...] = total


def vmem(count):
    return [pl.BlockSpec(memory_space=pltpu.VMEM)] * count


def smem(count):
    return [pl.BlockSpec(memory_space=pltpu.SMEM)] * count


def in_place(arr):
    return pltpu.with_memory_space_constraint(arr, pltpu.HBM)


def shift_table(table, blocks_first, blocks_second, size_first, size_second, dim, delta):
    blocks = table.reshape(blocks_first, blocks_second, -1)
    count = blocks.shape[dim]
    size = (size_first, size_second)[dim]
    parts = []
    for at in range(count):
        source = [s for s in range(count) if (s + delta) % size == at]
        if source:
            parts.append(lax.slice_in_dim(blocks, source[0], source[0] + 1, axis=dim))
        else:
            parts.append(jnp.zeros_like(lax.slice_in_dim(blocks, 0, 1, axis=dim)))
    return jnp.concatenate(parts, axis=dim).reshape(table.shape)


def offsets(size):
    return sorted({d % size for d in (-2, -1, 1, 2)} - {0})


def shift(arr, axis, amount):
    size = lax.axis_size(axis)
    return lax.ppermute(arr, axis, [(i, (i + amount) % size) for i in range(size)])


def swap(arr, target):
    size_first = lax.axis_size("gx")
    size_second = lax.axis_size("gy")
    pairs = []
    for i in range(size_first):
        for j in range(size_second):
            ti, tj = target(i, j)
            pairs.append((i * size_second + j, ti * size_second + tj))
    return lax.ppermute(arr, ("gx", "gy"), pairs)


def orb_swap(vals, bit):
    size = lax.axis_size("orb")
    return lax.ppermute(vals, "orb", [(i, i ^ bit) for i in range(size)])


def local(orbitals, local_pot, proj_vals, proj_ids, proj_energy, cheb_coef):
    count_orb, ex, ey, nz = orbitals.shape
    slots = proj_vals.shape[0]
    size_first = lax.axis_size("gx")
    size_second = lax.axis_size("gy")
    size_orb = lax.axis_size("orb")
    paired = size_orb == 4 and count_orb == 1
    owner_size = proj_energy.shape[0] // (size_first * size_second)
    whole = size_first == 4 and size_second == 2
    if whole:
        windows = (size_first, size_second)
    else:
        windows = (min(3, size_first), min(3, size_second))
    rows = windows[0] * windows[1] * owner_size // LANES
    sz = Sizes(ex, ey, nz, slots, owner_size, rows)
    here_first = lax.axis_index("gx")
    here_second = lax.axis_index("gy")

    if whole:
        flag = jnp.bitwise_and(here_first, 1).astype(jnp.int32).reshape(1)
        energy = proj_energy.reshape(rows, LANES)
        ids = proj_ids
    else:
        flag = jnp.zeros((1,), jnp.int32)
        owner = proj_ids // owner_size
        rel_first = (owner // size_second - here_first + 1) % size_first
        rel_second = (owner % size_second - here_second + 1) % size_second
        ids = (rel_first * windows[1] + rel_second) * owner_size + proj_ids % owner_size
        grid = proj_energy.reshape(size_first, size_second, owner_size)
        grid = jnp.roll(grid, (1 - here_first, 1 - here_second), (0, 1))
        energy = grid[: windows[0], : windows[1]].reshape(rows, LANES)

    ids = jnp.transpose(ids, (0, 3, 1, 2)).reshape(slots * sz.zb * ex, ey)
    pv = proj_vals.reshape(slots * sz.cells, nz)
    pot = local_pot.reshape(sz.cells, nz)
    message_shapes = (
        jax.ShapeDtypeStruct((sz.edge_rows, LANES), F32),
        jax.ShapeDtypeStruct((sz.edge_rows + rows, LANES), F32),
        jax.ShapeDtypeStruct((sz.yedge_rows + rows, LANES), F32),
        jax.ShapeDtypeStruct((rows, LANES), F32),
    )
    field = jax.ShapeDtypeStruct((sz.cells, nz), F32)
    params = pltpu.CompilerParams(vmem_limit_bytes=48 << 20)

    def exchange(to_a, to_b, to_y, table, aside):
        if whole:
            from_b = swap(to_b, lambda i, j: (size_first - 1 - i, j))
            from_y = swap(to_y, lambda i, j: (i, 1 - j))
            from_d = swap(table, lambda i, j: (size_first - 1 - i, 1 - j))
            from_a = swap(to_a, lambda i, j: (i ^ 1, j))
            if aside is not None:
                from_d, aside = lax.optimization_barrier((from_d, aside))
            table = table + from_d + from_b[sz.edge_rows :] + from_y[sz.yedge_rows :]
            other = swap(table, lambda i, j: (i ^ 1, j))
            return [table, other], from_a, from_b, [from_y], aside
        edges_b = to_b[: sz.edge_rows]
        edges_y = to_y[: sz.yedge_rows]
        below = shift(edges_y, "gy", 1)
        above = shift(edges_y, "gy", -1)
        from_a = shift(edges_b, "gx", -1)
        from_b = shift(to_a, "gx", 1)
        for dim, axis in ((1, "gy"), (0, "gx")):
            total = table
            for delta in offsets((size_first, size_second)[dim]):
                moved = shift(table, axis, -delta)
                total = total + shift_table(
                    moved, windows[0], windows[1], size_first, size_second, dim, delta
                )
            table = total
        return [table], from_a, from_b, [below, above], aside

    def square(cheb, row_of, hot, rest, tables, *before):
        args = (cheb, energy, pv, row_of, hot, rest, *tables, *before)
        return pl.pallas_call(
            functools.partial(last_kernel, sz, len(tables), len(before)),
            out_shape=field,
            in_specs=vmem(len(args)),
            out_specs=vmem(1)[0],
            compiler_params=params,
            name="square_more" if before else "square",
        )(*args)

    def one_orbital(start):
        *messages, row_of, hot, cheb = pl.pallas_call(
            functools.partial(first_kernel, sz),
            out_shape=message_shapes
            + (
                jax.ShapeDtypeStruct((slots * sz.zb, LANES), F32),
                jax.ShapeDtypeStruct((LANES, slots * sz.zb * sz.cells), BF16),
                jax.ShapeDtypeStruct((SUBLANES, LANES), F32),
            ),
            in_specs=smem(1) + [pl.BlockSpec(memory_space=pltpu.HBM)] * 4,
            out_specs=tuple(vmem(7)),
            scratch_shapes=[
                pltpu.VMEM(start.shape, start.dtype),
                pltpu.VMEM(pv.shape, pv.dtype),
                pltpu.VMEM(ids.shape, ids.dtype),
                pltpu.SMEM(cheb_coef.shape, cheb_coef.dtype),
                pltpu.SemaphoreType.DMA((4,)),
            ],
            compiler_params=params,
            name="project_first",
        )(flag, *(in_place(arr) for arr in (start, pv, ids, cheb_coef)))
        overlap = pl.pallas_call(
            functools.partial(overlap_kernel, sz),
            out_shape=jax.ShapeDtypeStruct((slots * slots * sz.zb, LANES), F32),
            in_specs=vmem(2),
            out_specs=vmem(1)[0],
            compiler_params=params,
            name="overlap",
        )(row_of, pv)
        history = [start]
        for degree in range(1, STEPS + 1):
            tables, from_a, from_b, from_y, aside = exchange(
                *messages, overlap if degree == 1 else None
            )
            overlap = overlap if aside is None else aside
            last = degree == STEPS
            sums_shape = jax.ShapeDtypeStruct((slots * sz.zb, LANES), F32)
            if last:
                args = (cheb, from_a, from_b, *from_y, pot, *history)
            else:
                args = (from_a, from_b, *from_y, pot, pv, *history)
            rest, *sums = pl.pallas_call(
                functools.partial(local_kernel, sz, degree, len(from_y)),
                out_shape=(field,) if last else (field, sums_shape),
                in_specs=smem(1) + vmem(len(args)),
                out_specs=tuple(vmem(1 if last else 2)),
                compiler_params=params,
                name=f"local_{degree}",
            )(flag, *args)
            if last:
                if not paired:
                    return square(cheb, row_of, hot, rest, tables)
                total = functools.reduce(jnp.add, tables)
                other, other_total = orb_swap(rest, 1), orb_swap(total, 1)
                own = square(cheb, row_of, hot, rest, [total])
                return square(cheb, row_of, hot, other, [other_total], own)
            args = (*tables, energy, rest, pv, row_of, hot, *sums, overlap)
            out = pl.pallas_call(
                functools.partial(nonlocal_kernel, sz, degree, len(tables)),
                out_shape=(field,) + message_shapes,
                in_specs=smem(1) + vmem(len(args)),
                out_specs=tuple(vmem(5)),
                compiler_params=params,
                name=f"nonlocal_{degree}",
            )(flag, *args)
            history.append(out[0])
            messages = out[1:]

    density = one_orbital(orbitals[0].reshape(sz.cells, nz))
    for at in range(1, count_orb):
        density = density + one_orbital(orbitals[at].reshape(sz.cells, nz))
    scale = 1.0 / (count_orb * size_orb)
    if paired:
        density = density + orb_swap(density, 3)
    else:
        density = lax.psum(density, "orb")
    return (density * scale).reshape(ex, ey, nz)


def solution(mesh):
    return jax.shard_map(
        local,
        mesh=mesh,
        in_specs=(
            P("orb", "gx", "gy", None),
            P("gx", "gy", None),
            P(None, "gx", "gy", None),
            P(None, "gx", "gy", None),
            P(),
            P(),
        ),
        out_specs=P("gx", "gy", None),
        check_vma=False,
    )
```

```python
import functools

import jax
import jax.numpy as jnp
from jax import lax
from jax.experimental import pallas as pl
from jax.experimental.pallas import tpu as pltpu
from jax.sharding import PartitionSpec as P

LANES = 128
SUBLANES = 8
STEPS = 3
E_MID = 4.0
E_HALF = 8.0
F32 = jnp.float32
BF16 = jnp.bfloat16


def pieces(vals):
    first = vals.astype(BF16)
    second = (vals - first.astype(F32)).astype(BF16)
    return first, second


def dot(a, b, contract):
    return lax.dot_general(a, b, (contract, ((), ())), preferred_element_type=F32)


NN = ((1,), (0,))
NT = ((1,), (1,))


def iota(shape, dim):
    return lax.broadcasted_iota(jnp.int32, shape, dim)


class Sizes:
    def __init__(self, extent_first, extent_second, extent_depth, slots, owner_size, rows):
        self.ex = extent_first
        self.ey = extent_second
        self.nz = extent_depth
        self.zb = extent_depth // LANES
        self.slots = slots
        self.cells = extent_first * extent_second
        self.rows = rows
        self.xedge = 2 * extent_second
        self.yedge = extent_first * SUBLANES // 2
        self.edge_rows = self.zb * self.xedge
        self.yedge_rows = self.zb * self.yedge
        assert extent_second == 2 * SUBLANES and extent_first % 2 == 0
        assert self.cells == LANES and extent_first == SUBLANES


def rows_of_ids(sz, ids):
    copies = jnp.where(
        jnp.bitwise_and(iota((sz.ey, LANES), 1), sz.ey - 1) == iota((sz.ey, LANES), 0), 1.0, 0.0
    ).astype(BF16)
    shape = (sz.slots * sz.zb, sz.ex, LANES)
    own = iota(shape, 2) // sz.ey == iota(shape, 1)

    def flat(part):
        spread = dot(part.astype(F32).astype(BF16), copies, NN).reshape(shape)
        return jnp.sum(jnp.where(own, spread, 0.0), axis=1)

    return flat(lax.shift_right_logical(ids, 7)), flat(jnp.bitwise_and(ids, LANES - 1))


def chunk(sz, arr, zb, slot):
    at = slot * sz.zb + zb
    return arr[at : at + 1, :]


def chunks(sz):
    return [(zb, slot) for zb in range(sz.zb) for slot in range(sz.slots)]


def slot_sums(sz, vals, pv_ref):
    eye = iota((sz.cells, LANES), 0) == iota((sz.cells, LANES), 1)
    eye_all = jnp.concatenate([eye] * sz.slots, axis=0)
    sums = {}
    for zb in range(sz.zb):
        first, second = pieces(vals[:, zb * LANES : (zb + 1) * LANES])
        weights = pv_ref[:, zb * LANES : (zb + 1) * LANES]
        cross = dot(
            jnp.concatenate([weights, weights], axis=1),
            jnp.concatenate([first, second], axis=1),
            NT,
        )
        cross = jnp.where(eye_all, cross, 0.0)
        for slot in range(sz.slots):
            part = cross[slot * sz.cells : (slot + 1) * sz.cells]
            sums[zb, slot] = jnp.sum(part, axis=0, keepdims=True)
    return sums


def partial_table(sz, sums, row_of, hot_ref):
    spread_first, spread_second = [], []
    table_iota = iota((sz.rows, LANES), 0).astype(F32)
    for zb, slot in chunks(sz):
        hit = chunk(sz, row_of, zb, slot) == table_iota
        a, b = pieces(sums[zb, slot])
        spread_first.append(jnp.where(hit, a.astype(F32), 0.0).astype(BF16))
        spread_second.append(jnp.where(hit, b.astype(F32), 0.0).astype(BF16))
    lhs = jnp.concatenate(
        [jnp.concatenate(spread_first, axis=1), jnp.concatenate(spread_second, axis=1)], axis=0
    )
    both = dot(lhs, hot_ref[...], NT)
    return both[: sz.rows] + both[sz.rows :]


def overlap_row(sz, slot, other, zb):
    return (slot * sz.slots + other) * sz.zb + zb


def overlap_kernel(sz, after_ref, pv_ref, overlap_ref):
    eye = iota((sz.cells, LANES), 0) == iota((sz.cells, LANES), 1)
    for zb in range(sz.zb):
        weights = pv_ref[:, zb * LANES : (zb + 1) * LANES]
        cross = dot(weights, weights, NT)
        for slot in range(sz.slots):
            rows = cross[slot * sz.cells : (slot + 1) * sz.cells]
            for other in range(slot, sz.slots):
                block = rows[:, other * sz.cells : (other + 1) * sz.cells]
                row = jnp.sum(jnp.where(eye, block, 0.0), axis=0, keepdims=True)
                for at in {(slot, other), (other, slot)}:
                    at = overlap_row(sz, *at, zb)
                    overlap_ref[at : at + 1, :] = row


def projected(sz, tables, pv_ref, row_of, hot_ref):
    count = len(tables)
    split = [piece for table in tables for piece in pieces(table)]
    found = dot(jnp.concatenate(split, axis=0), hot_ref[...], NN)
    found = [
        found[2 * n * sz.rows : (2 * n + 1) * sz.rows]
        + found[(2 * n + 1) * sz.rows : (2 * n + 2) * sz.rows]
        for n in range(count)
    ]
    table_iota = iota((sz.rows, LANES), 0).astype(F32)
    eye = iota((sz.cells, LANES), 0) == iota((sz.cells, LANES), 1)
    result = [[] for _ in tables]
    weights = [{} for _ in tables]
    for zb in range(sz.zb):
        diag = [[] for _ in range(2 * count)]
        for slot in range(sz.slots):
            at = (zb * sz.slots + slot) * LANES
            hit = chunk(sz, row_of, zb, slot) == table_iota
            for n in range(count):
                weight = jnp.sum(
                    jnp.where(hit, found[n][:, at : at + LANES], 0.0), axis=0, keepdims=True
                )
                weights[n][zb, slot] = weight
                a, b = pieces(jnp.where(eye, weight, 0.0))
                diag[2 * n].append(a)
                diag[2 * n + 1].append(b)
        lhs = jnp.concatenate([jnp.concatenate(parts, axis=1) for parts in diag], axis=0)
        both = dot(lhs, pv_ref[:, zb * LANES : (zb + 1) * LANES], NN)
        for n in range(count):
            at = 2 * n * sz.cells
            result[n].append(both[at : at + sz.cells] + both[at + sz.cells : at + 2 * sz.cells])
    return [jnp.concatenate(parts, axis=1) for parts in result], weights


def from_message(sz, msg_ref, rows):
    return jnp.concatenate(
        [msg_ref[zb * rows : (zb + 1) * rows, :] for zb in range(sz.zb)], axis=1
    )


def to_message(sz, msg_ref, vals):
    rows = vals.shape[0]
    for zb in range(sz.zb):
        msg_ref[zb * rows : (zb + 1) * rows, :] = vals[:, zb * LANES : (zb + 1) * LANES]


def second_edges(sz, vals):
    tiles = vals.reshape(sz.ex, 2, SUBLANES, sz.nz)
    sub = iota((sz.ex // 2, SUBLANES, sz.nz), 1)
    even = tiles.reshape(sz.ex // 2, 2, 2, SUBLANES, sz.nz)
    outer_even = jnp.where(sub < 4, even[:, 0, 0], even[:, 0, 1])
    outer_odd = jnp.where(sub < 4, even[:, 1, 0], even[:, 1, 1])
    odd = pltpu.roll(outer_odd, 4, axis=1)
    keep = jnp.logical_or(sub < 2, sub >= 6)
    return jnp.where(keep, outer_even, odd).reshape(sz.yedge, sz.nz)


def second_halo(sz, packed):
    pairs = packed.reshape(sz.ex // 2, SUBLANES, sz.nz)
    odd = pltpu.roll(pairs, 4, axis=1)
    return jnp.stack([pairs, odd], axis=1).reshape(sz.ex, SUBLANES, sz.nz)


def stencil(sz, vals, low, high, below, above):
    result = -90.0 * vals
    tall = jnp.concatenate([low, vals, high], axis=0)
    step = sz.ey
    cells = sz.cells
    near = tall[step : step + cells] + tall[3 * step : 3 * step + cells]
    far = tall[0:cells] + tall[4 * step : 4 * step + cells]

    near = near + pltpu.roll(vals, 1, axis=1) + pltpu.roll(vals, sz.nz - 1, axis=1)
    far = far + pltpu.roll(vals, 2, axis=1) + pltpu.roll(vals, sz.nz - 2, axis=1)

    tiles = vals.reshape(2 * sz.ex, SUBLANES, sz.nz)
    sub = iota((2 * sz.ex, SUBLANES, sz.nz), 1)

    def shifted(amount, outer, from_below):
        mine = pltpu.roll(tiles, amount, axis=1)
        theirs = pltpu.roll(outer, amount, axis=1)
        pairs = mine.reshape(sz.ex, 2, SUBLANES, sz.nz)
        if from_below:
            other = jnp.stack([theirs, pairs[:, 0]], axis=1)
            mask = sub < amount
        else:
            other = jnp.stack([pairs[:, 1], theirs], axis=1)
            mask = sub >= amount
        return jnp.where(mask, other.reshape(tiles.shape), mine).reshape(vals.shape)

    near = near + shifted(1, below, True) + shifted(SUBLANES - 1, above, False)
    far = far + shifted(2, below, True) + shifted(SUBLANES - 2, above, False)
    return result + 16.0 * near - far


def emit(sz, vals, table, flag_ref, ab_ref, bb_ref, yb_ref, table_ref):
    table_ref[...] = table
    flag = flag_ref[0]
    top = vals[sz.cells - sz.xedge :]
    bottom = vals[: sz.xedge]
    is_high = flag == 0
    to_message(sz, ab_ref, jnp.where(is_high, top, bottom))
    ab_ref[sz.edge_rows :, :] = table
    to_message(sz, bb_ref, jnp.where(is_high, bottom, top))
    bb_ref[sz.edge_rows :, :] = table
    to_message(sz, yb_ref, second_edges(sz, vals))
    yb_ref[sz.yedge_rows :, :] = table


def first_kernel(
    sz,
    flag_ref,
    vals_hbm,
    pv_hbm,
    ids_hbm,
    cheb_hbm,
    ab_ref,
    bb_ref,
    yb_ref,
    table_ref,
    rows_ref,
    hot_ref,
    cheb_out,
    vals_ref,
    pv_ref,
    ids_ref,
    cheb_ref,
    sems,
):
    get_ids = pltpu.make_async_copy(ids_hbm, ids_ref, sems.at[0])
    get_pv = pltpu.make_async_copy(pv_hbm, pv_ref, sems.at[1])
    get_vals = pltpu.make_async_copy(vals_hbm, vals_ref, sems.at[2])
    get_cheb = pltpu.make_async_copy(cheb_hbm, cheb_ref, sems.at[3])
    get_ids.start()
    get_vals.start()
    get_pv.start()
    get_cheb.start()
    get_ids.wait()
    row_of, lane_of = rows_of_ids(sz, ids_ref[...])
    rows_ref[...] = row_of
    lane_iota = iota((LANES, LANES), 0).astype(F32)
    for at, (zb, slot) in enumerate(chunks(sz)):
        hot_ref[:, at * LANES : (at + 1) * LANES] = jnp.where(
            chunk(sz, lane_of, zb, slot) == lane_iota, 1.0, 0.0
        ).astype(BF16)
    get_vals.wait()
    get_pv.wait()
    vals = vals_ref[...]
    table = partial_table(sz, slot_sums(sz, vals, pv_ref), row_of, hot_ref)
    emit(sz, vals, table, flag_ref, ab_ref, bb_ref, yb_ref, table_ref)
    get_cheb.wait()
    for n in range(STEPS + 1):
        cheb_out[n : n + 1, :] = jnp.full((1, LANES), cheb_ref[n], F32)


def coefficient(sz, cheb_ref, n):
    row = cheb_ref[n : n + 1, :]
    return jnp.concatenate([row] * sz.zb, axis=1)


def local_kernel(sz, degree, n_y, flag_ref, *refs):
    refs = list(refs)
    cheb_ref = refs.pop(0) if degree == STEPS else None
    a_ref, b_ref = refs.pop(0), refs.pop(0)
    y_refs = [refs.pop(0) for _ in range(n_y)]
    pot_ref = refs.pop(0)
    if degree < STEPS:
        pv_ref, sums_ref = refs.pop(0), refs.pop()
    *history, out_ref = refs
    vals = history[-1][...]

    from_a = from_message(sz, a_ref, sz.xedge)
    from_b = from_message(sz, b_ref, sz.xedge)
    is_high = flag_ref[0] == 0
    low = jnp.where(is_high, from_b, from_a)
    high = jnp.where(is_high, from_a, from_b)
    outer = [second_halo(sz, from_message(sz, ref, sz.yedge)) for ref in y_refs]
    laplace12 = stencil(sz, vals, low, high, outer[0], outer[-1])
    double = 1.0 if degree == 1 else 2.0
    result = laplace12 * (-0.5 / 12.0 / E_HALF * double) + vals * (
        (pot_ref[...] - E_MID) * (double / E_HALF)
    )
    if degree > 1:
        result = result - history[-2][...]
    if degree == STEPS:
        result = coefficient(sz, cheb_ref, STEPS) * result
        for n in range(STEPS):
            result = result + coefficient(sz, cheb_ref, n) * history[n][...]
    out_ref[...] = result
    if degree < STEPS:
        for (zb, slot), row in slot_sums(sz, result, pv_ref).items():
            at = slot * sz.zb + zb
            sums_ref[at : at + 1, :] = row


def added(table_refs):
    table = table_refs[0][...]
    for ref in table_refs[1:]:
        table = table + ref[...]
    return table


def nonlocal_kernel(sz, degree, n_tables, flag_ref, *refs):
    refs = list(refs)
    table_refs = [refs.pop(0) for _ in range(n_tables)]
    energy_ref, rest_ref, pv_ref, rows_ref, hot_ref = (refs.pop(0) for _ in range(5))
    sums_ref, overlap_ref = refs.pop(0), refs.pop(0)
    row_of = rows_ref[...]
    double = 1.0 if degree == 1 else 2.0
    table = added(table_refs) * (energy_ref[...] * (double / E_HALF))
    (part,), (weights,) = projected(sz, [table], pv_ref, row_of, hot_ref)
    sums = {}
    for zb, slot in chunks(sz):
        total = chunk(sz, sums_ref, zb, slot)
        for other in range(sz.slots):
            at = overlap_row(sz, slot, other, zb)
            total = total + overlap_ref[at : at + 1, :] * weights[zb, other]
        sums[zb, slot] = total
    table = partial_table(sz, sums, row_of, hot_ref)
    result = rest_ref[...] + part
    refs[0][...] = result
    emit(sz, result, table, flag_ref, *refs[1:])


def last_kernel(sz, n_tables, n_before, cheb_ref, *refs):
    refs = list(refs)
    energy_ref, pv_ref, rows_ref, hot_ref, rest_ref = (refs.pop(0) for _ in range(5))
    table = added([refs.pop(0) for _ in range(n_tables)])
    table = table * (energy_ref[...] * (2.0 / E_HALF * cheb_ref[STEPS : STEPS + 1, :]))
    (part,), _ = projected(sz, [table], pv_ref, rows_ref[...], hot_ref)
    filtered = rest_ref[...] + part
    total = filtered * filtered
    for _ in range(n_before):
        total = total + refs.pop(0)[...]
    refs[0][...] = total


def vmem(count):
    return [pl.BlockSpec(memory_space=pltpu.VMEM)] * count


def smem(count):
    return [pl.BlockSpec(memory_space=pltpu.SMEM)] * count


def in_place(arr):
    return pltpu.with_memory_space_constraint(arr, pltpu.HBM)


def shift_table(table, blocks_first, blocks_second, size_first, size_second, dim, delta):
    blocks = table.reshape(blocks_first, blocks_second, -1)
    count = blocks.shape[dim]
    size = (size_first, size_second)[dim]
    parts = []
    for at in range(count):
        source = [s for s in range(count) if (s + delta) % size == at]
        if source:
            parts.append(lax.slice_in_dim(blocks, source[0], source[0] + 1, axis=dim))
        else:
            parts.append(jnp.zeros_like(lax.slice_in_dim(blocks, 0, 1, axis=dim)))
    return jnp.concatenate(parts, axis=dim).reshape(table.shape)


def offsets(size):
    return sorted({d % size for d in (-2, -1, 1, 2)} - {0})


def shift(arr, axis, amount):
    size = lax.axis_size(axis)
    return lax.ppermute(arr, axis, [(i, (i + amount) % size) for i in range(size)])


def swap(arr, target):
    size_first = lax.axis_size("gx")
    size_second = lax.axis_size("gy")
    pairs = []
    for i in range(size_first):
        for j in range(size_second):
            ti, tj = target(i, j)
            pairs.append((i * size_second + j, ti * size_second + tj))
    return lax.ppermute(arr, ("gx", "gy"), pairs)


def orb_swap(vals, bit):
    size = lax.axis_size("orb")
    return lax.ppermute(vals, "orb", [(i, i ^ bit) for i in range(size)])


def local(orbitals, local_pot, proj_vals, proj_ids, proj_energy, cheb_coef):
    count_orb, ex, ey, nz = orbitals.shape
    slots = proj_vals.shape[0]
    size_first = lax.axis_size("gx")
    size_second = lax.axis_size("gy")
    size_orb = lax.axis_size("orb")
    paired = size_orb == 4 and count_orb == 1
    owner_size = proj_energy.shape[0] // (size_first * size_second)
    whole = size_first == 4 and size_second == 2
    if whole:
        windows = (size_first, size_second)
    else:
        windows = (min(3, size_first), min(3, size_second))
    rows = windows[0] * windows[1] * owner_size // LANES
    sz = Sizes(ex, ey, nz, slots, owner_size, rows)
    here_first = lax.axis_index("gx")
    here_second = lax.axis_index("gy")

    if whole:
        flag = jnp.bitwise_and(here_first, 1).astype(jnp.int32).reshape(1)
        energy = proj_energy.reshape(rows, LANES)
        ids = proj_ids
    else:
        flag = jnp.zeros((1,), jnp.int32)
        owner = proj_ids // owner_size
        rel_first = (owner // size_second - here_first + 1) % size_first
        rel_second = (owner % size_second - here_second + 1) % size_second
        ids = (rel_first * windows[1] + rel_second) * owner_size + proj_ids % owner_size
        grid = proj_energy.reshape(size_first, size_second, owner_size)
        grid = jnp.roll(grid, (1 - here_first, 1 - here_second), (0, 1))
        energy = grid[: windows[0], : windows[1]].reshape(rows, LANES)

    ids = jnp.transpose(ids, (0, 3, 1, 2)).reshape(slots * sz.zb * ex, ey)
    pv = proj_vals.reshape(slots * sz.cells, nz)
    pot = local_pot.reshape(sz.cells, nz)
    message_shapes = (
        jax.ShapeDtypeStruct((sz.edge_rows + rows, LANES), F32),
        jax.ShapeDtypeStruct((sz.edge_rows + rows, LANES), F32),
        jax.ShapeDtypeStruct((sz.yedge_rows + rows, LANES), F32),
        jax.ShapeDtypeStruct((rows, LANES), F32),
    )
    field = jax.ShapeDtypeStruct((sz.cells, nz), F32)
    params = pltpu.CompilerParams(vmem_limit_bytes=48 << 20)

    def exchange(to_a, to_b, to_y, table, aside, pair_last):
        if whole and pair_last:
            from_b = swap(to_b, lambda i, j: (size_first - 1 - i, j))
            from_y = swap(to_y, lambda i, j: (i, 1 - j))
            from_d = swap(table, lambda i, j: (size_first - 1 - i, 1 - j))
            from_a = swap(to_a[: sz.edge_rows], lambda i, j: (i ^ 1, j))
            if aside is not None:
                from_d, aside = lax.optimization_barrier((from_d, aside))
            table = table + from_d + from_y[sz.yedge_rows :] + from_b[sz.edge_rows :]
            other = swap(table, lambda i, j: (i ^ 1, j))
            return [table, other], from_a, from_b, [from_y], aside
        if whole:
            from_a = swap(to_a, lambda i, j: (i ^ 1, j))
            from_b = swap(to_b, lambda i, j: (size_first - 1 - i, j))
            from_y = swap(to_y, lambda i, j: (i, 1 - j))
            chip = table + from_a[sz.edge_rows :]
            if aside is not None:
                aside = aside(chip, pv)
            from_d = swap(chip, lambda i, j: (size_first - 1 - i, 1 - j))
            if aside is not None:
                from_y, aside = lax.optimization_barrier((from_y, aside))
            beside = from_y[sz.yedge_rows :] + from_b[sz.edge_rows :]
            other = swap(beside, lambda i, j: (i ^ 1, j))
            return [chip, beside, other, from_d], from_a, from_b, [from_y], aside
        to_a = to_a[: sz.edge_rows]
        if aside is not None:
            aside = aside(table, pv)
        edges_b = to_b[: sz.edge_rows]
        edges_y = to_y[: sz.yedge_rows]
        below = shift(edges_y, "gy", 1)
        above = shift(edges_y, "gy", -1)
        from_a = shift(edges_b, "gx", -1)
        from_b = shift(to_a, "gx", 1)
        for dim, axis in ((1, "gy"), (0, "gx")):
            total = table
            for delta in offsets((size_first, size_second)[dim]):
                moved = shift(table, axis, -delta)
                total = total + shift_table(
                    moved, windows[0], windows[1], size_first, size_second, dim, delta
                )
            table = total
        return [table], from_a, from_b, [below, above], aside

    def square(cheb, row_of, hot, rest, tables, *before):
        args = (cheb, energy, pv, row_of, hot, rest, *tables, *before)
        return pl.pallas_call(
            functools.partial(last_kernel, sz, len(tables), len(before)),
            out_shape=field,
            in_specs=vmem(len(args)),
            out_specs=vmem(1)[0],
            compiler_params=params,
            name="square_more" if before else "square",
        )(*args)

    def one_orbital(start):
        *messages, row_of, hot, cheb = pl.pallas_call(
            functools.partial(first_kernel, sz),
            out_shape=message_shapes
            + (
                jax.ShapeDtypeStruct((slots * sz.zb, LANES), F32),
                jax.ShapeDtypeStruct((LANES, slots * sz.zb * sz.cells), BF16),
                jax.ShapeDtypeStruct((SUBLANES, LANES), F32),
            ),
            in_specs=smem(1) + [pl.BlockSpec(memory_space=pltpu.HBM)] * 4,
            out_specs=tuple(vmem(7)),
            scratch_shapes=[
                pltpu.VMEM(start.shape, start.dtype),
                pltpu.VMEM(pv.shape, pv.dtype),
                pltpu.VMEM(ids.shape, ids.dtype),
                pltpu.SMEM(cheb_coef.shape, cheb_coef.dtype),
                pltpu.SemaphoreType.DMA((4,)),
            ],
            compiler_params=params,
            name="project_first",
        )(flag, *(in_place(arr) for arr in (start, pv, ids, cheb_coef)))
        overlap_after = pl.pallas_call(
            functools.partial(overlap_kernel, sz),
            out_shape=jax.ShapeDtypeStruct((slots * slots * sz.zb, LANES), F32),
            in_specs=vmem(2),
            out_specs=vmem(1)[0],
            compiler_params=params,
            name="overlap",
        )
        overlap = None
        history = [start]
        for degree in range(1, STEPS + 1):
            tables, from_a, from_b, from_y, aside = exchange(
                *messages, overlap_after if degree == 1 else None, degree == STEPS
            )
            overlap = overlap if aside is None else aside
            last = degree == STEPS
            sums_shape = jax.ShapeDtypeStruct((slots * sz.zb, LANES), F32)
            if last:
                args = (cheb, from_a, from_b, *from_y, pot, *history)
            else:
                args = (from_a, from_b, *from_y, pot, pv, *history)
            rest, *sums = pl.pallas_call(
                functools.partial(local_kernel, sz, degree, len(from_y)),
                out_shape=(field,) if last else (field, sums_shape),
                in_specs=smem(1) + vmem(len(args)),
                out_specs=tuple(vmem(1 if last else 2)),
                compiler_params=params,
                name=f"local_{degree}",
            )(flag, *args)
            if last:
                if not paired:
                    return square(cheb, row_of, hot, rest, tables)
                total = functools.reduce(jnp.add, tables)
                other, other_total = orb_swap(rest, 1), orb_swap(total, 1)
                own = square(cheb, row_of, hot, rest, [total])
                return square(cheb, row_of, hot, other, [other_total], own)
            args = (*tables, energy, rest, pv, row_of, hot, *sums, overlap)
            out = pl.pallas_call(
                functools.partial(nonlocal_kernel, sz, degree, len(tables)),
                out_shape=(field,) + message_shapes,
                in_specs=smem(1) + vmem(len(args)),
                out_specs=tuple(vmem(5)),
                compiler_params=params,
                name=f"nonlocal_{degree}",
            )(flag, *args)
            history.append(out[0])
            messages = out[1:]

    density = one_orbital(orbitals[0].reshape(sz.cells, nz))
    for at in range(1, count_orb):
        density = density + one_orbital(orbitals[at].reshape(sz.cells, nz))
    scale = 1.0 / (count_orb * size_orb)
    if paired:
        density = density + orb_swap(density, 3)
    else:
        density = lax.psum(density, "orb")
    return (density * scale).reshape(ex, ey, nz)


def solution(mesh):
    return jax.shard_map(
        local,
        mesh=mesh,
        in_specs=(
            P("orb", "gx", "gy", None),
            P("gx", "gy", None),
            P(None, "gx", "gy", None),
            P(None, "gx", "gy", None),
            P(),
            P(),
        ),
        out_specs=P("gx", "gy", None),
        check_vma=False,
    )
```

```python
import functools

import jax
import jax.numpy as jnp
from jax import lax
from jax.experimental import pallas as pl
from jax.experimental.pallas import tpu as pltpu
from jax.sharding import PartitionSpec as P

LANES = 128
SUBLANES = 8
STEPS = 3
E_MID = 4.0
E_HALF = 8.0
F32 = jnp.float32
BF16 = jnp.bfloat16


def pieces(vals):
    first = vals.astype(BF16)
    second = (vals - first.astype(F32)).astype(BF16)
    return first, second


def dot(a, b, contract):
    return lax.dot_general(a, b, (contract, ((), ())), preferred_element_type=F32)


NN = ((1,), (0,))
NT = ((1,), (1,))


def iota(shape, dim):
    return lax.broadcasted_iota(jnp.int32, shape, dim)


class Sizes:
    def __init__(self, extent_first, extent_second, extent_depth, slots, owner_size, rows):
        self.ex = extent_first
        self.ey = extent_second
        self.nz = extent_depth
        self.zb = extent_depth // LANES
        self.slots = slots
        self.cells = extent_first * extent_second
        self.rows = rows
        self.xedge = 2 * extent_second
        self.yedge = extent_first * SUBLANES // 2
        self.edge_rows = self.zb * self.xedge
        self.yedge_rows = self.zb * self.yedge
        assert extent_second == 2 * SUBLANES and extent_first % 2 == 0
        assert self.cells == LANES and extent_first == SUBLANES


def rows_of_ids(sz, ids):
    copies = jnp.where(
        jnp.bitwise_and(iota((sz.ey, LANES), 1), sz.ey - 1) == iota((sz.ey, LANES), 0), 1.0, 0.0
    ).astype(BF16)
    shape = (sz.slots * sz.zb, sz.ex, LANES)
    own = iota(shape, 2) // sz.ey == iota(shape, 1)

    def flat(part):
        spread = dot(part.astype(F32).astype(BF16), copies, NN).reshape(shape)
        return jnp.sum(jnp.where(own, spread, 0.0), axis=1)

    return flat(lax.shift_right_logical(ids, 7)), flat(jnp.bitwise_and(ids, LANES - 1))


def chunk(sz, arr, zb, slot):
    at = slot * sz.zb + zb
    return arr[at : at + 1, :]


def chunks(sz):
    return [(zb, slot) for zb in range(sz.zb) for slot in range(sz.slots)]


def slot_sums(sz, vals, pv_ref):
    eye = iota((sz.cells, LANES), 0) == iota((sz.cells, LANES), 1)
    eye_all = jnp.concatenate([eye] * sz.slots, axis=0)
    sums = {}
    for zb in range(sz.zb):
        first, second = pieces(vals[:, zb * LANES : (zb + 1) * LANES])
        weights = pv_ref[:, zb * LANES : (zb + 1) * LANES]
        cross = dot(
            jnp.concatenate([weights, weights], axis=1),
            jnp.concatenate([first, second], axis=1),
            NT,
        )
        cross = jnp.where(eye_all, cross, 0.0)
        for slot in range(sz.slots):
            part = cross[slot * sz.cells : (slot + 1) * sz.cells]
            sums[zb, slot] = jnp.sum(part, axis=0, keepdims=True)
    return sums


def partial_table(sz, sums, row_of, hot_ref):
    spread_first, spread_second = [], []
    table_iota = iota((sz.rows, LANES), 0).astype(F32)
    for zb, slot in chunks(sz):
        hit = chunk(sz, row_of, zb, slot) == table_iota
        a, b = pieces(sums[zb, slot])
        spread_first.append(jnp.where(hit, a.astype(F32), 0.0).astype(BF16))
        spread_second.append(jnp.where(hit, b.astype(F32), 0.0).astype(BF16))
    lhs = jnp.concatenate(
        [jnp.concatenate(spread_first, axis=1), jnp.concatenate(spread_second, axis=1)], axis=0
    )
    both = dot(lhs, hot_ref[...], NT)
    return both[: sz.rows] + both[sz.rows :]


def overlap_row(sz, slot, other, zb):
    return (slot * sz.slots + other) * sz.zb + zb


def overlap_kernel(sz, after_ref, pv_ref, overlap_ref):
    eye = iota((sz.cells, LANES), 0) == iota((sz.cells, LANES), 1)
    for zb in range(sz.zb):
        weights = pv_ref[:, zb * LANES : (zb + 1) * LANES]
        cross = dot(weights, weights, NT)
        for slot in range(sz.slots):
            rows = cross[slot * sz.cells : (slot + 1) * sz.cells]
            for other in range(slot, sz.slots):
                block = rows[:, other * sz.cells : (other + 1) * sz.cells]
                row = jnp.sum(jnp.where(eye, block, 0.0), axis=0, keepdims=True)
                for at in {(slot, other), (other, slot)}:
                    at = overlap_row(sz, *at, zb)
                    overlap_ref[at : at + 1, :] = row


def projected(sz, tables, pv_ref, row_of, hot_ref):
    count = len(tables)
    split = [piece for table in tables for piece in pieces(table)]
    found = dot(jnp.concatenate(split, axis=0), hot_ref[...], NN)
    found = [
        found[2 * n * sz.rows : (2 * n + 1) * sz.rows]
        + found[(2 * n + 1) * sz.rows : (2 * n + 2) * sz.rows]
        for n in range(count)
    ]
    table_iota = iota((sz.rows, LANES), 0).astype(F32)
    eye = iota((sz.cells, LANES), 0) == iota((sz.cells, LANES), 1)
    result = [[] for _ in tables]
    weights = [{} for _ in tables]
    for zb in range(sz.zb):
        diag = [[] for _ in range(2 * count)]
        for slot in range(sz.slots):
            at = (zb * sz.slots + slot) * LANES
            hit = chunk(sz, row_of, zb, slot) == table_iota
            for n in range(count):
                weight = jnp.sum(
                    jnp.where(hit, found[n][:, at : at + LANES], 0.0), axis=0, keepdims=True
                )
                weights[n][zb, slot] = weight
                a, b = pieces(jnp.where(eye, weight, 0.0))
                diag[2 * n].append(a)
                diag[2 * n + 1].append(b)
        lhs = jnp.concatenate([jnp.concatenate(parts, axis=1) for parts in diag], axis=0)
        both = dot(lhs, pv_ref[:, zb * LANES : (zb + 1) * LANES], NN)
        for n in range(count):
            at = 2 * n * sz.cells
            result[n].append(both[at : at + sz.cells] + both[at + sz.cells : at + 2 * sz.cells])
    return [jnp.concatenate(parts, axis=1) for parts in result], weights


def from_message(sz, msg_ref, rows):
    return jnp.concatenate(
        [msg_ref[zb * rows : (zb + 1) * rows, :] for zb in range(sz.zb)], axis=1
    )


def to_message(sz, msg_ref, vals):
    rows = vals.shape[0]
    for zb in range(sz.zb):
        msg_ref[zb * rows : (zb + 1) * rows, :] = vals[:, zb * LANES : (zb + 1) * LANES]


def second_edges(sz, vals):
    tiles = vals.reshape(sz.ex, 2, SUBLANES, sz.nz)
    sub = iota((sz.ex // 2, SUBLANES, sz.nz), 1)
    even = tiles.reshape(sz.ex // 2, 2, 2, SUBLANES, sz.nz)
    outer_even = jnp.where(sub < 4, even[:, 0, 0], even[:, 0, 1])
    outer_odd = jnp.where(sub < 4, even[:, 1, 0], even[:, 1, 1])
    odd = pltpu.roll(outer_odd, 4, axis=1)
    keep = jnp.logical_or(sub < 2, sub >= 6)
    return jnp.where(keep, outer_even, odd).reshape(sz.yedge, sz.nz)


def second_halo(sz, packed):
    pairs = packed.reshape(sz.ex // 2, SUBLANES, sz.nz)
    odd = pltpu.roll(pairs, 4, axis=1)
    return jnp.stack([pairs, odd], axis=1).reshape(sz.ex, SUBLANES, sz.nz)


def stencil(sz, vals, low, high, below, above):
    result = -90.0 * vals
    tall = jnp.concatenate([low, vals, high], axis=0)
    step = sz.ey
    cells = sz.cells
    near = tall[step : step + cells] + tall[3 * step : 3 * step + cells]
    far = tall[0:cells] + tall[4 * step : 4 * step + cells]

    near = near + pltpu.roll(vals, 1, axis=1) + pltpu.roll(vals, sz.nz - 1, axis=1)
    far = far + pltpu.roll(vals, 2, axis=1) + pltpu.roll(vals, sz.nz - 2, axis=1)

    tiles = vals.reshape(2 * sz.ex, SUBLANES, sz.nz)
    sub = iota((2 * sz.ex, SUBLANES, sz.nz), 1)

    def shifted(amount, outer, from_below):
        mine = pltpu.roll(tiles, amount, axis=1)
        theirs = pltpu.roll(outer, amount, axis=1)
        pairs = mine.reshape(sz.ex, 2, SUBLANES, sz.nz)
        if from_below:
            other = jnp.stack([theirs, pairs[:, 0]], axis=1)
            mask = sub < amount
        else:
            other = jnp.stack([pairs[:, 1], theirs], axis=1)
            mask = sub >= amount
        return jnp.where(mask, other.reshape(tiles.shape), mine).reshape(vals.shape)

    near = near + shifted(1, below, True) + shifted(SUBLANES - 1, above, False)
    far = far + shifted(2, below, True) + shifted(SUBLANES - 2, above, False)
    return result + 16.0 * near - far


def emit(sz, vals, table, flag_ref, ab_ref, bb_ref, yb_ref, table_ref):
    table_ref[...] = table
    flag = flag_ref[0]
    top = vals[sz.cells - sz.xedge :]
    bottom = vals[: sz.xedge]
    is_high = flag == 0
    to_message(sz, ab_ref, jnp.where(is_high, top, bottom))
    ab_ref[sz.edge_rows :, :] = table
    to_message(sz, bb_ref, jnp.where(is_high, bottom, top))
    bb_ref[sz.edge_rows :, :] = table
    to_message(sz, yb_ref, second_edges(sz, vals))
    yb_ref[sz.yedge_rows :, :] = table


def first_kernel(
    sz,
    flag_ref,
    vals_hbm,
    pv_hbm,
    ids_hbm,
    cheb_hbm,
    ab_ref,
    bb_ref,
    yb_ref,
    table_ref,
    rows_ref,
    hot_ref,
    cheb_out,
    vals_ref,
    pv_ref,
    ids_ref,
    cheb_ref,
    sems,
):
    get_ids = pltpu.make_async_copy(ids_hbm, ids_ref, sems.at[0])
    get_pv = pltpu.make_async_copy(pv_hbm, pv_ref, sems.at[1])
    get_vals = pltpu.make_async_copy(vals_hbm, vals_ref, sems.at[2])
    get_cheb = pltpu.make_async_copy(cheb_hbm, cheb_ref, sems.at[3])
    get_ids.start()
    get_vals.start()
    get_pv.start()
    get_cheb.start()
    get_ids.wait()
    row_of, lane_of = rows_of_ids(sz, ids_ref[...])
    rows_ref[...] = row_of
    lane_iota = iota((LANES, LANES), 0).astype(F32)
    for at, (zb, slot) in enumerate(chunks(sz)):
        hot_ref[:, at * LANES : (at + 1) * LANES] = jnp.where(
            chunk(sz, lane_of, zb, slot) == lane_iota, 1.0, 0.0
        ).astype(BF16)
    get_vals.wait()
    get_pv.wait()
    vals = vals_ref[...]
    table = partial_table(sz, slot_sums(sz, vals, pv_ref), row_of, hot_ref)
    emit(sz, vals, table, flag_ref, ab_ref, bb_ref, yb_ref, table_ref)
    get_cheb.wait()
    for n in range(STEPS + 1):
        cheb_out[n : n + 1, :] = jnp.full((1, LANES), cheb_ref[n], F32)


def coefficient(sz, cheb_ref, n):
    row = cheb_ref[n : n + 1, :]
    return jnp.concatenate([row] * sz.zb, axis=1)


def local_kernel(sz, degree, n_y, flag_ref, *refs):
    refs = list(refs)
    cheb_ref = refs.pop(0) if degree == STEPS else None
    a_ref, b_ref = refs.pop(0), refs.pop(0)
    y_refs = [refs.pop(0) for _ in range(n_y)]
    pot_ref = refs.pop(0)
    if degree < STEPS:
        pv_ref, sums_ref = refs.pop(0), refs.pop()
    *history, out_ref = refs
    vals = history[-1][...]

    from_a = from_message(sz, a_ref, sz.xedge)
    from_b = from_message(sz, b_ref, sz.xedge)
    is_high = flag_ref[0] == 0
    low = jnp.where(is_high, from_b, from_a)
    high = jnp.where(is_high, from_a, from_b)
    outer = [second_halo(sz, from_message(sz, ref, sz.yedge)) for ref in y_refs]
    laplace12 = stencil(sz, vals, low, high, outer[0], outer[-1])
    double = 1.0 if degree == 1 else 2.0
    result = laplace12 * (-0.5 / 12.0 / E_HALF * double) + vals * (
        (pot_ref[...] - E_MID) * (double / E_HALF)
    )
    if degree > 1:
        result = result - history[-2][...]
    if degree == STEPS:
        result = coefficient(sz, cheb_ref, STEPS) * result
        for n in range(STEPS):
            result = result + coefficient(sz, cheb_ref, n) * history[n][...]
    out_ref[...] = result
    if degree < STEPS:
        for (zb, slot), row in slot_sums(sz, result, pv_ref).items():
            at = slot * sz.zb + zb
            sums_ref[at : at + 1, :] = row


def added(table_refs):
    table = table_refs[0][...]
    for ref in table_refs[1:]:
        table = table + ref[...]
    return table


def nonlocal_kernel(sz, degree, n_tables, flag_ref, *refs):
    refs = list(refs)
    table_refs = [refs.pop(0) for _ in range(n_tables)]
    energy_ref, rest_ref, pv_ref, rows_ref, hot_ref = (refs.pop(0) for _ in range(5))
    sums_ref, overlap_ref = refs.pop(0), refs.pop(0)
    row_of = rows_ref[...]
    double = 1.0 if degree == 1 else 2.0
    table = added(table_refs) * (energy_ref[...] * (double / E_HALF))
    (part,), (weights,) = projected(sz, [table], pv_ref, row_of, hot_ref)
    sums = {}
    for zb, slot in chunks(sz):
        total = chunk(sz, sums_ref, zb, slot)
        for other in range(sz.slots):
            at = overlap_row(sz, slot, other, zb)
            total = total + overlap_ref[at : at + 1, :] * weights[zb, other]
        sums[zb, slot] = total
    table = partial_table(sz, sums, row_of, hot_ref)
    result = rest_ref[...] + part
    refs[0][...] = result
    emit(sz, result, table, flag_ref, *refs[1:])


def last_kernel(sz, n_tables, n_before, cheb_ref, *refs):
    refs = list(refs)
    energy_ref, pv_ref, rows_ref, hot_ref, rest_ref = (refs.pop(0) for _ in range(5))
    table = added([refs.pop(0) for _ in range(n_tables)])
    table = table * (energy_ref[...] * (2.0 / E_HALF * cheb_ref[STEPS : STEPS + 1, :]))
    (part,), _ = projected(sz, [table], pv_ref, rows_ref[...], hot_ref)
    filtered = rest_ref[...] + part
    total = filtered * filtered
    for _ in range(n_before):
        total = total + refs.pop(0)[...]
    refs[0][...] = total


def vmem(count):
    return [pl.BlockSpec(memory_space=pltpu.VMEM)] * count


def smem(count):
    return [pl.BlockSpec(memory_space=pltpu.SMEM)] * count


def in_place(arr):
    return pltpu.with_memory_space_constraint(arr, pltpu.HBM)


def shift_table(table, blocks_first, blocks_second, size_first, size_second, dim, delta):
    blocks = table.reshape(blocks_first, blocks_second, -1)
    count = blocks.shape[dim]
    size = (size_first, size_second)[dim]
    parts = []
    for at in range(count):
        source = [s for s in range(count) if (s + delta) % size == at]
        if source:
            parts.append(lax.slice_in_dim(blocks, source[0], source[0] + 1, axis=dim))
        else:
            parts.append(jnp.zeros_like(lax.slice_in_dim(blocks, 0, 1, axis=dim)))
    return jnp.concatenate(parts, axis=dim).reshape(table.shape)


def offsets(size):
    return sorted({d % size for d in (-2, -1, 1, 2)} - {0})


def shift(arr, axis, amount):
    size = lax.axis_size(axis)
    return lax.ppermute(arr, axis, [(i, (i + amount) % size) for i in range(size)])


def swap(arr, target):
    size_first = lax.axis_size("gx")
    size_second = lax.axis_size("gy")
    pairs = []
    for i in range(size_first):
        for j in range(size_second):
            ti, tj = target(i, j)
            pairs.append((i * size_second + j, ti * size_second + tj))
    return lax.ppermute(arr, ("gx", "gy"), pairs)


def orb_swap(vals, bit):
    size = lax.axis_size("orb")
    return lax.ppermute(vals, "orb", [(i, i ^ bit) for i in range(size)])


def local(orbitals, local_pot, proj_vals, proj_ids, proj_energy, cheb_coef):
    count_orb, ex, ey, nz = orbitals.shape
    slots = proj_vals.shape[0]
    size_first = lax.axis_size("gx")
    size_second = lax.axis_size("gy")
    size_orb = lax.axis_size("orb")
    paired = size_orb == 4 and count_orb == 1
    owner_size = proj_energy.shape[0] // (size_first * size_second)
    whole = size_first == 4 and size_second == 2
    if whole:
        windows = (size_first, size_second)
    else:
        windows = (min(3, size_first), min(3, size_second))
    rows = windows[0] * windows[1] * owner_size // LANES
    sz = Sizes(ex, ey, nz, slots, owner_size, rows)
    here_first = lax.axis_index("gx")
    here_second = lax.axis_index("gy")

    if whole:
        flag = jnp.bitwise_and(here_first, 1).astype(jnp.int32).reshape(1)
        energy = proj_energy.reshape(rows, LANES)
        ids = proj_ids
    else:
        flag = jnp.zeros((1,), jnp.int32)
        owner = proj_ids // owner_size
        rel_first = (owner // size_second - here_first + 1) % size_first
        rel_second = (owner % size_second - here_second + 1) % size_second
        ids = (rel_first * windows[1] + rel_second) * owner_size + proj_ids % owner_size
        grid = proj_energy.reshape(size_first, size_second, owner_size)
        grid = jnp.roll(grid, (1 - here_first, 1 - here_second), (0, 1))
        energy = grid[: windows[0], : windows[1]].reshape(rows, LANES)

    ids = jnp.transpose(ids, (0, 3, 1, 2)).reshape(slots * sz.zb * ex, ey)
    pv = proj_vals.reshape(slots * sz.cells, nz)
    pot = local_pot.reshape(sz.cells, nz)
    message_shapes = (
        jax.ShapeDtypeStruct((sz.edge_rows + rows, LANES), F32),
        jax.ShapeDtypeStruct((sz.edge_rows + rows, LANES), F32),
        jax.ShapeDtypeStruct((sz.yedge_rows + rows, LANES), F32),
        jax.ShapeDtypeStruct((rows, LANES), F32),
    )
    field = jax.ShapeDtypeStruct((sz.cells, nz), F32)
    params = pltpu.CompilerParams(vmem_limit_bytes=48 << 20)

    def exchange(to_a, to_b, to_y, table, aside, pair_last):
        if whole and pair_last:
            from_b = swap(to_b, lambda i, j: (size_first - 1 - i, j))
            from_y = swap(to_y, lambda i, j: (i, 1 - j))
            from_d = swap(table, lambda i, j: (size_first - 1 - i, 1 - j))
            from_a = swap(to_a[: sz.edge_rows], lambda i, j: (i ^ 1, j))
            if aside is not None:
                from_d, aside = lax.optimization_barrier((from_d, aside))
            table = table + from_d + from_b[sz.edge_rows :] + from_y[sz.yedge_rows :]
            other = swap(table, lambda i, j: (i ^ 1, j))
            return [table, other], from_a, from_b, [from_y], aside
        if whole:
            from_a = swap(to_a, lambda i, j: (i ^ 1, j))
            from_b = swap(to_b, lambda i, j: (size_first - 1 - i, j))
            from_y = swap(to_y, lambda i, j: (i, 1 - j))
            chip = table + from_a[sz.edge_rows :]
            from_d = swap(chip, lambda i, j: (size_first - 1 - i, 1 - j))
            if aside is not None:
                from_y, aside = lax.optimization_barrier((from_y, aside))
            beside = from_y[sz.yedge_rows :] + from_b[sz.edge_rows :]
            other = swap(beside, lambda i, j: (i ^ 1, j))
            return [chip, beside, other, from_d], from_a, from_b, [from_y], aside
        to_a = to_a[: sz.edge_rows]
        edges_b = to_b[: sz.edge_rows]
        edges_y = to_y[: sz.yedge_rows]
        below = shift(edges_y, "gy", 1)
        above = shift(edges_y, "gy", -1)
        from_a = shift(edges_b, "gx", -1)
        from_b = shift(to_a, "gx", 1)
        for dim, axis in ((1, "gy"), (0, "gx")):
            total = table
            for delta in offsets((size_first, size_second)[dim]):
                moved = shift(table, axis, -delta)
                total = total + shift_table(
                    moved, windows[0], windows[1], size_first, size_second, dim, delta
                )
            table = total
        return [table], from_a, from_b, [below, above], aside

    def square(cheb, row_of, hot, rest, tables, *before):
        args = (cheb, energy, pv, row_of, hot, rest, *tables, *before)
        return pl.pallas_call(
            functools.partial(last_kernel, sz, len(tables), len(before)),
            out_shape=field,
            in_specs=vmem(len(args)),
            out_specs=vmem(1)[0],
            compiler_params=params,
            name="square_more" if before else "square",
        )(*args)

    def one_orbital(start):
        *messages, row_of, hot, cheb = pl.pallas_call(
            functools.partial(first_kernel, sz),
            out_shape=message_shapes
            + (
                jax.ShapeDtypeStruct((slots * sz.zb, LANES), F32),
                jax.ShapeDtypeStruct((LANES, slots * sz.zb * sz.cells), BF16),
                jax.ShapeDtypeStruct((SUBLANES, LANES), F32),
            ),
            in_specs=smem(1) + [pl.BlockSpec(memory_space=pltpu.HBM)] * 4,
            out_specs=tuple(vmem(7)),
            scratch_shapes=[
                pltpu.VMEM(start.shape, start.dtype),
                pltpu.VMEM(pv.shape, pv.dtype),
                pltpu.VMEM(ids.shape, ids.dtype),
                pltpu.SMEM(cheb_coef.shape, cheb_coef.dtype),
                pltpu.SemaphoreType.DMA((4,)),
            ],
            compiler_params=params,
            name="project_first",
        )(flag, *(in_place(arr) for arr in (start, pv, ids, cheb_coef)))
        overlap = pl.pallas_call(
            functools.partial(overlap_kernel, sz),
            out_shape=jax.ShapeDtypeStruct((slots * slots * sz.zb, LANES), F32),
            in_specs=vmem(2),
            out_specs=vmem(1)[0],
            compiler_params=params,
            name="overlap",
        )(row_of, pv)
        history = [start]
        for degree in range(1, STEPS + 1):
            tables, from_a, from_b, from_y, aside = exchange(
                *messages, overlap if degree == 1 else None, degree != 2
            )
            overlap = overlap if aside is None else aside
            last = degree == STEPS
            sums_shape = jax.ShapeDtypeStruct((slots * sz.zb, LANES), F32)
            if last:
                args = (cheb, from_a, from_b, *from_y, pot, *history)
            else:
                args = (from_a, from_b, *from_y, pot, pv, *history)
            rest, *sums = pl.pallas_call(
                functools.partial(local_kernel, sz, degree, len(from_y)),
                out_shape=(field,) if last else (field, sums_shape),
                in_specs=smem(1) + vmem(len(args)),
                out_specs=tuple(vmem(1 if last else 2)),
                compiler_params=params,
                name=f"local_{degree}",
            )(flag, *args)
            if last:
                if not paired:
                    return square(cheb, row_of, hot, rest, tables)
                total = functools.reduce(jnp.add, tables)
                other, other_total = orb_swap(rest, 1), orb_swap(total, 1)
                own = square(cheb, row_of, hot, rest, [total])
                return square(cheb, row_of, hot, other, [other_total], own)
            args = (*tables, energy, rest, pv, row_of, hot, *sums, overlap)
            out = pl.pallas_call(
                functools.partial(nonlocal_kernel, sz, degree, len(tables)),
                out_shape=(field,) + message_shapes,
                in_specs=smem(1) + vmem(len(args)),
                out_specs=tuple(vmem(5)),
                compiler_params=params,
                name=f"nonlocal_{degree}",
            )(flag, *args)
            history.append(out[0])
            messages = out[1:]

    density = one_orbital(orbitals[0].reshape(sz.cells, nz))
    for at in range(1, count_orb):
        density = density + one_orbital(orbitals[at].reshape(sz.cells, nz))
    scale = 1.0 / (count_orb * size_orb)
    if paired:
        density = density + orb_swap(density, 3)
    else:
        density = lax.psum(density, "orb")
    return (density * scale).reshape(ex, ey, nz)


def solution(mesh):
    return jax.shard_map(
        local,
        mesh=mesh,
        in_specs=(
            P("orb", "gx", "gy", None),
            P("gx", "gy", None),
            P(None, "gx", "gy", None),
            P(None, "gx", "gy", None),
            P(),
            P(),
        ),
        out_specs=P("gx", "gy", None),
        check_vma=False,
    )
```

```python
import functools

import jax
import jax.numpy as jnp
from jax import lax
from jax.experimental import pallas as pl
from jax.experimental.pallas import tpu as pltpu
from jax.sharding import PartitionSpec as P

LANES = 128
SUBLANES = 8
STEPS = 3
E_MID = 4.0
E_HALF = 8.0
F32 = jnp.float32
BF16 = jnp.bfloat16


def pieces(vals):
    first = vals.astype(BF16)
    second = (vals - first.astype(F32)).astype(BF16)
    return first, second


def dot(a, b, contract):
    return lax.dot_general(a, b, (contract, ((), ())), preferred_element_type=F32)


NN = ((1,), (0,))
NT = ((1,), (1,))


def iota(shape, dim):
    return lax.broadcasted_iota(jnp.int32, shape, dim)


class Sizes:
    def __init__(self, extent_first, extent_second, extent_depth, slots, owner_size, rows):
        self.ex = extent_first
        self.ey = extent_second
        self.nz = extent_depth
        self.zb = extent_depth // LANES
        self.slots = slots
        self.cells = extent_first * extent_second
        self.rows = rows
        self.xedge = 2 * extent_second
        self.yedge = extent_first * SUBLANES // 2
        self.edge_rows = self.zb * self.xedge
        self.yedge_rows = self.zb * self.yedge
        assert extent_second == 2 * SUBLANES and extent_first % 2 == 0
        assert self.cells == LANES and extent_first == SUBLANES


def rows_of_ids(sz, ids):
    copies = jnp.where(
        jnp.bitwise_and(iota((sz.ey, LANES), 1), sz.ey - 1) == iota((sz.ey, LANES), 0), 1.0, 0.0
    ).astype(BF16)
    shape = (sz.slots * sz.zb, sz.ex, LANES)
    own = iota(shape, 2) // sz.ey == iota(shape, 1)

    def flat(part):
        spread = dot(part.astype(F32).astype(BF16), copies, NN).reshape(shape)
        return jnp.sum(jnp.where(own, spread, 0.0), axis=1)

    return flat(lax.shift_right_logical(ids, 7)), flat(jnp.bitwise_and(ids, LANES - 1))


def chunk(sz, arr, zb, slot):
    at = slot * sz.zb + zb
    return arr[at : at + 1, :]


def chunks(sz):
    return [(zb, slot) for zb in range(sz.zb) for slot in range(sz.slots)]


def slot_sums(sz, vals, pv_ref):
    eye = iota((sz.cells, LANES), 0) == iota((sz.cells, LANES), 1)
    eye_all = jnp.concatenate([eye] * sz.slots, axis=0)
    sums = {}
    for zb in range(sz.zb):
        first, second = pieces(vals[:, zb * LANES : (zb + 1) * LANES])
        weights = pv_ref[:, zb * LANES : (zb + 1) * LANES]
        cross = dot(
            jnp.concatenate([weights, weights], axis=1),
            jnp.concatenate([first, second], axis=1),
            NT,
        )
        cross = jnp.where(eye_all, cross, 0.0)
        for slot in range(sz.slots):
            part = cross[slot * sz.cells : (slot + 1) * sz.cells]
            sums[zb, slot] = jnp.sum(part, axis=0, keepdims=True)
    return sums


def partial_table(sz, sums, row_of, hot_ref):
    spread_first, spread_second = [], []
    table_iota = iota((sz.rows, LANES), 0).astype(F32)
    for zb, slot in chunks(sz):
        hit = chunk(sz, row_of, zb, slot) == table_iota
        a, b = pieces(sums[zb, slot])
        spread_first.append(jnp.where(hit, a.astype(F32), 0.0).astype(BF16))
        spread_second.append(jnp.where(hit, b.astype(F32), 0.0).astype(BF16))
    lhs = jnp.concatenate(
        [jnp.concatenate(spread_first, axis=1), jnp.concatenate(spread_second, axis=1)], axis=0
    )
    both = dot(lhs, hot_ref[...], NT)
    return both[: sz.rows] + both[sz.rows :]


def overlap_row(sz, slot, other, zb):
    return (slot * sz.slots + other) * sz.zb + zb


def overlap_kernel(sz, after_ref, pv_ref, overlap_ref):
    eye = iota((sz.cells, LANES), 0) == iota((sz.cells, LANES), 1)
    for zb in range(sz.zb):
        weights = pv_ref[:, zb * LANES : (zb + 1) * LANES]
        cross = dot(weights, weights, NT)
        for slot in range(sz.slots):
            rows = cross[slot * sz.cells : (slot + 1) * sz.cells]
            for other in range(slot, sz.slots):
                block = rows[:, other * sz.cells : (other + 1) * sz.cells]
                row = jnp.sum(jnp.where(eye, block, 0.0), axis=0, keepdims=True)
                for at in {(slot, other), (other, slot)}:
                    at = overlap_row(sz, *at, zb)
                    overlap_ref[at : at + 1, :] = row


def projected(sz, tables, pv_ref, row_of, hot_ref):
    count = len(tables)
    split = [piece for table in tables for piece in pieces(table)]
    found = dot(jnp.concatenate(split, axis=0), hot_ref[...], NN)
    found = [
        found[2 * n * sz.rows : (2 * n + 1) * sz.rows]
        + found[(2 * n + 1) * sz.rows : (2 * n + 2) * sz.rows]
        for n in range(count)
    ]
    table_iota = iota((sz.rows, LANES), 0).astype(F32)
    eye = iota((sz.cells, LANES), 0) == iota((sz.cells, LANES), 1)
    result = [[] for _ in tables]
    weights = [{} for _ in tables]
    for zb in range(sz.zb):
        diag = [[] for _ in range(2 * count)]
        for slot in range(sz.slots):
            at = (zb * sz.slots + slot) * LANES
            hit = chunk(sz, row_of, zb, slot) == table_iota
            for n in range(count):
                weight = jnp.sum(
                    jnp.where(hit, found[n][:, at : at + LANES], 0.0), axis=0, keepdims=True
                )
                weights[n][zb, slot] = weight
                a, b = pieces(jnp.where(eye, weight, 0.0))
                diag[2 * n].append(a)
                diag[2 * n + 1].append(b)
        lhs = jnp.concatenate([jnp.concatenate(parts, axis=1) for parts in diag], axis=0)
        both = dot(lhs, pv_ref[:, zb * LANES : (zb + 1) * LANES], NN)
        for n in range(count):
            at = 2 * n * sz.cells
            result[n].append(both[at : at + sz.cells] + both[at + sz.cells : at + 2 * sz.cells])
    return [jnp.concatenate(parts, axis=1) for parts in result], weights


def from_message(sz, msg_ref, rows):
    return jnp.concatenate(
        [msg_ref[zb * rows : (zb + 1) * rows, :] for zb in range(sz.zb)], axis=1
    )


def to_message(sz, msg_ref, vals):
    rows = vals.shape[0]
    for zb in range(sz.zb):
        msg_ref[zb * rows : (zb + 1) * rows, :] = vals[:, zb * LANES : (zb + 1) * LANES]


def second_edges(sz, vals):
    tiles = vals.reshape(sz.ex, 2, SUBLANES, sz.nz)
    sub = iota((sz.ex // 2, SUBLANES, sz.nz), 1)
    even = tiles.reshape(sz.ex // 2, 2, 2, SUBLANES, sz.nz)
    outer_even = jnp.where(sub < 4, even[:, 0, 0], even[:, 0, 1])
    outer_odd = jnp.where(sub < 4, even[:, 1, 0], even[:, 1, 1])
    odd = pltpu.roll(outer_odd, 4, axis=1)
    keep = jnp.logical_or(sub < 2, sub >= 6)
    return jnp.where(keep, outer_even, odd).reshape(sz.yedge, sz.nz)


def second_halo(sz, packed):
    pairs = packed.reshape(sz.ex // 2, SUBLANES, sz.nz)
    odd = pltpu.roll(pairs, 4, axis=1)
    return jnp.stack([pairs, odd], axis=1).reshape(sz.ex, SUBLANES, sz.nz)


def stencil(sz, vals, low, high, below, above):
    result = -90.0 * vals
    tall = jnp.concatenate([low, vals, high], axis=0)
    step = sz.ey
    cells = sz.cells
    near = tall[step : step + cells] + tall[3 * step : 3 * step + cells]
    far = tall[0:cells] + tall[4 * step : 4 * step + cells]

    near = near + pltpu.roll(vals, 1, axis=1) + pltpu.roll(vals, sz.nz - 1, axis=1)
    far = far + pltpu.roll(vals, 2, axis=1) + pltpu.roll(vals, sz.nz - 2, axis=1)

    tiles = vals.reshape(2 * sz.ex, SUBLANES, sz.nz)
    sub = iota((2 * sz.ex, SUBLANES, sz.nz), 1)

    def shifted(amount, outer, from_below):
        mine = pltpu.roll(tiles, amount, axis=1)
        theirs = pltpu.roll(outer, amount, axis=1)
        pairs = mine.reshape(sz.ex, 2, SUBLANES, sz.nz)
        if from_below:
            other = jnp.stack([theirs, pairs[:, 0]], axis=1)
            mask = sub < amount
        else:
            other = jnp.stack([pairs[:, 1], theirs], axis=1)
            mask = sub >= amount
        return jnp.where(mask, other.reshape(tiles.shape), mine).reshape(vals.shape)

    near = near + shifted(1, below, True) + shifted(SUBLANES - 1, above, False)
    far = far + shifted(2, below, True) + shifted(SUBLANES - 2, above, False)
    return result + 16.0 * near - far


def emit(sz, vals, table, flag_ref, ab_ref, bb_ref, yb_ref, table_ref):
    table_ref[...] = table
    flag = flag_ref[0]
    top = vals[sz.cells - sz.xedge :]
    bottom = vals[: sz.xedge]
    is_high = flag == 0
    to_message(sz, ab_ref, jnp.where(is_high, top, bottom))
    ab_ref[sz.edge_rows :, :] = table
    to_message(sz, bb_ref, jnp.where(is_high, bottom, top))
    bb_ref[sz.edge_rows :, :] = table
    to_message(sz, yb_ref, second_edges(sz, vals))
    yb_ref[sz.yedge_rows :, :] = table


def first_kernel(
    sz,
    flag_ref,
    vals_hbm,
    pv_hbm,
    ids_hbm,
    cheb_hbm,
    ab_ref,
    bb_ref,
    yb_ref,
    table_ref,
    rows_ref,
    hot_ref,
    cheb_out,
    vals_ref,
    pv_ref,
    ids_ref,
    cheb_ref,
    sems,
):
    get_ids = pltpu.make_async_copy(ids_hbm, ids_ref, sems.at[0])
    get_pv = pltpu.make_async_copy(pv_hbm, pv_ref, sems.at[1])
    get_vals = pltpu.make_async_copy(vals_hbm, vals_ref, sems.at[2])
    get_cheb = pltpu.make_async_copy(cheb_hbm, cheb_ref, sems.at[3])
    get_ids.start()
    get_vals.start()
    get_pv.start()
    get_cheb.start()
    get_ids.wait()
    row_of, lane_of = rows_of_ids(sz, ids_ref[...])
    rows_ref[...] = row_of
    lane_iota = iota((LANES, LANES), 0).astype(F32)
    for at, (zb, slot) in enumerate(chunks(sz)):
        hot_ref[:, at * LANES : (at + 1) * LANES] = jnp.where(
            chunk(sz, lane_of, zb, slot) == lane_iota, 1.0, 0.0
        ).astype(BF16)
    get_vals.wait()
    get_pv.wait()
    vals = vals_ref[...]
    table = partial_table(sz, slot_sums(sz, vals, pv_ref), row_of, hot_ref)
    emit(sz, vals, table, flag_ref, ab_ref, bb_ref, yb_ref, table_ref)
    get_cheb.wait()
    for n in range(STEPS + 1):
        cheb_out[n : n + 1, :] = jnp.full((1, LANES), cheb_ref[n], F32)


def coefficient(sz, cheb_ref, n):
    row = cheb_ref[n : n + 1, :]
    return jnp.concatenate([row] * sz.zb, axis=1)


def local_kernel(sz, degree, n_y, flag_ref, *refs):
    refs = list(refs)
    cheb_ref = refs.pop(0) if degree == STEPS else None
    a_ref, b_ref = refs.pop(0), refs.pop(0)
    y_refs = [refs.pop(0) for _ in range(n_y)]
    pot_ref = refs.pop(0)
    if degree < STEPS:
        pv_ref, sums_ref = refs.pop(0), refs.pop()
    *history, out_ref = refs
    vals = history[-1][...]

    from_a = from_message(sz, a_ref, sz.xedge)
    from_b = from_message(sz, b_ref, sz.xedge)
    is_high = flag_ref[0] == 0
    low = jnp.where(is_high, from_b, from_a)
    high = jnp.where(is_high, from_a, from_b)
    outer = [second_halo(sz, from_message(sz, ref, sz.yedge)) for ref in y_refs]
    laplace12 = stencil(sz, vals, low, high, outer[0], outer[-1])
    double = 1.0 if degree == 1 else 2.0
    result = laplace12 * (-0.5 / 12.0 / E_HALF * double) + vals * (
        (pot_ref[...] - E_MID) * (double / E_HALF)
    )
    if degree > 1:
        result = result - history[-2][...]
    if degree == STEPS:
        result = coefficient(sz, cheb_ref, STEPS) * result
        for n in range(STEPS):
            result = result + coefficient(sz, cheb_ref, n) * history[n][...]
    out_ref[...] = result
    if degree < STEPS:
        for (zb, slot), row in slot_sums(sz, result, pv_ref).items():
            at = slot * sz.zb + zb
            sums_ref[at : at + 1, :] = row


def added(table_refs):
    table = table_refs[0][...]
    for ref in table_refs[1:]:
        table = table + ref[...]
    return table


def nonlocal_kernel(sz, degree, n_tables, flag_ref, *refs):
    refs = list(refs)
    table_refs = [refs.pop(0) for _ in range(n_tables)]
    energy_ref, rest_ref, pv_ref, rows_ref, hot_ref = (refs.pop(0) for _ in range(5))
    sums_ref, overlap_ref = refs.pop(0), refs.pop(0)
    row_of = rows_ref[...]
    double = 1.0 if degree == 1 else 2.0
    table = added(table_refs) * (energy_ref[...] * (double / E_HALF))
    (part,), (weights,) = projected(sz, [table], pv_ref, row_of, hot_ref)
    sums = {}
    for zb, slot in chunks(sz):
        total = chunk(sz, sums_ref, zb, slot)
        for other in range(sz.slots):
            at = overlap_row(sz, slot, other, zb)
            total = total + overlap_ref[at : at + 1, :] * weights[zb, other]
        sums[zb, slot] = total
    table = partial_table(sz, sums, row_of, hot_ref)
    result = rest_ref[...] + part
    refs[0][...] = result
    emit(sz, result, table, flag_ref, *refs[1:])


def last_kernel(sz, n_tables, n_before, cheb_ref, *refs):
    refs = list(refs)
    energy_ref, pv_ref, rows_ref, hot_ref, rest_ref = (refs.pop(0) for _ in range(5))
    table = added([refs.pop(0) for _ in range(n_tables)])
    table = table * (energy_ref[...] * (2.0 / E_HALF * cheb_ref[STEPS : STEPS + 1, :]))
    (part,), _ = projected(sz, [table], pv_ref, rows_ref[...], hot_ref)
    filtered = rest_ref[...] + part
    total = filtered * filtered
    for _ in range(n_before):
        total = total + refs.pop(0)[...]
    refs[0][...] = total


def vmem(count):
    return [pl.BlockSpec(memory_space=pltpu.VMEM)] * count


def smem(count):
    return [pl.BlockSpec(memory_space=pltpu.SMEM)] * count


def in_place(arr):
    return pltpu.with_memory_space_constraint(arr, pltpu.HBM)


def shift_table(table, blocks_first, blocks_second, size_first, size_second, dim, delta):
    blocks = table.reshape(blocks_first, blocks_second, -1)
    count = blocks.shape[dim]
    size = (size_first, size_second)[dim]
    parts = []
    for at in range(count):
        source = [s for s in range(count) if (s + delta) % size == at]
        if source:
            parts.append(lax.slice_in_dim(blocks, source[0], source[0] + 1, axis=dim))
        else:
            parts.append(jnp.zeros_like(lax.slice_in_dim(blocks, 0, 1, axis=dim)))
    return jnp.concatenate(parts, axis=dim).reshape(table.shape)


def offsets(size):
    return sorted({d % size for d in (-2, -1, 1, 2)} - {0})


def shift(arr, axis, amount):
    size = lax.axis_size(axis)
    return lax.ppermute(arr, axis, [(i, (i + amount) % size) for i in range(size)])


def swap(arr, target):
    size_first = lax.axis_size("gx")
    size_second = lax.axis_size("gy")
    pairs = []
    for i in range(size_first):
        for j in range(size_second):
            ti, tj = target(i, j)
            pairs.append((i * size_second + j, ti * size_second + tj))
    return lax.ppermute(arr, ("gx", "gy"), pairs)


def orb_swap(vals, bit):
    size = lax.axis_size("orb")
    return lax.ppermute(vals, "orb", [(i, i ^ bit) for i in range(size)])


def local(orbitals, local_pot, proj_vals, proj_ids, proj_energy, cheb_coef):
    count_orb, ex, ey, nz = orbitals.shape
    slots = proj_vals.shape[0]
    size_first = lax.axis_size("gx")
    size_second = lax.axis_size("gy")
    size_orb = lax.axis_size("orb")
    paired = size_orb == 4 and count_orb == 1
    owner_size = proj_energy.shape[0] // (size_first * size_second)
    whole = size_first == 4 and size_second == 2
    if whole:
        windows = (size_first, size_second)
    else:
        windows = (min(3, size_first), min(3, size_second))
    rows = windows[0] * windows[1] * owner_size // LANES
    sz = Sizes(ex, ey, nz, slots, owner_size, rows)
    here_first = lax.axis_index("gx")
    here_second = lax.axis_index("gy")

    if whole:
        flag = jnp.bitwise_and(here_first, 1).astype(jnp.int32).reshape(1)
        energy = proj_energy.reshape(rows, LANES)
        ids = proj_ids
    else:
        flag = jnp.zeros((1,), jnp.int32)
        owner = proj_ids // owner_size
        rel_first = (owner // size_second - here_first + 1) % size_first
        rel_second = (owner % size_second - here_second + 1) % size_second
        ids = (rel_first * windows[1] + rel_second) * owner_size + proj_ids % owner_size
        grid = proj_energy.reshape(size_first, size_second, owner_size)
        grid = jnp.roll(grid, (1 - here_first, 1 - here_second), (0, 1))
        energy = grid[: windows[0], : windows[1]].reshape(rows, LANES)

    ids = jnp.transpose(ids, (0, 3, 1, 2)).reshape(slots * sz.zb * ex, ey)
    pv = proj_vals.reshape(slots * sz.cells, nz)
    pot = local_pot.reshape(sz.cells, nz)
    message_shapes = (
        jax.ShapeDtypeStruct((sz.edge_rows + rows, LANES), F32),
        jax.ShapeDtypeStruct((sz.edge_rows + rows, LANES), F32),
        jax.ShapeDtypeStruct((sz.yedge_rows + rows, LANES), F32),
        jax.ShapeDtypeStruct((rows, LANES), F32),
    )
    field = jax.ShapeDtypeStruct((sz.cells, nz), F32)
    params = pltpu.CompilerParams(vmem_limit_bytes=48 << 20)

    def exchange(to_a, to_b, to_y, table, aside, pair_last):
        if whole and pair_last:
            from_b = swap(to_b, lambda i, j: (size_first - 1 - i, j))
            from_y = swap(to_y, lambda i, j: (i, 1 - j))
            from_d = swap(table, lambda i, j: (size_first - 1 - i, 1 - j))
            from_a = swap(to_a[: sz.edge_rows], lambda i, j: (i ^ 1, j))
            if aside is not None:
                from_d, aside = lax.optimization_barrier((from_d, aside))
            table = table + from_d + from_y[sz.yedge_rows :] + from_b[sz.edge_rows :]
            other = swap(table, lambda i, j: (i ^ 1, j))
            return [table, other], from_a, from_b, [from_y], aside
        if whole:
            from_a = swap(to_a, lambda i, j: (i ^ 1, j))
            from_b = swap(to_b, lambda i, j: (size_first - 1 - i, j))
            from_y = swap(to_y, lambda i, j: (i, 1 - j))
            chip = table + from_a[sz.edge_rows :]
            from_d = swap(chip, lambda i, j: (size_first - 1 - i, 1 - j))
            if aside is not None:
                aside = aside(from_y, pv)
                from_b, aside = lax.optimization_barrier((from_b, aside))
            beside = from_y[sz.yedge_rows :] + from_b[sz.edge_rows :]
            other = swap(beside, lambda i, j: (i ^ 1, j))
            return [chip, beside, other, from_d], from_a, from_b, [from_y], aside
        to_a = to_a[: sz.edge_rows]
        if aside is not None:
            aside = aside(table, pv)
        edges_b = to_b[: sz.edge_rows]
        edges_y = to_y[: sz.yedge_rows]
        below = shift(edges_y, "gy", 1)
        above = shift(edges_y, "gy", -1)
        from_a = shift(edges_b, "gx", -1)
        from_b = shift(to_a, "gx", 1)
        for dim, axis in ((1, "gy"), (0, "gx")):
            total = table
            for delta in offsets((size_first, size_second)[dim]):
                moved = shift(table, axis, -delta)
                total = total + shift_table(
                    moved, windows[0], windows[1], size_first, size_second, dim, delta
                )
            table = total
        return [table], from_a, from_b, [below, above], aside

    def square(cheb, row_of, hot, rest, tables, *before):
        args = (cheb, energy, pv, row_of, hot, rest, *tables, *before)
        return pl.pallas_call(
            functools.partial(last_kernel, sz, len(tables), len(before)),
            out_shape=field,
            in_specs=vmem(len(args)),
            out_specs=vmem(1)[0],
            compiler_params=params,
            name="square_more" if before else "square",
        )(*args)

    def one_orbital(start):
        *messages, row_of, hot, cheb = pl.pallas_call(
            functools.partial(first_kernel, sz),
            out_shape=message_shapes
            + (
                jax.ShapeDtypeStruct((slots * sz.zb, LANES), F32),
                jax.ShapeDtypeStruct((LANES, slots * sz.zb * sz.cells), BF16),
                jax.ShapeDtypeStruct((SUBLANES, LANES), F32),
            ),
            in_specs=smem(1) + [pl.BlockSpec(memory_space=pltpu.HBM)] * 4,
            out_specs=tuple(vmem(7)),
            scratch_shapes=[
                pltpu.VMEM(start.shape, start.dtype),
                pltpu.VMEM(pv.shape, pv.dtype),
                pltpu.VMEM(ids.shape, ids.dtype),
                pltpu.SMEM(cheb_coef.shape, cheb_coef.dtype),
                pltpu.SemaphoreType.DMA((4,)),
            ],
            compiler_params=params,
            name="project_first",
        )(flag, *(in_place(arr) for arr in (start, pv, ids, cheb_coef)))
        overlap_after = pl.pallas_call(
            functools.partial(overlap_kernel, sz),
            out_shape=jax.ShapeDtypeStruct((slots * slots * sz.zb, LANES), F32),
            in_specs=vmem(2),
            out_specs=vmem(1)[0],
            compiler_params=params,
            name="overlap",
        )
        overlap = None
        history = [start]
        for degree in range(1, STEPS + 1):
            tables, from_a, from_b, from_y, aside = exchange(
                *messages, overlap_after if degree == 1 else None, degree == STEPS
            )
            overlap = overlap if aside is None else aside
            last = degree == STEPS
            sums_shape = jax.ShapeDtypeStruct((slots * sz.zb, LANES), F32)
            if last:
                args = (cheb, from_a, from_b, *from_y, pot, *history)
            else:
                args = (from_a, from_b, *from_y, pot, pv, *history)
            rest, *sums = pl.pallas_call(
                functools.partial(local_kernel, sz, degree, len(from_y)),
                out_shape=(field,) if last else (field, sums_shape),
                in_specs=smem(1) + vmem(len(args)),
                out_specs=tuple(vmem(1 if last else 2)),
                compiler_params=params,
                name=f"local_{degree}",
            )(flag, *args)
            if last:
                if not paired:
                    return square(cheb, row_of, hot, rest, tables)
                total = functools.reduce(jnp.add, tables)
                other, other_total = orb_swap(rest, 1), orb_swap(total, 1)
                own = square(cheb, row_of, hot, rest, [total])
                return square(cheb, row_of, hot, other, [other_total], own)
            args = (*tables, energy, rest, pv, row_of, hot, *sums, overlap)
            out = pl.pallas_call(
                functools.partial(nonlocal_kernel, sz, degree, len(tables)),
                out_shape=(field,) + message_shapes,
                in_specs=smem(1) + vmem(len(args)),
                out_specs=tuple(vmem(5)),
                compiler_params=params,
                name=f"nonlocal_{degree}",
            )(flag, *args)
            history.append(out[0])
            messages = out[1:]

    density = one_orbital(orbitals[0].reshape(sz.cells, nz))
    for at in range(1, count_orb):
        density = density + one_orbital(orbitals[at].reshape(sz.cells, nz))
    scale = 1.0 / (count_orb * size_orb)
    if paired:
        density = density + orb_swap(density, 3)
    else:
        density = lax.psum(density, "orb")
    return (density * scale).reshape(ex, ey, nz)


def solution(mesh):
    return jax.shard_map(
        local,
        mesh=mesh,
        in_specs=(
            P("orb", "gx", "gy", None),
            P("gx", "gy", None),
            P(None, "gx", "gy", None),
            P(None, "gx", "gy", None),
            P(),
            P(),
        ),
        out_specs=P("gx", "gy", None),
        check_vma=False,
    )
```
